32 devices in a mesh: group: 8 (over z, y), expert: 4 (over x, core).
Axes of the slice: x: 2, y: 2, z: 4, core: 2. Of those that a mesh axis runs over, the one named last changes fastest.
Arguments:
- layer_in: bfloat16 [4, 1024, 2048], P('expert', 'group'), may hold values from -6 to 6
- segment_ids: int32 [4, 1024], P('expert', 'group'), may hold values from 0 to 4, never falling along the last dimension, each value on 1 to 512 neighbouring positions
- routing: int32 [4, 1024, 8], P('expert', 'group'), may hold values from 0 to 15, all different within a row; in each aligned block of 128 rows (0 to 127, 128 to 255, ..., all dimensions but the last counted through in order) at most 85 rows name the same one
- out_grad: bfloat16 [4, 1024, 2048], P('expert', 'group'), may hold values from -6 to 6
- attn_gain: float32 [2048], replicated, may hold values from 0.5 to 1.5
- w_query: bfloat16 [2048, 2048], replicated, may hold values from -0.125 to 0.125
- w_key: bfloat16 [2048, 2048], replicated, may hold values from -0.125 to 0.125
- w_value: bfloat16 [2048, 2048], replicated, may hold values from -0.125 to 0.125
- query_gain: float32 [2048], replicated, may hold values from 0.5 to 1.5
- key_gain: float32 [2048], replicated, may hold values from 0.5 to 1.5
- w_out: bfloat16 [2048, 2048], replicated, may hold values from -1 to 1
- mlp_gain: float32 [2048], replicated, may hold values from 0.5 to 1.5
- w_router: bfloat16 [2048, 16], replicated, may hold values from -0.0625 to 0.0625
- w_gate: bfloat16 [16, 2048, 1024], P('expert', 'group'), may hold values from -0.125 to 0.125
- w_up: bfloat16 [16, 2048, 1024], P('expert', 'group'), may hold values from -0.125 to 0.125
- w_down: bfloat16 [16, 1024, 2048], P('expert', None, 'group'), may hold values from -2 to 2
Outputs:
- layer_out: bfloat16 [4, 1024, 2048], P('expert', 'group')
- x_grad: float32 [4, 1024, 2048], P('expert', 'group')
- attn_gain_grad: float32 [2048], P(('group', 'expert'))
- query_w_grad: float32 [2048, 2048], P(('group', 'expert'))
- key_w_grad: float32 [2048, 2048], P(('group', 'expert'))
- value_w_grad: float32 [2048, 2048], P(('group', 'expert'))
- query_gain_grad: float32 [2048], P(('group', 'expert'))
- key_gain_grad: float32 [2048], P(('group', 'expert'))
- out_w_grad: float32 [2048, 2048], P(('group', 'expert'))
- mlp_gain_grad: float32 [2048], P(('group', 'expert'))
- router_grad: float32 [2048, 16], P(('group', 'expert'))
- gate_grad: float32 [16, 2048, 1024], P('expert', 'group')
- up_grad: float32 [16, 2048, 1024], P('expert', 'group')
- down_grad: float32 [16, 1024, 2048], P('expert', None, 'group')
The draws below stay inside these ranges and needn't reach their ends.
Inputs may be any that keep to these rules, and one draw needn't show every extreme that they name: `routing`: each row names 8 different experts. Within each aligned block of 128 rows of a sequence no expert is named by more than 85 rows. `segment_ids`: document numbers never fall along a sequence; a document has at most 512 tokens.
All inputs are finite; a program needn't handle non-finite values.
Results may differ from the reference program's by a relative error of at most 0.019.
Values may be sent and summed in bfloat16 or wider, within the bound.
A program may use at most 320 MiB of HBM per device.

```python
import math
import jax
import jax.numpy as jnp
import numpy as np
from jax import lax

D = 2048
HEADS = 16
HEAD_DIM = 128
FF_E = 1024
TOPK = 8
EXPERTS = 16
TOK_DEV = 128
SEQS = 4
LEN = 1024
TOKENS = 4096
CAP = 85
DOCS = 5
DOC_MAX = 512
N_GROUP = 8
N_EXPERT = 4


def steps_of(key, dims, split, least, high):
    loudness, own = 1.0, jax.random.fold_in(key, 6)
    for dim, blocks in split:
        draws = jnp.exp(jax.random.uniform(jax.random.fold_in(own, dim), (blocks,), jnp.float32, least / len(split), high / len(split)))
        loudness = loudness * jnp.repeat(draws, dims[dim] // blocks).reshape([-1 if axis == dim else 1 for axis in range(len(dims))])
    return loudness


def split_up(number_of, total, most, slope):
    portions = [(1 << 20) // math.isqrt(standing ** slope) + 1 for standing in range(2, number_of + 1)]
    surplus, given = total - most - (number_of - 1), [1] * (number_of - 1)
    while surplus > 0:
        candidates = [i for i in range(number_of - 1) if given[i] < most]
        pool, remaining = sum([portions[i] for i in candidates]), surplus
        for i in candidates:
            addition = min(most - given[i], max(1, remaining * portions[i] // pool), surplus)
            given[i] = given[i] + addition
            surplus = surplus - addition
    return np.array([most] + given)


def ragged_sizes(key, amount, total, reach, lean):
    if amount == 2:
        one = jax.random.randint(key, (), max(1, total - reach), min(reach, total - 1) + 1)
        return jnp.stack([one, total - one])
    tallies = jnp.asarray(split_up(amount, total, reach, lean), jnp.int32)
    couples = (amount - 1) // 2
    source_of, receiver = tallies[1:1 + 2 * couples:2], tallies[2:2 + 2 * couples:2]
    margin = jnp.minimum(source_of - 1, reach - receiver)
    moved = jax.random.randint(jax.random.fold_in(key, 1), (couples,), 0, 1 << 20) % (margin + 1)
    tallies = tallies.at[1:1 + 2 * couples:2].set(source_of - moved).at[2:2 + 2 * couples:2].set(receiver + moved)
    return tallies[jax.random.permutation(jax.random.fold_in(key, 2), amount)]


def assign_block(key, own, number, rows, number_of, top, reach, slope):
    sequence = jax.random.permutation(key, number_of)
    packed, usual = load_shares(number_of, rows * top, reach, slope, True), load_shares(number_of, rows * top, reach, slope, False)
    places = jnp.arange(number_of)

    def named(sizes, turn):
        used = int((sizes > 0).sum())
        fixed = max(1, used // 4)
        passed = fixed + (places - fixed + turn * (used - fixed)) % max(1, number_of - fixed)
        return jnp.zeros((number_of,), jnp.int32).at[sequence[jnp.where(places < fixed, places, passed)]].set(jnp.asarray(sizes, jnp.int32))

    sizes = jnp.where(number % 4 == 0, named(packed, number // 4), named(usual, number - number // 4 - 1))
    mixed = jax.random.permutation(jax.random.fold_in(own, 3), number_of)
    source_of, taker = mixed[0:number_of // 2 * 2:2], mixed[1:number_of // 2 * 2:2]
    slack = jnp.minimum(sizes[source_of] - 1, reach - sizes[taker]) // 2
    slack = jnp.where((source_of == sequence[0]) | (taker == sequence[0]) | (sizes[taker] == 0), 0, jnp.maximum(slack, 0))
    passed = jax.random.randint(jax.random.fold_in(own, 4), (number_of // 2,), 0, 1 << 20) % (slack + 1)
    sizes = sizes.at[source_of].add(-passed).at[taker].add(passed)
    items = jnp.searchsorted(jnp.cumsum(sizes), jnp.arange(rows * top), side="right").astype(jnp.int32)
    grid = items.reshape(top, rows).T
    grid = grid[jax.random.permutation(jax.random.fold_in(own, 1), rows)]
    turn = jax.random.randint(jax.random.fold_in(own, 2), (rows, 1), 0, top)
    return jnp.take_along_axis(grid, (jnp.arange(top)[None, :] + turn) % top, axis=1)


def load_shares(number_of, total, bound, lean, full):
    weights = [(1 << 20) // math.isqrt(standing ** lean) + 1 for standing in range(1, number_of + 1)]
    largest = bound if full else min(bound, max(-(-total // number_of), total * weights[0] // sum(weights)))
    least = 1 if total - largest >= number_of - 1 else 0
    given, surplus = [largest] + [least] * (number_of - 1), total - largest - least * (number_of - 1)
    while surplus > 0:
        movable = [i for i in range(1, number_of) if given[i] < largest] or [i for i in range(1, number_of) if given[i] < bound]
        whole, left = sum([weights[i] for i in movable]), surplus
        for i in movable:
            extra = min(bound - given[i], max(1, left * weights[i] // whole), surplus)
            given[i] = given[i] + extra
            surplus = surplus - extra
    return np.array(given)


def noise(rng, dims, width, reach, shards=(), kind=jnp.bfloat16):
    array = width * jax.random.normal(rng, dims, jnp.float32)
    if shards:
        array = array * steps_of(rng, dims, shards, -0.22, 0.18)
    return jnp.clip(array, -reach, reach).astype(kind)


def setup_inputs(seed: int = 0) -> dict:
    splits = jax.random.split(jax.random.key(seed), 17)
    layer_in = noise(splits[0], (SEQS, LEN, D), 1.0, 6.0, ((0, 4), (1, 8)))
    segment_ids = jax.vmap(lambda own: jnp.searchsorted(jnp.cumsum(ragged_sizes(own, DOCS, LEN, DOC_MAX, 1)), jnp.arange(LEN), side="right"))(jax.random.split(splits[1], SEQS)).reshape((SEQS, LEN)).astype(jnp.int32)
    routing_keys = jax.random.split(jax.random.fold_in(splits[2], 1), SEQS * LEN // TOK_DEV)
    routing_turns = jax.random.permutation(jax.random.fold_in(splits[2], 3), SEQS * LEN // TOK_DEV)
    routing = jax.vmap(lambda own, number: assign_block(jax.random.fold_in(splits[2], 2), own, number, TOK_DEV, EXPERTS, TOPK, CAP, 1))(routing_keys, routing_turns).reshape((SEQS, LEN, TOPK))
    out_grad = noise(splits[3], (SEQS, LEN, D), 1.0, 6.0, ((0, 4), (1, 8)))
    attn_gain = jnp.clip(1.0 + 0.1 * jax.random.normal(splits[4], (D,), jnp.float32), 0.5, 1.5)
    w_query = noise(splits[5], (D, D), D ** -0.5, 0.125)
    w_key = noise(splits[6], (D, D), D ** -0.5, 0.125)
    w_value = noise(splits[7], (D, D), D ** -0.5, 0.125)
    query_gain = jnp.clip(1.0 + 0.1 * jax.random.normal(splits[8], (D,), jnp.float32), 0.5, 1.5)
    key_gain = jnp.clip(1.0 + 0.1 * jax.random.normal(splits[9], (D,), jnp.float32), 0.5, 1.5)
    w_out = noise(splits[10], (D, D), (max(1, D // 64)) ** -0.5, 1.0)
    mlp_gain = jnp.clip(1.0 + 0.1 * jax.random.normal(splits[11], (D,), jnp.float32), 0.5, 1.5)
    w_router = noise(splits[12], (D, EXPERTS), (4 * D) ** -0.5, 0.0625)
    w_gate = noise(splits[13], (EXPERTS, D, FF_E), D ** -0.5, 0.125, ((0, 4), (1, 8)))
    w_up = noise(splits[14], (EXPERTS, D, FF_E), D ** -0.5, 0.125, ((0, 4), (1, 8)))
    w_down = noise(splits[15], (EXPERTS, FF_E, D), (max(1, FF_E // 100)) ** -0.5, 2.0, ((0, 4), (2, 8)))
    return {"layer_in": layer_in, "segment_ids": segment_ids, "routing": routing, "out_grad": out_grad, "attn_gain": attn_gain, "w_query": w_query, "w_key": w_key, "w_value": w_value, "query_gain": query_gain, "key_gain": key_gain, "w_out": w_out, "mlp_gain": mlp_gain, "w_router": w_router, "w_gate": w_gate, "w_up": w_up, "w_down": w_down}


@jax.custom_vjp
def low(v):
    return lax.optimization_barrier(v.astype(jnp.bfloat16)).astype(jnp.float32)

@jax.custom_vjp
def low_back(v):
    return v

def low_keep(v):
    return (low(v), None)

def low_pass(kept, grad):
    return (grad,)

def back_keep(v):
    return (v, None)

def back_low(kept, grad):
    return (low(grad),)
low.defvjp(low_keep, low_pass)
low_back.defvjp(back_keep, back_low)
EPSILON = 1e-05
MASKED = -1000000000.0
HIGHEST = lax.Precision.HIGHEST

def rms_norm(values_in, gain_vec):
    return values_in * lax.rsqrt(lax.optimization_barrier(jnp.mean(values_in * values_in, axis=-1, keepdims=True)) + EPSILON) * gain_vec

def angles(row_start, row_count, head_dim):
    places = (row_start + jnp.arange(row_count, dtype=jnp.int32)).astype(jnp.float32)
    frequency = jnp.exp(-math.log(10000.0) * 2.0 * jnp.arange(head_dim // 2, dtype=jnp.float32) / head_dim)
    turn_angle = places[:, None] * frequency[None, :]
    return (jnp.cos(turn_angle)[:, None, :], jnp.sin(turn_angle)[:, None, :])

def rotate(values_in, cosine, sine):
    half_dim = values_in.shape[-1] // 2
    first_half = values_in[..., :half_dim]
    second = values_in[..., half_dim:]
    return jnp.concatenate([first_half * cosine - second * sine, second * cosine + first_half * sine], axis=-1)

def attend_one(items):
    queries, key_rows, value_rows, seg_row = items
    positions = jnp.arange(LEN, dtype=jnp.int32)
    raw_scores = low_back(jnp.einsum('qhd,khd->hqk', queries, key_rows, precision=HIGHEST)) * (1.0 / math.sqrt(HEAD_DIM))
    allowed = (seg_row[:, None] == seg_row[None, :]) & (positions[None, :] <= positions[:, None])
    probs = low(jax.nn.softmax(jnp.where(allowed[None], raw_scores, MASKED), axis=-1))
    return low(low_back(jnp.einsum('hqk,khd->qhd', probs, value_rows, precision=HIGHEST)))

def reference(layer_in, segment_ids, routing, out_grad, attn_gain, w_query, w_key, w_value, query_gain, key_gain, w_out, mlp_gain, w_router, w_gate, w_up, w_down):
    cosine, sine = angles(0, LEN, HEAD_DIM)
    flat_route = routing.reshape(-1)
    pad_index = TOKENS * TOPK
    slot_cap = CAP * N_GROUP * N_EXPERT
    pick_table = jnp.stack([jnp.nonzero(flat_route == expert_id, size=slot_cap, fill_value=pad_index)[0].astype(jnp.int32) for expert_id in range(EXPERTS)])
    row_table = (pick_table // TOPK).astype(jnp.int32)
    route_rows = routing.reshape(TOKENS, TOPK)

    def layer(inputs, attn_gain_f, w_query_f, w_key_f, w_value_f, query_gain_f, key_gain_f, w_out_f, mlp_gain_f, w_router_f, w_gate_f, w_up_f, w_down_f):
        rows_in = inputs.reshape(TOKENS, D)
        normed = low(rms_norm(rows_in, attn_gain_f))
        query_raw = low_back(jnp.dot(normed, w_query_f, precision=HIGHEST))
        key_raw = low_back(jnp.dot(normed, w_key_f, precision=HIGHEST))
        value_rows = low(low_back(jnp.dot(normed, w_value_f, precision=HIGHEST)))
        queries = low(rotate(rms_norm(query_raw, query_gain_f).reshape(SEQS, LEN, HEADS, HEAD_DIM), cosine, sine))
        key_rows = low(rotate(rms_norm(key_raw, key_gain_f).reshape(SEQS, LEN, HEADS, HEAD_DIM), cosine, sine))
        mixed = lax.map(jax.checkpoint(attend_one), (queries, key_rows, value_rows.reshape(SEQS, LEN, HEADS, HEAD_DIM), segment_ids))
        attn_out = low_back(jnp.dot(mixed.reshape(TOKENS, D), w_out_f, precision=HIGHEST))
        resid = rows_in + attn_out
        normed_mlp = low(rms_norm(resid, mlp_gain_f))
        logits = low_back(jnp.dot(normed_mlp, w_router_f, precision=HIGHEST))
        router = jax.nn.softmax(logits, axis=-1)
        picked = jnp.take_along_axis(router, route_rows, axis=1).reshape(-1)
        picked_pad = jnp.concatenate([picked, jnp.zeros((1,), jnp.float32)])
        normed_pad = jnp.concatenate([normed_mlp, jnp.zeros((1, D), jnp.float32)], axis=0)

        def expert_step(total, items):
            gate_w, up_w, down_w, row_ids, pick_ids = items
            expert_in = low_back(jnp.take(normed_pad, row_ids, axis=0))
            gate_pre = low_back(jnp.dot(expert_in, gate_w, precision=HIGHEST))
            up_pre = low_back(jnp.dot(expert_in, up_w, precision=HIGHEST))
            hidden = low(jax.nn.silu(gate_pre) * up_pre)
            expert_out = low(low_back(jnp.dot(hidden, down_w, precision=HIGHEST)))
            weights = jnp.take(picked_pad, pick_ids)
            return (total.at[row_ids].add(weights[:, None] * expert_out), None)
        mixture, _ = lax.scan(jax.checkpoint(expert_step), jnp.zeros((TOKENS + 1, D), jnp.float32), (w_gate_f, w_up_f, w_down_f, row_table, pick_table))
        return (resid + mixture[:TOKENS]).reshape(SEQS, LEN, D)
    floats = (layer_in.astype(jnp.float32), attn_gain.astype(jnp.float32), w_query.astype(jnp.float32), w_key.astype(jnp.float32), w_value.astype(jnp.float32), query_gain.astype(jnp.float32), key_gain.astype(jnp.float32), w_out.astype(jnp.float32), mlp_gain.astype(jnp.float32), w_router.astype(jnp.float32), w_gate.astype(jnp.float32), w_up.astype(jnp.float32), w_down.astype(jnp.float32))
    result, layer_back = jax.vjp(layer, *floats)
    grads = layer_back(out_grad.astype(jnp.float32))
    return (result.astype(jnp.bfloat16), grads[0], grads[1], grads[2], grads[3], grads[4], grads[5], grads[6], grads[7], grads[8], grads[9], grads[10], grads[11], grads[12])
```

```python
import math

import jax
import jax.numpy as jnp
from jax import lax
from jax.sharding import PartitionSpec as P

HEADS = 16
EPSILON = 1e-05
MASKED = -1000000000.0
BF16 = jnp.bfloat16
F32 = jnp.float32


def rms_norm(values_in, gain_vec):
    return (
        values_in
        * lax.rsqrt(jnp.mean(values_in * values_in, axis=-1, keepdims=True) + EPSILON)
        * gain_vec
    )


def angles(row_count, head_dim):
    places = jnp.arange(row_count, dtype=jnp.int32).astype(F32)
    frequency = jnp.exp(-math.log(10000.0) * 2.0 * jnp.arange(head_dim // 2, dtype=F32) / head_dim)
    turn_angle = places[:, None] * frequency[None, :]
    return (jnp.cos(turn_angle)[:, None, :], jnp.sin(turn_angle)[:, None, :])


def rotate(values_in, cosine, sine):
    half_dim = values_in.shape[-1] // 2
    first_half = values_in[..., :half_dim]
    second = values_in[..., half_dim:]
    return jnp.concatenate(
        [first_half * cosine - second * sine, second * cosine + first_half * sine], axis=-1
    )


def mm(left, right):
    return jnp.dot(left, right, preferred_element_type=F32)


def mm_tn(left, right):
    return lax.dot_general(left, right, (((0,), (0,)), ((), ())), preferred_element_type=F32)


def mm_nt(left, right):
    return lax.dot_general(left, right, (((1,), (1,)), ((), ())), preferred_element_type=F32)


def ein(spec, *ops):
    return jnp.einsum(spec, *ops, preferred_element_type=F32)


def shards(
    layer_in,
    segment_ids,
    routing,
    out_grad,
    attn_gain,
    w_query,
    w_key,
    w_value,
    query_gain,
    key_gain,
    w_out,
    mlp_gain,
    w_router,
    w_gate,
    w_up,
    w_down,
):
    groups = lax.axis_size("group")
    sources = lax.axis_size("expert")
    me = lax.axis_index("group")
    rows = layer_in.shape[1]
    width = layer_in.shape[2]
    length = rows * groups
    head_dim = width // HEADS
    heads = HEADS // groups
    cols = width // groups
    local_experts = w_gate.shape[0]
    experts = local_experts * sources
    hidden_size = w_gate.shape[2]
    parts = groups // local_experts
    part = hidden_size // parts
    score_scale = 1.0 / math.sqrt(head_dim)

    def gather(block):
        return lax.all_gather(block, "group", axis=0, tiled=True)

    def own_cols(matrix, axis):
        return lax.dynamic_slice_in_dim(matrix, me * cols, cols, axis)

    def slices_in(w):
        w = w.reshape(local_experts, w.shape[1], parts, part).transpose(0, 2, 1, 3)
        w = w.reshape(groups, w.shape[2], part)
        w = lax.all_to_all(w, "group", 0, 0, tiled=True).reshape(width, part)
        return lax.all_gather(w, "expert", axis=0, tiled=False)

    gate_w = slices_in(w_gate)
    up_w = slices_in(w_up)
    down_w = w_down.reshape(groups, part, cols)
    down_w = lax.all_to_all(down_w, "group", 0, 0, tiled=True).transpose(1, 0, 2)
    down_w = lax.all_gather(down_w.reshape(part, width), "expert", axis=0, tiled=False)

    inputs = layer_in[0].astype(F32)
    normed_b = rms_norm(inputs, attn_gain).astype(BF16)
    normed_all = gather(normed_b)
    seg_all = gather(segment_ids[0])
    route_all = gather(routing[0])
    grad_all = gather(out_grad[0])
    wq, wk, wv = own_cols(w_query, 1), own_cols(w_key, 1), own_cols(w_value, 1)
    query_raw, key_raw = mm(normed_all, wq), mm(normed_all, wk)
    values_b = mm(normed_all, wv).astype(BF16).reshape(length, heads, head_dim)
    squares = jnp.stack(
        [jnp.sum(query_raw * query_raw, axis=1), jnp.sum(key_raw * key_raw, axis=1)], axis=1
    )
    scales = lax.rsqrt(lax.psum(squares, "group") / width + EPSILON)
    query_scale, key_scale = scales[:, :1], scales[:, 1:]
    query_gain_c, key_gain_c = own_cols(query_gain, 0), own_cols(key_gain, 0)
    cosine, sine = angles(length, head_dim)

    def turned(raw, scale, gain):
        return rotate((raw * scale * gain).reshape(length, heads, head_dim), cosine, sine)

    queries_b = turned(query_raw, query_scale, query_gain_c).astype(BF16)
    keys_b = turned(key_raw, key_scale, key_gain_c).astype(BF16)
    place = jnp.arange(length, dtype=jnp.int32)
    allowed = (seg_all[:, None] == seg_all[None, :]) & (place[None, :] <= place[:, None])
    scores = jnp.where(allowed[None], ein("qhd,khd->hqk", queries_b, keys_b) * score_scale, MASKED)
    top_score = jnp.max(scores, axis=-1, keepdims=True)
    log_total = top_score + jnp.log(jnp.sum(jnp.exp(scores - top_score), axis=-1, keepdims=True))
    probs = jnp.exp(scores - log_total)
    probs_b = probs.astype(BF16)
    mixed_c = ein("hqk,khd->qhd", probs_b, values_b).reshape(length, cols).astype(BF16)
    mixed_b = lax.all_to_all(mixed_c, "group", 0, 1, tiled=True)
    resid = inputs + mm(mixed_b, w_out)
    normed_mlp_b = rms_norm(resid, mlp_gain).astype(BF16)
    mlp_all = gather(normed_mlp_b)

    expert_ids = jnp.arange(experts, dtype=jnp.int32)
    chosen = jnp.any(route_all[:, :, None] == expert_ids[None, None, :], axis=1)
    router_all = jax.nn.softmax(mm(mlp_all, w_router), axis=-1)
    picked = jnp.where(chosen, router_all, 0.0).reshape(length, sources, local_experts)
    picked = lax.dynamic_index_in_dim(picked, me // parts, 2, keepdims=True)
    gate_pre = ein("td,edf->tef", mlp_all, gate_w)
    up_pre = ein("td,edf->tef", mlp_all, up_w)
    sigma = jax.nn.sigmoid(gate_pre)
    hidden = gate_pre * sigma * up_pre
    hidden_b = (hidden * picked).astype(BF16)
    out_part = ein("tef,efd->td", hidden_b, down_w).astype(BF16)
    mixture = lax.psum_scatter(out_part, "group", scatter_dimension=0, tiled=True)
    hidden_grad = ein("td,efd->tef", grad_all, down_w)
    picked_grad = jnp.sum(hidden * hidden_grad, axis=2)
    hidden_grad = hidden_grad * picked
    gate_grad_b = (hidden_grad * up_pre * sigma * (1.0 + gate_pre * (1.0 - sigma))).astype(BF16)
    up_grad_b = (hidden_grad * gate_pre * sigma).astype(BF16)
    slot_part = ein("tef,edf->td", gate_grad_b, gate_w) + ein("tef,edf->td", up_grad_b, up_w)
    slot_sum = lax.psum_scatter(slot_part.astype(BF16), "group", scatter_dimension=0, tiled=True)
    own_expert = jnp.arange(local_experts, dtype=jnp.int32) == me // parts
    full_part = jnp.where(own_expert[None, None, :], picked_grad[:, :, None], 0.0)
    full_part = jnp.where(chosen, full_part.reshape(length, experts), 0.0)
    router_full_grad = lax.psum_scatter(full_part, "group", scatter_dimension=0, tiled=True)
    gate_w_part = ein("td,tef->edf", mlp_all, gate_grad_b).astype(BF16)
    up_w_part = ein("td,tef->edf", mlp_all, up_grad_b).astype(BF16)
    down_w_part = ein("tef,td->efd", hidden_b, grad_all).astype(BF16)

    def slices_out(w):
        w = lax.psum_scatter(w, "expert", scatter_dimension=0, tiled=False)
        w = lax.all_to_all(w.reshape(groups, cols, part), "group", 0, 0, tiled=True)
        w = w.reshape(local_experts, parts, cols, part).transpose(0, 2, 1, 3)
        return w.reshape(local_experts, cols, hidden_size).astype(F32)

    gate_sum = slices_out(gate_w_part)
    up_sum = slices_out(up_w_part)
    down_sum = lax.psum_scatter(down_w_part, "expert", scatter_dimension=0, tiled=False)
    down_sum = down_sum.reshape(part, groups, cols).transpose(1, 0, 2)
    down_sum = lax.all_to_all(down_sum, "group", 0, 0, tiled=True)
    down_sum = down_sum.reshape(local_experts, hidden_size, cols).astype(F32)

    result = (resid + mixture.astype(F32)).astype(BF16)
    grad_out = out_grad[0].astype(F32)
    router = jax.nn.softmax(mm(normed_mlp_b, w_router), axis=-1)
    logits_grad_b = (
        router * (router_full_grad - jnp.sum(router * router_full_grad, axis=-1, keepdims=True))
    ).astype(BF16)
    router_w_grad = mm_tn(normed_mlp_b, logits_grad_b)
    mlp_in_grad = slot_sum.astype(F32) + mm_nt(logits_grad_b, w_router)
    _, mlp_back = jax.vjp(rms_norm, resid, mlp_gain)
    resid_part, mlp_gain_grad = mlp_back(mlp_in_grad)
    resid_grad = grad_out + resid_part
    attn_grad_b = resid_grad.astype(BF16)
    attn_grad_all = gather(attn_grad_b)
    out_w_part = mm_tn(mixed_c, attn_grad_all).astype(BF16)
    out_w_grad = lax.psum_scatter(out_w_part, "expert", scatter_dimension=0, tiled=True)
    mixed_grad_b = mm_nt(attn_grad_b, w_out).astype(BF16)
    mixed_grad_c = lax.all_to_all(mixed_grad_b, "group", 1, 0, tiled=True)
    mixed_grad_c = mixed_grad_c.reshape(length, heads, head_dim)

    prob_grad = ein("qhd,khd->hqk", mixed_grad_c, values_b)
    delta = jnp.sum(probs * prob_grad, axis=-1, keepdims=True)
    score_grad_b = (probs * (prob_grad - delta) * score_scale).astype(BF16)
    query_grad = ein("hqk,khd->qhd", score_grad_b, keys_b)
    key_grad = ein("hqk,qhd->khd", score_grad_b, queries_b)
    value_grad_b = ein("hqk,qhd->khd", probs_b, mixed_grad_c).astype(BF16).reshape(length, cols)

    def unturned(grad):
        return rotate(grad, cosine, -sine).reshape(length, cols)

    query_turn, key_turn = unturned(query_grad), unturned(key_grad)
    query_mix, key_mix = query_turn * query_gain_c, key_turn * key_gain_c
    dots = jnp.stack(
        [jnp.sum(query_mix * query_raw, axis=1), jnp.sum(key_mix * key_raw, axis=1)], axis=1
    )
    dots = lax.psum(dots, "group") / width
    query_raw_b = (
        query_scale * query_mix - query_raw * query_scale**3 * dots[:, :1]
    ).astype(BF16)
    key_raw_b = (key_scale * key_mix - key_raw * key_scale**3 * dots[:, 1:]).astype(BF16)
    query_gain_part = jnp.sum(query_turn * query_raw * query_scale, axis=0)
    key_gain_part = jnp.sum(key_turn * key_raw * key_scale, axis=0)
    raw_grads = jnp.concatenate([query_raw_b, key_raw_b, value_grad_b], axis=1)
    qkv_part = mm_tn(normed_all, raw_grads).astype(BF16).reshape(groups, sources, -1, 3 * cols)
    qkv_part = lax.psum_scatter(qkv_part, "expert", scatter_dimension=1, tiled=False)
    qkv_part = lax.all_to_all(qkv_part, "group", 0, 0, tiled=True)
    qkv_part = qkv_part.transpose(1, 0, 2).reshape(-1, groups, 3, cols).astype(F32)
    gain_part = jnp.stack([query_gain_part, key_gain_part])
    gain_grads = lax.psum_scatter(gain_part, "expert", scatter_dimension=1, tiled=True)
    raw_own = lax.all_to_all(raw_grads, "group", 0, 1, tiled=True).reshape(rows, groups, 3, cols)
    normed_grad = (
        mm_nt(raw_own[:, :, 0].reshape(rows, width), w_query)
        + mm_nt(raw_own[:, :, 1].reshape(rows, width), w_key)
        + mm_nt(raw_own[:, :, 2].reshape(rows, width), w_value)
    )
    _, attn_back = jax.vjp(rms_norm, inputs, attn_gain)
    input_part, attn_gain_grad = attn_back(normed_grad)
    input_grad = resid_grad + input_part
    small = jnp.concatenate(
        [router_w_grad, mlp_gain_grad[:, None], attn_gain_grad[:, None]], axis=1
    )
    small = lax.psum_scatter(small, ("group", "expert"), scatter_dimension=0, tiled=True)
    return (
        result[None],
        input_grad[None],
        small[:, experts + 1],
        qkv_part[:, :, 0].reshape(-1, width),
        qkv_part[:, :, 1].reshape(-1, width),
        qkv_part[:, :, 2].reshape(-1, width),
        gain_grads[0],
        gain_grads[1],
        out_w_grad.astype(F32),
        small[:, experts],
        small[:, :experts],
        gate_sum,
        up_sum,
        down_sum,
    )


def solution(mesh):
    token = P("expert", "group", None)
    every = P(("group", "expert"))
    return jax.shard_map(
        shards,
        mesh=mesh,
        in_specs=(token, P("expert", "group"), token, token)
        + (P(),) * 9
        + (token, token, P("expert", None, "group")),
        out_specs=(token, token)
        + (every,) * 9
        + (token, token, P("expert", None, "group")),
        check_vma=False,
    )
```

```python
import functools
import math

import jax
import jax.numpy as jnp
from jax import lax
from jax.experimental import pallas as pl
from jax.experimental.pallas import tpu as pltpu
from jax.sharding import PartitionSpec as P

HEADS = 16
EPSILON = 1e-05
MASKED = -1000000000.0
BF16 = jnp.bfloat16
F32 = jnp.float32
MESH = pl.DeviceIdType.MESH
DMA = pltpu.SemaphoreType.DMA
VMEM_SPEC = pl.BlockSpec(memory_space=pltpu.VMEM)


def remote(src, dst, send_sem, recv_sem, where):
    return pltpu.make_async_remote_copy(
        src, dst, send_sem, recv_sem, device_id=where, device_id_type=MESH
    )


def comm_params(collective_id):
    return pltpu.CompilerParams(collective_id=collective_id, has_side_effects=True)


def greet(peers):
    barrier = pltpu.get_barrier_semaphore()
    total = 0
    for here, where in peers:

        @pl.when(here)
        def _(where=where):
            pl.semaphore_signal(barrier, inc=1, device_id=where, device_id_type=MESH)

        total = total + jnp.where(here, 1, 0)
    pl.semaphore_wait(barrier, total)


def greet_all(count, device):
    barrier = pltpu.get_barrier_semaphore()

    def body(k, carry):
        pl.semaphore_signal(barrier, inc=1, device_id=device(k), device_id_type=MESH)
        return carry

    lax.fori_loop(1, count, body, 0)
    pl.semaphore_wait(barrier, count - 1)


def gather_kernel(nz, ny, pieces, block, out, own_sem, send_sem, recv_sem):
    me = lax.axis_index("group")
    z, y = me // ny, me % ny
    rows = block.shape[0] // pieces

    def at(z_to, y_to):
        return {"group": z_to * ny + y_to}

    greet(
        [
            (z > 0, at(z - 1, y)),
            (z < nz - 1, at(z + 1, y)),
            (y > 0, at(z, y - 1)),
            (y < ny - 1, at(z, y + 1)),
        ]
    )
    own = pltpu.make_async_copy(block, out.at[me], own_sem)
    own.start()

    def part(ref, c):
        return ref.at[pl.ds(c * rows, rows)]

    def copy(slot, source, c, where, first):
        return remote(
            part(block, c) if first else part(out.at[source], c),
            part(out.at[source], c),
            send_sem.at[slot, source, c],
            recv_sem.at[source, c],
            where,
        )

    def outgoing(source, go):
        sz, sy = source // ny, source % ny
        column = go & (sy == y)
        return [
            (column & (sz <= z) & (z < nz - 1), 0, at(z + 1, y)),
            (column & (sz >= z) & (z > 0), 1, at(z - 1, y)),
            (go & (sy <= y) & (y < ny - 1), 2, at(z, y + 1)),
            (go & (sy >= y) & (y > 0), 3, at(z, y - 1)),
        ]

    def act(source, first, go, start):
        for c in range(pieces):
            if start and not first:

                @pl.when(go)
                def _():
                    copy(0, source, c, at(z, y), False).wait_recv()

            for cond, slot, where in outgoing(source, go):

                @pl.when(cond)
                def _(slot=slot, where=where):
                    one = copy(slot, source, c, where, first)
                    if start:
                        one.start()
                    else:
                        one.wait_send()

    order = []
    for dz in range(nz):
        for sz in [z] if dz == 0 else [z - dz, z + dz]:
            for dy in range(ny):
                for sy in [y] if dy == 0 else [y - dy, y + dy]:
                    inside = (sz >= 0) & (sz < nz) & (sy >= 0) & (sy < ny)
                    source = jnp.clip(sz, 0, nz - 1) * ny + jnp.clip(sy, 0, ny - 1)
                    order.append((dz + dy, dz, source, inside))
    order = sorted(order, key=lambda t: (t[0], -t[1]))
    for start in (True, False):
        for distance, _, source, inside in order:
            act(source, distance == 0, inside, start)
        if start:
            own.wait()


def gather_rows(block, groups, collective_id, pieces=2):
    nz = min(4, groups)
    return pl.pallas_call(
        functools.partial(gather_kernel, nz, groups // nz, pieces),
        name="gather_rows",
        out_shape=jax.ShapeDtypeStruct((groups,) + block.shape, block.dtype),
        in_specs=[VMEM_SPEC],
        out_specs=pl.BlockSpec(memory_space=pl.ANY),
        scratch_shapes=[DMA, DMA((4, groups, pieces)), DMA((groups, pieces))],
        compiler_params=comm_params(collective_id),
        cost_estimate=pl.CostEstimate(flops=0, bytes_accessed=100_000_000, transcendentals=0),
    )(block).reshape(groups * block.shape[0], block.shape[1])


def reduce_kernel(nz, ny, pieces, parts, out, ybuf, zbuf, ysend, yrecv, zsend, zrecv):
    me = lax.axis_index("group")
    z, y = me // ny, me % ny
    rows = parts.shape[1] // pieces

    def at(z_to, y_to):
        return {"group": z_to * ny + y_to}

    greet([(z > 0, at(z - 1, y)), (z < nz - 1, at(z + 1, y)), (z >= 0, at(z, 1 - y))])

    def part(ref, c):
        return ref.at[pl.ds(c * rows, rows)]

    def y_copy(dest, c):
        src, dst = part(parts.at[dest * ny + 1 - y], c), part(ybuf.at[dest], c)
        return remote(src, dst, ysend.at[dest, c], yrecv.at[dest, c], at(z, 1 - y))

    def z_copy(side, dest, c):
        src, dst = part(ybuf.at[dest], c), part(zbuf.at[side, dest], c)
        where = at(z - 1, y) if side else at(z + 1, y)
        return remote(src, dst, zsend.at[dest, c], zrecv.at[side, dest, c], where)

    order = []
    for d in range(nz - 1, 0, -1):
        order += [(z + d, z + d < nz, 0), (z - d, z - d >= 0, 1)]
    order = [(jnp.clip(dest, 0, nz - 1), inside, side) for dest, inside, side in order]
    for dest, inside, side in order:

        @pl.when(inside)
        def _():
            for c in range(pieces):
                y_copy(dest, c).start()

    for c in range(pieces):
        y_copy(z, c).start()
    for dest, inside, side in order:
        further = (z < nz - 1) if side else (z > 0)
        for c in range(pieces):
            span = pl.ds(c * rows, rows)

            @pl.when(inside)
            def _():
                y_copy(dest, c).wait_recv()
                pair = parts[dest * ny + y, span, :].astype(F32) + ybuf[dest, span, :].astype(F32)

                @pl.when(further)
                def _():
                    z_copy(side, dest, c).wait_recv()
                    ybuf[dest, span, :] = (pair + zbuf[side, dest, span, :].astype(F32)).astype(BF16)

                @pl.when(jnp.logical_not(further))
                def _():
                    ybuf[dest, span, :] = pair.astype(BF16)

                z_copy(side, dest, c).start()

    for c in range(pieces):
        span = pl.ds(c * rows, rows)
        y_copy(z, c).wait_recv()
        out[span, :] = parts[me, span, :].astype(F32) + ybuf[z, span, :].astype(F32)

        @pl.when(z > 0)
        def _():
            z_copy(0, z, c).wait_recv()
            out[span, :] += zbuf[0, z, span, :].astype(F32)

        @pl.when(z < nz - 1)
        def _():
            z_copy(1, z, c).wait_recv()
            out[span, :] += zbuf[1, z, span, :].astype(F32)

    for dest, inside, side in order:

        @pl.when(inside)
        def _():
            for c in range(pieces):
                y_copy(dest, c).wait_send()
                z_copy(side, dest, c).wait_send()

    for c in range(pieces):
        y_copy(z, c).wait_send()


def reduce_rows(parts, groups, collective_id, pieces=2):
    nz = min(4, groups)
    ny = groups // nz
    if ny != 2:
        return lax.psum_scatter(parts, "group", scatter_dimension=0, tiled=True).astype(F32)
    rows, width = parts.shape[0] // groups, parts.shape[1]
    return pl.pallas_call(
        functools.partial(reduce_kernel, nz, ny, pieces),
        name="reduce_rows",
        out_shape=jax.ShapeDtypeStruct((rows, width), F32),
        in_specs=[VMEM_SPEC],
        out_specs=VMEM_SPEC,
        scratch_shapes=[
            pltpu.VMEM((nz, rows, width), BF16),
            pltpu.VMEM((2, nz, rows, width), BF16),
            DMA((nz, pieces)),
            DMA((nz, pieces)),
            DMA((nz, pieces)),
            DMA((2, nz, pieces)),
        ],
        compiler_params=comm_params(collective_id),
        cost_estimate=pl.CostEstimate(flops=0, bytes_accessed=100_000_000, transcendentals=0),
    )(parts.reshape(groups, rows, width))


def swap_kernel(groups, to_rows, *refs):
    count = (len(refs) - 2) // 2
    ins, outs, (send_sem, recv_sem) = refs[:count], refs[count : 2 * count], refs[2 * count :]
    me = lax.axis_index("group")
    columns = ins[0].shape[-1] // (groups if to_rows else 1)
    wide = lambda ref, i: ref.at[:, pl.ds(pl.multiple_of(i * columns, columns), columns)]
    thin = lambda ref, i: ref.at[i]
    source, target = (wide, thin) if to_rows else (thin, wide)

    def peer(k):
        return lax.rem(me + k, groups)

    greet_all(groups, lambda k: {"group": peer(k)})

    def copy(n, k):
        to = peer(k)
        return remote(
            source(ins[n], to), target(outs[n], me), send_sem.at[n, k], recv_sem.at[n, k], {"group": to}
        )

    for k in range(1, groups):
        for n in range(count):
            copy(n, k).start()
    for n in range(count):
        if to_rows:
            outs[n][me] = ins[n][:, pl.ds(pl.multiple_of(me * columns, columns), columns)]
        else:
            outs[n][:, pl.ds(pl.multiple_of(me * columns, columns), columns)] = ins[n][me]
    for k in range(1, groups):
        for n in range(count):
            copy(n, k).wait()


def swap(arrays, groups, to_rows, collective_id):
    shape, count = arrays[0].shape, len(arrays)
    if to_rows:
        rows, columns = shape[0], shape[1] // groups
        out = (groups, rows, columns)
    else:
        rows, columns = shape[0] // groups, shape[1]
        arrays = [a.reshape(groups, rows, columns) for a in arrays]
        out = (rows, groups * columns)
    outs = pl.pallas_call(
        functools.partial(swap_kernel, groups, to_rows),
        name="swap",
        out_shape=[jax.ShapeDtypeStruct(out, a.dtype) for a in arrays],
        in_specs=[VMEM_SPEC] * count,
        out_specs=[VMEM_SPEC] * count,
        scratch_shapes=[DMA((count, groups)), DMA((count, groups))],
        compiler_params=comm_params(collective_id),
        cost_estimate=pl.CostEstimate(flops=0, bytes_accessed=30_000_000, transcendentals=0),
    )(*arrays)
    return [o.reshape(groups * rows, columns) if to_rows else o for o in outs]


def small_sum_kernel(axes, scatter, values, out, landed, send_sem, recv_sem):
    sizes = [lax.axis_size(a) for a in axes]
    count = math.prod(sizes)
    me = 0
    for a, n in zip(axes, sizes):
        me = me * n + lax.axis_index(a)

    def peer(k):
        return lax.rem(me + k, count)

    def device(k):
        to = peer(k)
        if len(axes) == 1:
            return {axes[0]: to}
        return {axes[0]: to // sizes[1], axes[1]: lax.rem(to, sizes[1])}

    greet_all(count, device)

    def copy(k):
        src = values.at[peer(k)] if scatter else values
        return remote(src, landed.at[k], send_sem.at[k], recv_sem.at[k], device(k))

    def start(k, carry):
        copy(k).start()
        return carry

    def wait(k, carry):
        copy(k).wait()
        return carry

    lax.fori_loop(1, count, start, 0)
    landed[0] = values[me] if scatter else values[...]
    lax.fori_loop(1, count, wait, 0)
    out[...] = jnp.sum(landed[...], axis=0)


def small_sum(values, axes, scatter, collective_id):
    count = math.prod(lax.axis_size(a) for a in axes)
    shape = values.shape[-2:]
    return pl.pallas_call(
        functools.partial(small_sum_kernel, axes, scatter),
        name="small_sum",
        out_shape=jax.ShapeDtypeStruct(shape, F32),
        in_specs=[VMEM_SPEC],
        out_specs=VMEM_SPEC,
        scratch_shapes=[pltpu.VMEM((count,) + shape, F32), DMA((count,)), DMA((count,))],
        compiler_params=comm_params(collective_id),
        cost_estimate=pl.CostEstimate(flops=0, bytes_accessed=10_000_000, transcendentals=0),
    )(values)


def rms_norm(values_in, gain_vec):
    return (
        values_in
        * lax.rsqrt(jnp.mean(values_in * values_in, axis=-1, keepdims=True) + EPSILON)
        * gain_vec
    )


def angles(row_count, head_dim):
    places = jnp.arange(row_count, dtype=jnp.int32).astype(F32)
    frequency = jnp.exp(-math.log(10000.0) * 2.0 * jnp.arange(head_dim // 2, dtype=F32) / head_dim)
    turn_angle = places[:, None] * frequency[None, :]
    return (jnp.cos(turn_angle)[:, None, :], jnp.sin(turn_angle)[:, None, :])


def rotate(values_in, cosine, sine):
    half_dim = values_in.shape[-1] // 2
    first_half = values_in[..., :half_dim]
    second = values_in[..., half_dim:]
    return jnp.concatenate(
        [first_half * cosine - second * sine, second * cosine + first_half * sine], axis=-1
    )


def mm(left, right):
    return jnp.dot(left, right, preferred_element_type=F32)


def mm_tn(left, right):
    return lax.dot_general(left, right, (((0,), (0,)), ((), ())), preferred_element_type=F32)


def mm_nt(left, right):
    return lax.dot_general(left, right, (((1,), (1,)), ((), ())), preferred_element_type=F32)


def ein(spec, *ops):
    return jnp.einsum(spec, *ops, preferred_element_type=F32)


def shards(
    layer_in,
    segment_ids,
    routing,
    out_grad,
    attn_gain,
    w_query,
    w_key,
    w_value,
    query_gain,
    key_gain,
    w_out,
    mlp_gain,
    w_router,
    w_gate,
    w_up,
    w_down,
):
    groups = lax.axis_size("group")
    sources = lax.axis_size("expert")
    me = lax.axis_index("group")
    rows = layer_in.shape[1]
    width = layer_in.shape[2]
    length = rows * groups
    head_dim = width // HEADS
    heads = HEADS // groups
    cols = width // groups
    local_experts = w_gate.shape[0]
    experts = local_experts * sources
    hidden_size = w_gate.shape[2]
    parts = groups // local_experts
    part = hidden_size // parts
    score_scale = 1.0 / math.sqrt(head_dim)

    def gather(block):
        return lax.all_gather(block, "group", axis=0, tiled=True)

    def own_cols(matrix, axis):
        return lax.dynamic_slice_in_dim(matrix, me * cols, cols, axis)

    def slices_in(w):
        w = w.reshape(local_experts, w.shape[1], parts, part).transpose(0, 2, 1, 3)
        w = w.reshape(groups, w.shape[2], part)
        w = lax.all_to_all(w, "group", 0, 0, tiled=True).reshape(width, part)
        return lax.all_gather(w, "expert", axis=0, tiled=False)

    gate_w = slices_in(w_gate)
    up_w = slices_in(w_up)
    down_w = w_down.reshape(groups, part, cols)
    down_w = lax.all_to_all(down_w, "group", 0, 0, tiled=True).transpose(1, 0, 2)
    down_w = lax.all_gather(down_w.reshape(part, width), "expert", axis=0, tiled=False)

    inputs = layer_in[0].astype(F32)
    normed_b = rms_norm(inputs, attn_gain).astype(BF16)
    expert_ids = jnp.arange(experts, dtype=jnp.int32)
    marks = jnp.any(routing[0][:, :, None] == expert_ids[None, None, :], axis=1).astype(F32)
    marks = jnp.concatenate([marks.T, segment_ids[0].astype(F32)[None]], axis=0)
    marks = lax.all_gather(marks, "group", axis=1, tiled=True)
    chosen, seg_all = marks[:experts].T > 0.5, marks[experts]
    normed_all = gather_rows(normed_b, groups, 1)
    grad_all = gather(out_grad[0])
    wq, wk, wv = own_cols(w_query, 1), own_cols(w_key, 1), own_cols(w_value, 1)
    query_raw, key_raw = mm(normed_all, wq), mm(normed_all, wk)
    values_b = mm(normed_all, wv).astype(BF16).reshape(length, heads, head_dim)

    def row_sums(first, second, collective_id):
        sums = jnp.stack([jnp.sum(first, axis=1), jnp.sum(second, axis=1)])
        sums = small_sum(sums.reshape(-1, 128), ("group",), False, collective_id)
        return sums.reshape(2, length, 1) / width

    scales = lax.rsqrt(row_sums(query_raw * query_raw, key_raw * key_raw, 2) + EPSILON)
    query_scale, key_scale = scales[0], scales[1]
    query_gain_c, key_gain_c = own_cols(query_gain, 0), own_cols(key_gain, 0)
    cosine, sine = angles(length, head_dim)

    def turned(raw, scale, gain):
        return rotate((raw * scale * gain).reshape(length, heads, head_dim), cosine, sine)

    queries_b = turned(query_raw, query_scale, query_gain_c).astype(BF16)
    keys_b = turned(key_raw, key_scale, key_gain_c).astype(BF16)
    place = jnp.arange(length, dtype=jnp.int32)
    allowed = (seg_all[:, None] == seg_all[None, :]) & (place[None, :] <= place[:, None])
    scores = jnp.where(allowed[None], ein("qhd,khd->hqk", queries_b, keys_b) * score_scale, MASKED)
    top_score = jnp.max(scores, axis=-1, keepdims=True)
    log_total = top_score + jnp.log(jnp.sum(jnp.exp(scores - top_score), axis=-1, keepdims=True))
    probs = jnp.exp(scores - log_total)
    probs_b = probs.astype(BF16)
    mixed_c = ein("hqk,khd->qhd", probs_b, values_b).reshape(length, cols).astype(BF16)
    (mixed_b,) = swap([mixed_c], groups, False, 3)
    resid = inputs + mm(mixed_b, w_out)
    normed_mlp_b = rms_norm(resid, mlp_gain).astype(BF16)
    mlp_all = gather_rows(normed_mlp_b, groups, 4)

    router_all = jax.nn.softmax(mm(mlp_all, w_router), axis=-1)
    picked = jnp.where(chosen, router_all, 0.0).reshape(length, sources, local_experts)
    picked = lax.dynamic_index_in_dim(picked, me // parts, 2, keepdims=True)
    gate_pre = ein("td,edf->tef", mlp_all, gate_w)
    up_pre = ein("td,edf->tef", mlp_all, up_w)
    sigma = jax.nn.sigmoid(gate_pre)
    hidden = gate_pre * sigma * up_pre
    hidden_b = (hidden * picked).astype(BF16)
    out_part = ein("tef,efd->td", hidden_b, down_w).astype(BF16)
    mixture = lax.psum_scatter(out_part, "group", scatter_dimension=0, tiled=True)
    hidden_grad = ein("td,efd->tef", grad_all, down_w)
    picked_grad = jnp.sum(hidden * hidden_grad, axis=2)
    hidden_grad = hidden_grad * picked
    gate_grad_b = (hidden_grad * up_pre * sigma * (1.0 + gate_pre * (1.0 - sigma))).astype(BF16)
    up_grad_b = (hidden_grad * gate_pre * sigma).astype(BF16)
    slot_part = ein("tef,edf->td", gate_grad_b, gate_w) + ein("tef,edf->td", up_grad_b, up_w)
    slot_sum = reduce_rows(slot_part.astype(BF16), groups, 5)
    own_expert = jnp.arange(local_experts, dtype=jnp.int32) == me // parts
    full_part = jnp.where(own_expert[None, None, :], picked_grad[:, :, None], 0.0)
    full_part = jnp.where(chosen, full_part.reshape(length, experts), 0.0)
    router_full_grad = lax.psum_scatter(full_part, "group", scatter_dimension=0, tiled=True)
    gate_w_part = ein("td,tef->edf", mlp_all, gate_grad_b).astype(BF16)
    up_w_part = ein("td,tef->edf", mlp_all, up_grad_b).astype(BF16)
    down_w_part = ein("tef,td->efd", hidden_b, grad_all).astype(BF16)

    def slices_out(w):
        w = lax.psum_scatter(w, "expert", scatter_dimension=0, tiled=False)
        w = lax.all_to_all(w.reshape(groups, cols, part), "group", 0, 0, tiled=True)
        w = w.reshape(local_experts, parts, cols, part).transpose(0, 2, 1, 3)
        return w.reshape(local_experts, cols, hidden_size).astype(F32)

    gate_sum = slices_out(gate_w_part)
    up_sum = slices_out(up_w_part)
    down_sum = lax.psum_scatter(down_w_part, "expert", scatter_dimension=0, tiled=False)
    down_sum = down_sum.reshape(part, groups, cols).transpose(1, 0, 2)
    down_sum = lax.all_to_all(down_sum, "group", 0, 0, tiled=True)
    down_sum = down_sum.reshape(local_experts, hidden_size, cols).astype(F32)

    result = (resid + mixture.astype(F32)).astype(BF16)
    grad_out = out_grad[0].astype(F32)
    router = jax.nn.softmax(mm(normed_mlp_b, w_router), axis=-1)
    logits_grad_b = (
        router * (router_full_grad - jnp.sum(router * router_full_grad, axis=-1, keepdims=True))
    ).astype(BF16)
    router_w_grad = mm_tn(normed_mlp_b, logits_grad_b)
    mlp_in_grad = slot_sum + mm_nt(logits_grad_b, w_router)
    _, mlp_back = jax.vjp(rms_norm, resid, mlp_gain)
    resid_part, mlp_gain_grad = mlp_back(mlp_in_grad)
    resid_grad = grad_out + resid_part
    attn_grad_b = resid_grad.astype(BF16)
    attn_grad_all = gather(attn_grad_b)
    out_w_part = mm_tn(mixed_c, attn_grad_all).astype(BF16)
    out_w_grad = lax.psum_scatter(out_w_part, "expert", scatter_dimension=0, tiled=True)
    mixed_grad_b = mm_nt(attn_grad_b, w_out).astype(BF16)
    (mixed_grad_c,) = swap([mixed_grad_b], groups, True, 6)
    mixed_grad_c = mixed_grad_c.reshape(length, heads, head_dim)

    prob_grad = ein("qhd,khd->hqk", mixed_grad_c, values_b)
    delta = jnp.sum(probs * prob_grad, axis=-1, keepdims=True)
    score_grad_b = (probs * (prob_grad - delta) * score_scale).astype(BF16)
    query_grad = ein("hqk,khd->qhd", score_grad_b, keys_b)
    key_grad = ein("hqk,qhd->khd", score_grad_b, queries_b)
    value_grad_b = ein("hqk,qhd->khd", probs_b, mixed_grad_c).astype(BF16).reshape(length, cols)

    def unturned(grad):
        return rotate(grad, cosine, -sine).reshape(length, cols)

    query_turn, key_turn = unturned(query_grad), unturned(key_grad)
    query_mix, key_mix = query_turn * query_gain_c, key_turn * key_gain_c
    dots = row_sums(query_mix * query_raw, key_mix * key_raw, 7)
    query_raw_b = (
        query_scale * query_mix - query_raw * query_scale**3 * dots[0]
    ).astype(BF16)
    key_raw_b = (key_scale * key_mix - key_raw * key_scale**3 * dots[1]).astype(BF16)
    query_gain_part = jnp.sum(query_turn * query_raw * query_scale, axis=0)
    key_gain_part = jnp.sum(key_turn * key_raw * key_scale, axis=0)
    raw_grads = jnp.concatenate([query_raw_b, key_raw_b, value_grad_b], axis=1)
    qkv_part = mm_tn(normed_all, raw_grads).astype(BF16).reshape(groups, sources, -1, 3 * cols)
    qkv_part = lax.psum_scatter(qkv_part, "expert", scatter_dimension=1, tiled=False)
    qkv_part = lax.all_to_all(qkv_part, "group", 0, 0, tiled=True)
    qkv_part = qkv_part.transpose(1, 0, 2).reshape(-1, groups, 3, cols).astype(F32)
    query_own, key_own, value_own = swap([query_raw_b, key_raw_b, value_grad_b], groups, False, 8)
    normed_grad = mm_nt(query_own, w_query) + mm_nt(key_own, w_key) + mm_nt(value_own, w_value)
    _, attn_back = jax.vjp(rms_norm, inputs, attn_gain)
    input_part, attn_gain_grad = attn_back(normed_grad)
    input_grad = resid_grad + input_part
    wide = [
        lax.dynamic_update_slice_in_dim(jnp.zeros((width,), F32), part, me * cols, 0)
        for part in (query_gain_part, key_gain_part)
    ]
    small = jnp.concatenate([router_w_grad.T, jnp.stack([mlp_gain_grad, attn_gain_grad] + wide)])
    devices = groups * sources
    small = small.reshape(-1, devices, width // devices).transpose(1, 0, 2).reshape(devices, -1)
    used = small.shape[1]
    small = jnp.pad(small, ((0, 0), (0, -used % 1024))).reshape(devices, -1, 128)
    small = small_sum(small, ("group", "expert"), True, 9).reshape(-1)[:used]
    small = small.reshape(-1, width // devices)
    return (
        result[None],
        input_grad[None],
        small[experts + 1],
        qkv_part[:, :, 0].reshape(-1, width),
        qkv_part[:, :, 1].reshape(-1, width),
        qkv_part[:, :, 2].reshape(-1, width),
        small[experts + 2],
        small[experts + 3],
        out_w_grad.astype(F32),
        small[experts],
        small[:experts].T,
        gate_sum,
        up_sum,
        down_sum,
    )


def solution(mesh):
    token = P("expert", "group", None)
    every = P(("group", "expert"))
    return jax.shard_map(
        shards,
        mesh=mesh,
        in_specs=(token, P("expert", "group"), token, token)
        + (P(),) * 9
        + (token, token, P("expert", None, "group")),
        out_specs=(token, token)
        + (every,) * 9
        + (token, token, P("expert", None, "group")),
        check_vma=False,
    )
```

```python
import functools
import math

import jax
import jax.numpy as jnp
from jax import lax
from jax.experimental import pallas as pl
from jax.experimental.pallas import tpu as pltpu
from jax.sharding import PartitionSpec as P

HEADS = 16
EPSILON = 1e-05
MASKED = -1000000000.0
BF16 = jnp.bfloat16
F32 = jnp.float32
MESH = pl.DeviceIdType.MESH
DMA = pltpu.SemaphoreType.DMA
VMEM_SPEC = pl.BlockSpec(memory_space=pltpu.VMEM)


def remote(src, dst, send_sem, recv_sem, where):
    return pltpu.make_async_remote_copy(
        src, dst, send_sem, recv_sem, device_id=where, device_id_type=MESH
    )


def comm_params(collective_id):
    return pltpu.CompilerParams(collective_id=collective_id, has_side_effects=True)


def greet(peers):
    barrier = pltpu.get_barrier_semaphore()
    total = 0
    for here, where in peers:

        @pl.when(here)
        def _(where=where):
            pl.semaphore_signal(barrier, inc=1, device_id=where, device_id_type=MESH)

        total = total + jnp.where(here, 1, 0)
    pl.semaphore_wait(barrier, total)


def greet_all(count, device):
    barrier = pltpu.get_barrier_semaphore()

    def body(k, carry):
        pl.semaphore_signal(barrier, inc=1, device_id=device(k), device_id_type=MESH)
        return carry

    lax.fori_loop(1, count, body, 0)
    pl.semaphore_wait(barrier, count - 1)


def gather_kernel(nz, ny, pieces, *refs):
    if len(refs) == 5:
        block, out, own_sem, send_sem, recv_sem = refs
        note = None
    else:
        block, note, out, note_out, own_sem, send_sem, recv_sem, note_send, note_recv = refs
    me = lax.axis_index("group")
    z, y = me // ny, me % ny
    rows = block.shape[0] // pieces

    def at(z_to, y_to):
        return {"group": z_to * ny + y_to}

    def note_copy(k):
        to = {"group": lax.rem(me + k, nz * ny)}
        return remote(note, note_out.at[me], note_send.at[k], note_recv.at[k], to)

    if note is None:
        greet(
            [
                (z > 0, at(z - 1, y)),
                (z < nz - 1, at(z + 1, y)),
                (y > 0, at(z, y - 1)),
                (y < ny - 1, at(z, y + 1)),
            ]
        )
    else:
        greet_all(nz * ny, lambda k: {"group": lax.rem(me + k, nz * ny)})
        for k in range(1, nz * ny):
            note_copy(k).start()
        note_out[me] = note[...]
    own = pltpu.make_async_copy(block, out.at[me], own_sem)
    own.start()

    def part(ref, c):
        return ref.at[pl.ds(c * rows, rows)]

    def copy(slot, source, c, where, first):
        return remote(
            part(block, c) if first else part(out.at[source], c),
            part(out.at[source], c),
            send_sem.at[slot, source, c],
            recv_sem.at[source, c],
            where,
        )

    def outgoing(source, go):
        sz, sy = source // ny, source % ny
        column = go & (sy == y)
        return [
            (column & (sz <= z) & (z < nz - 1), 0, at(z + 1, y)),
            (column & (sz >= z) & (z > 0), 1, at(z - 1, y)),
            (go & (sy <= y) & (y < ny - 1), 2, at(z, y + 1)),
            (go & (sy >= y) & (y > 0), 3, at(z, y - 1)),
        ]

    def act(source, first, go, start):
        for c in range(pieces):
            if start and not first:

                @pl.when(go)
                def _():
                    copy(0, source, c, at(z, y), False).wait_recv()

            for cond, slot, where in outgoing(source, go):

                @pl.when(cond)
                def _(slot=slot, where=where):
                    one = copy(slot, source, c, where, first)
                    if start:
                        one.start()
                    else:
                        one.wait_send()

    order = []
    for dz in range(nz):
        for sz in [z] if dz == 0 else [z - dz, z + dz]:
            for dy in range(ny):
                for sy in [y] if dy == 0 else [y - dy, y + dy]:
                    inside = (sz >= 0) & (sz < nz) & (sy >= 0) & (sy < ny)
                    source = jnp.clip(sz, 0, nz - 1) * ny + jnp.clip(sy, 0, ny - 1)
                    order.append((dz + dy, dz, source, inside))
    order = sorted(order, key=lambda t: (t[0], -t[1]))
    for start in (True, False):
        for distance, _, source, inside in order:
            act(source, distance == 0, inside, start)
        if start:
            own.wait()
    if note is not None:
        for k in range(1, nz * ny):
            note_copy(k).wait()


def gather_rows(block, groups, collective_id, pieces=2, note=None):
    nz = min(4, groups)
    notes = [] if note is None else [note]
    outs = pl.pallas_call(
        functools.partial(gather_kernel, nz, groups // nz, pieces),
        name="gather_rows",
        out_shape=[jax.ShapeDtypeStruct((groups,) + a.shape, a.dtype) for a in [block] + notes],
        in_specs=[VMEM_SPEC] * (1 + len(notes)),
        out_specs=[pl.BlockSpec(memory_space=pl.ANY)] + [VMEM_SPEC] * len(notes),
        scratch_shapes=[DMA, DMA((4, groups, pieces)), DMA((groups, pieces))]
        + [DMA((groups,))] * 2 * len(notes),
        compiler_params=comm_params(collective_id),
        cost_estimate=pl.CostEstimate(flops=0, bytes_accessed=200_000_000, transcendentals=0),
    )(block, *notes)
    rows = outs[0].reshape(groups * block.shape[0], block.shape[1])
    return rows if note is None else (rows, outs[1])


def reduce_kernel(nz, ny, pieces, parts, out, ybuf, zbuf, ysend, yrecv, zsend, zrecv):
    me = lax.axis_index("group")
    z, y = me // ny, me % ny
    rows = parts.shape[1] // pieces

    def at(z_to, y_to):
        return {"group": z_to * ny + y_to}

    greet([(z > 0, at(z - 1, y)), (z < nz - 1, at(z + 1, y)), (z >= 0, at(z, 1 - y))])

    def part(ref, c):
        return ref.at[pl.ds(c * rows, rows)]

    def y_copy(dest, c):
        src, dst = part(parts.at[dest * ny + 1 - y], c), part(ybuf.at[dest], c)
        return remote(src, dst, ysend.at[dest, c], yrecv.at[dest, c], at(z, 1 - y))

    def z_copy(side, dest, c):
        src, dst = part(ybuf.at[dest], c), part(zbuf.at[side, dest], c)
        where = at(z - 1, y) if side else at(z + 1, y)
        return remote(src, dst, zsend.at[dest, c], zrecv.at[side, dest, c], where)

    order = []
    for d in range(nz - 1, 0, -1):
        order += [(z + d, z + d < nz, 0), (z - d, z - d >= 0, 1)]
    order = [(jnp.clip(dest, 0, nz - 1), inside, side) for dest, inside, side in order]
    for dest, inside, side in order:

        @pl.when(inside)
        def _():
            for c in range(pieces):
                y_copy(dest, c).start()

    for c in range(pieces):
        y_copy(z, c).start()
    for dest, inside, side in order:
        further = (z < nz - 1) if side else (z > 0)
        for c in range(pieces):
            span = pl.ds(c * rows, rows)

            @pl.when(inside)
            def _():
                y_copy(dest, c).wait_recv()
                pair = parts[dest * ny + y, span, :].astype(F32) + ybuf[dest, span, :].astype(F32)

                @pl.when(further)
                def _():
                    z_copy(side, dest, c).wait_recv()
                    ybuf[dest, span, :] = (pair + zbuf[side, dest, span, :].astype(F32)).astype(BF16)

                @pl.when(jnp.logical_not(further))
                def _():
                    ybuf[dest, span, :] = pair.astype(BF16)

                z_copy(side, dest, c).start()

    for c in range(pieces):
        span = pl.ds(c * rows, rows)
        y_copy(z, c).wait_recv()
        out[span, :] = parts[me, span, :].astype(F32) + ybuf[z, span, :].astype(F32)

        @pl.when(z > 0)
        def _():
            z_copy(0, z, c).wait_recv()
            out[span, :] += zbuf[0, z, span, :].astype(F32)

        @pl.when(z < nz - 1)
        def _():
            z_copy(1, z, c).wait_recv()
            out[span, :] += zbuf[1, z, span, :].astype(F32)

    for dest, inside, side in order:

        @pl.when(inside)
        def _():
            for c in range(pieces):
                y_copy(dest, c).wait_send()
                z_copy(side, dest, c).wait_send()

    for c in range(pieces):
        y_copy(z, c).wait_send()


def reduce_rows(parts, groups, collective_id, pieces=2):
    nz = min(4, groups)
    ny = groups // nz
    if ny != 2:
        return lax.psum_scatter(parts, "group", scatter_dimension=0, tiled=True).astype(F32)
    rows, width = parts.shape[0] // groups, parts.shape[1]
    return pl.pallas_call(
        functools.partial(reduce_kernel, nz, ny, pieces),
        name="reduce_rows",
        out_shape=jax.ShapeDtypeStruct((rows, width), F32),
        in_specs=[VMEM_SPEC],
        out_specs=VMEM_SPEC,
        scratch_shapes=[
            pltpu.VMEM((nz, rows, width), BF16),
            pltpu.VMEM((2, nz, rows, width), BF16),
            DMA((nz, pieces)),
            DMA((nz, pieces)),
            DMA((nz, pieces)),
            DMA((2, nz, pieces)),
        ],
        compiler_params=comm_params(collective_id),
        cost_estimate=pl.CostEstimate(flops=0, bytes_accessed=100_000_000, transcendentals=0),
    )(parts.reshape(groups, rows, width))


def swap_kernel(groups, to_rows, *refs):
    count = (len(refs) - 2) // 2
    ins, outs, (send_sem, recv_sem) = refs[:count], refs[count : 2 * count], refs[2 * count :]
    me = lax.axis_index("group")
    columns = ins[0].shape[-1] // (groups if to_rows else 1)
    wide = lambda ref, i: ref.at[:, pl.ds(pl.multiple_of(i * columns, columns), columns)]
    thin = lambda ref, i: ref.at[i]
    source, target = (wide, thin) if to_rows else (thin, wide)

    def peer(k):
        return lax.rem(me + k, groups)

    greet_all(groups, lambda k: {"group": peer(k)})

    def copy(n, k):
        to = peer(k)
        return remote(
            source(ins[n], to), target(outs[n], me), send_sem.at[n, k], recv_sem.at[n, k], {"group": to}
        )

    for k in range(1, groups):
        for n in range(count):
            copy(n, k).start()
    for n in range(count):
        if to_rows:
            outs[n][me] = ins[n][:, pl.ds(pl.multiple_of(me * columns, columns), columns)]
        else:
            outs[n][:, pl.ds(pl.multiple_of(me * columns, columns), columns)] = ins[n][me]
    for k in range(1, groups):
        for n in range(count):
            copy(n, k).wait()


def swap(arrays, groups, to_rows, collective_id):
    shape, count = arrays[0].shape, len(arrays)
    if to_rows:
        rows, columns = shape[0], shape[1] // groups
        out = (groups, rows, columns)
    else:
        rows, columns = shape[0] // groups, shape[1]
        arrays = [a.reshape(groups, rows, columns) for a in arrays]
        out = (rows, groups * columns)
    outs = pl.pallas_call(
        functools.partial(swap_kernel, groups, to_rows),
        name="swap",
        out_shape=[jax.ShapeDtypeStruct(out, a.dtype) for a in arrays],
        in_specs=[VMEM_SPEC] * count,
        out_specs=[VMEM_SPEC] * count,
        scratch_shapes=[DMA((count, groups)), DMA((count, groups))],
        compiler_params=comm_params(collective_id),
        cost_estimate=pl.CostEstimate(flops=0, bytes_accessed=30_000_000, transcendentals=0),
    )(*arrays)
    return [o.reshape(groups * rows, columns) if to_rows else o for o in outs]


def small_sum_kernel(axes, scatter, values, out, landed, send_sem, recv_sem):
    sizes = [lax.axis_size(a) for a in axes]
    count = math.prod(sizes)
    me = 0
    for a, n in zip(axes, sizes):
        me = me * n + lax.axis_index(a)

    def peer(k):
        return lax.rem(me + k, count)

    def device(k):
        to = peer(k)
        if len(axes) == 1:
            return {axes[0]: to}
        return {axes[0]: to // sizes[1], axes[1]: lax.rem(to, sizes[1])}

    greet_all(count, device)

    def copy(k):
        src = values.at[peer(k)] if scatter else values
        return remote(src, landed.at[k], send_sem.at[k], recv_sem.at[k], device(k))

    def start(k, carry):
        copy(k).start()
        return carry

    def wait(k, carry):
        copy(k).wait()
        return carry

    lax.fori_loop(1, count, start, 0)
    landed[0] = values[me] if scatter else values[...]
    lax.fori_loop(1, count, wait, 0)
    out[...] = jnp.sum(landed[...], axis=0)


def small_sum(values, axes, scatter, collective_id):
    count = math.prod(lax.axis_size(a) for a in axes)
    shape = values.shape[-2:]
    return pl.pallas_call(
        functools.partial(small_sum_kernel, axes, scatter),
        name="small_sum",
        out_shape=jax.ShapeDtypeStruct(shape, F32),
        in_specs=[VMEM_SPEC],
        out_specs=VMEM_SPEC,
        scratch_shapes=[pltpu.VMEM((count,) + shape, F32), DMA((count,)), DMA((count,))],
        compiler_params=comm_params(collective_id),
        cost_estimate=pl.CostEstimate(flops=0, bytes_accessed=10_000_000, transcendentals=0),
    )(values)


def rms_norm(values_in, gain_vec):
    return (
        values_in
        * lax.rsqrt(jnp.mean(values_in * values_in, axis=-1, keepdims=True) + EPSILON)
        * gain_vec
    )


def angles(row_count, head_dim):
    places = jnp.arange(row_count, dtype=jnp.int32).astype(F32)
    frequency = jnp.exp(-math.log(10000.0) * 2.0 * jnp.arange(head_dim // 2, dtype=F32) / head_dim)
    turn_angle = places[:, None] * frequency[None, :]
    return (jnp.cos(turn_angle)[:, None, :], jnp.sin(turn_angle)[:, None, :])


def rotate(values_in, cosine, sine):
    half_dim = values_in.shape[-1] // 2
    first_half = values_in[..., :half_dim]
    second = values_in[..., half_dim:]
    return jnp.concatenate(
        [first_half * cosine - second * sine, second * cosine + first_half * sine], axis=-1
    )


def mm(left, right):
    return jnp.dot(left, right, preferred_element_type=F32)


def mm_tn(left, right):
    return lax.dot_general(left, right, (((0,), (0,)), ((), ())), preferred_element_type=F32)


def mm_nt(left, right):
    return lax.dot_general(left, right, (((1,), (1,)), ((), ())), preferred_element_type=F32)


def ein(spec, *ops):
    return jnp.einsum(spec, *ops, preferred_element_type=F32)


def shards(
    layer_in,
    segment_ids,
    routing,
    out_grad,
    attn_gain,
    w_query,
    w_key,
    w_value,
    query_gain,
    key_gain,
    w_out,
    mlp_gain,
    w_router,
    w_gate,
    w_up,
    w_down,
):
    groups = lax.axis_size("group")
    sources = lax.axis_size("expert")
    me = lax.axis_index("group")
    rows = layer_in.shape[1]
    width = layer_in.shape[2]
    length = rows * groups
    head_dim = width // HEADS
    heads = HEADS // groups
    cols = width // groups
    local_experts = w_gate.shape[0]
    experts = local_experts * sources
    hidden_size = w_gate.shape[2]
    parts = groups // local_experts
    part = hidden_size // parts
    score_scale = 1.0 / math.sqrt(head_dim)

    def own_cols(matrix, axis):
        return lax.dynamic_slice_in_dim(matrix, me * cols, cols, axis)

    def slices(w):
        w = w.reshape(local_experts, w.shape[1], parts, part).transpose(0, 2, 1, 3)
        return w.reshape(groups, w.shape[2], part)

    def exchange(w):
        return lax.all_to_all(w, "group", 0, 0, tiled=True)

    def row_of_devices(w):
        return lax.all_gather(w, "expert", axis=0, tiled=False)

    together = lax.optimization_barrier
    gate_own = exchange(slices(w_gate))

    inputs = layer_in[0].astype(F32)
    normed_b = rms_norm(inputs, attn_gain).astype(BF16)
    expert_ids = jnp.arange(experts, dtype=jnp.int32)
    marks = jnp.any(routing[0][:, :, None] == expert_ids[None, None, :], axis=1).astype(F32)
    marks = jnp.concatenate([marks.T, segment_ids[0].astype(F32)[None]], axis=0)
    normed_all, marks = gather_rows(normed_b, groups, 1, note=marks)
    marks = marks.transpose(1, 0, 2).reshape(experts + 1, length)
    chosen, seg_all = marks[:experts].T > 0.5, marks[experts]
    gate_own, up_in, normed_late = together((gate_own, slices(w_up), normed_all))
    gate_w = row_of_devices(gate_own.reshape(width, part))
    up_own = exchange(up_in)
    wq, wk, wv = own_cols(w_query, 1), own_cols(w_key, 1), own_cols(w_value, 1)
    query_raw, key_raw = mm(normed_all, wq), mm(normed_all, wk)
    values_b = mm(normed_all, wv).astype(BF16).reshape(length, heads, head_dim)

    def row_sums(first, second, collective_id):
        sums = jnp.stack([jnp.sum(first, axis=1), jnp.sum(second, axis=1)])
        sums = small_sum(sums.reshape(-1, 128), ("group",), False, collective_id)
        return sums.reshape(2, length, 1) / width

    scales = lax.rsqrt(row_sums(query_raw * query_raw, key_raw * key_raw, 2) + EPSILON)
    query_scale, key_scale = scales[0], scales[1]
    query_gain_c, key_gain_c = own_cols(query_gain, 0), own_cols(key_gain, 0)
    cosine, sine = angles(length, head_dim)

    def turned(raw, scale, gain):
        return rotate((raw * scale * gain).reshape(length, heads, head_dim), cosine, sine)

    queries_b = turned(query_raw, query_scale, query_gain_c).astype(BF16)
    keys_b = turned(key_raw, key_scale, key_gain_c).astype(BF16)
    place = jnp.arange(length, dtype=jnp.int32)
    allowed = (seg_all[:, None] == seg_all[None, :]) & (place[None, :] <= place[:, None])
    scores = jnp.where(allowed[None], ein("qhd,khd->hqk", queries_b, keys_b) * score_scale, MASKED)
    top_score = jnp.max(scores, axis=-1, keepdims=True)
    log_total = top_score + jnp.log(jnp.sum(jnp.exp(scores - top_score), axis=-1, keepdims=True))
    probs = jnp.exp(scores - log_total)
    probs_b = probs.astype(BF16)
    mixed_c = ein("hqk,khd->qhd", probs_b, values_b).reshape(length, cols).astype(BF16)
    up_own, down_in, mixed_c = together((up_own, w_down.reshape(groups, part, cols), mixed_c))
    up_w = row_of_devices(up_own.reshape(width, part))
    down_own = exchange(down_in)
    (mixed_b,) = swap([mixed_c], groups, False, 3)
    resid = inputs + mm(mixed_b, w_out)
    normed_mlp_b = rms_norm(resid, mlp_gain).astype(BF16)
    mlp_all = gather_rows(normed_mlp_b, groups, 4)
    down_own, grad_in, mlp_late = together((down_own, out_grad[0], mlp_all))
    down_w = row_of_devices(down_own.transpose(1, 0, 2).reshape(part, width))
    grad_all = exchange(jnp.broadcast_to(grad_in, (groups, rows, width))).reshape(length, width)

    router_all = jax.nn.softmax(mm(mlp_all, w_router), axis=-1)
    picked = jnp.where(chosen, router_all, 0.0).reshape(length, sources, local_experts)
    picked = lax.dynamic_index_in_dim(picked, me // parts, 2, keepdims=True)
    gate_pre = ein("td,edf->tef", mlp_all, gate_w)
    up_pre = ein("td,edf->tef", mlp_all, up_w)
    sigma = jax.nn.sigmoid(gate_pre)
    hidden = gate_pre * sigma * up_pre
    hidden_b = (hidden * picked).astype(BF16)
    out_part = ein("tef,efd->td", hidden_b, down_w).astype(BF16)
    out_part, grad_all, mixed_in = together((out_part, grad_all, mixed_b))
    mixture = lax.psum_scatter(out_part, "group", scatter_dimension=0, tiled=True)
    mixed_all = exchange(jnp.broadcast_to(mixed_in, (groups, rows, width))).reshape(length, width)
    hidden_grad = ein("td,efd->tef", grad_all, down_w)
    picked_grad = jnp.sum(hidden * hidden_grad, axis=2)
    hidden_grad = hidden_grad * picked
    gate_grad_b = (hidden_grad * up_pre * sigma * (1.0 + gate_pre * (1.0 - sigma))).astype(BF16)
    up_grad_b = (hidden_grad * gate_pre * sigma).astype(BF16)
    own_expert = jnp.arange(local_experts, dtype=jnp.int32) == me // parts
    full_part = jnp.where(own_expert[None, None, :], picked_grad[:, :, None], 0.0)
    full_part = jnp.where(chosen, full_part.reshape(length, experts), 0.0)
    full_part = full_part.T.reshape(experts, groups, rows).transpose(1, 0, 2)
    router_full_grad = small_sum(full_part, ("group",), True, 10).T
    gate_w_part = ein("td,tef->edf", mlp_late, gate_grad_b).astype(BF16)
    up_w_part = ein("td,tef->edf", mlp_late, up_grad_b).astype(BF16)
    down_w_part = ein("tef,td->efd", hidden_b, grad_all).astype(BF16)
    up_w_part, down_w_part, gate_grad_b, up_grad_b = together(
        (up_w_part, down_w_part, gate_grad_b, up_grad_b)
    )

    def over_row(w):
        return lax.psum_scatter(w, "expert", scatter_dimension=0, tiled=False)

    gate_sum, up_sum, down_sum = over_row(gate_w_part), over_row(up_w_part), over_row(down_w_part)
    slot_part = ein("tef,edf->td", gate_grad_b, gate_w) + ein("tef,edf->td", up_grad_b, up_w)
    slot_part, mixture, mixed_all = together((slot_part.astype(BF16), mixture, mixed_all))
    slot_sum = reduce_rows(slot_part, groups, 5)

    def slices_out(w):
        w = w.reshape(local_experts, parts, cols, part).transpose(0, 2, 1, 3)
        return w.reshape(local_experts, cols, hidden_size).astype(F32)

    result = (resid + mixture.astype(F32)).astype(BF16)
    grad_out = out_grad[0].astype(F32)
    router = jax.nn.softmax(mm(normed_mlp_b, w_router), axis=-1)
    logits_grad_b = (
        router * (router_full_grad - jnp.sum(router * router_full_grad, axis=-1, keepdims=True))
    ).astype(BF16)
    router_w_grad = mm_tn(normed_mlp_b, logits_grad_b)
    mlp_in_grad = slot_sum + mm_nt(logits_grad_b, w_router)
    _, mlp_back = jax.vjp(rms_norm, resid, mlp_gain)
    resid_part, mlp_gain_grad = mlp_back(mlp_in_grad)
    resid_grad = grad_out + resid_part
    attn_grad_b = resid_grad.astype(BF16)
    mixed_grad_b = mm_nt(attn_grad_b, w_out).astype(BF16)
    gate_sum, mixed_grad_b, attn_grad_b = together((gate_sum, mixed_grad_b, attn_grad_b))
    gate_sum = exchange(gate_sum.reshape(groups, cols, part))
    mixed_grad_c, attn_grad_c = swap([mixed_grad_b, attn_grad_b], groups, True, 6)
    up_sum, mixed_grad_c, attn_grad_c = together((up_sum, mixed_grad_c, attn_grad_c))
    out_w_part = mm_tn(mixed_all, attn_grad_c).astype(BF16)
    mixed_grad_c = mixed_grad_c.reshape(length, heads, head_dim)

    prob_grad = ein("qhd,khd->hqk", mixed_grad_c, values_b)
    delta = jnp.sum(probs * prob_grad, axis=-1, keepdims=True)
    score_grad_b = (probs * (prob_grad - delta) * score_scale).astype(BF16)
    query_grad = ein("hqk,khd->qhd", score_grad_b, keys_b)
    key_grad = ein("hqk,qhd->khd", score_grad_b, queries_b)
    value_grad_b = ein("hqk,qhd->khd", probs_b, mixed_grad_c).astype(BF16).reshape(length, cols)

    def unturned(grad):
        return rotate(grad, cosine, -sine).reshape(length, cols)

    query_turn, key_turn = unturned(query_grad), unturned(key_grad)
    query_mix, key_mix = query_turn * query_gain_c, key_turn * key_gain_c
    query_dots, key_dots, gate_sum, up_sum = together(
        (query_mix * query_raw, key_mix * key_raw, gate_sum, up_sum)
    )
    up_sum = exchange(up_sum.reshape(groups, cols, part))
    dots = row_sums(query_dots, key_dots, 7)
    query_raw_b = (
        query_scale * query_mix - query_raw * query_scale**3 * dots[0]
    ).astype(BF16)
    key_raw_b = (key_scale * key_mix - key_raw * key_scale**3 * dots[1]).astype(BF16)
    query_gain_part = jnp.sum(query_turn * query_raw * query_scale, axis=0)
    key_gain_part = jnp.sum(key_turn * key_raw * key_scale, axis=0)
    raw_grads = jnp.concatenate([query_raw_b, key_raw_b, value_grad_b], axis=1)
    qkv_part = jnp.concatenate([mm_tn(normed_late, raw_grads).astype(BF16), out_w_part], axis=1)
    qkv_part = qkv_part.reshape(groups, sources, -1, 4 * cols).transpose(1, 0, 2, 3)
    qkv_part = qkv_part.reshape(sources, -1, 4 * cols)
    qkv_part = lax.psum_scatter(qkv_part, "expert", scatter_dimension=0, tiled=False)
    qkv_part = lax.all_to_all(qkv_part.reshape(groups, -1, 4 * cols), "group", 0, 0, tiled=True)
    qkv_part = qkv_part.transpose(1, 0, 2).reshape(-1, groups, 4, cols).astype(F32)
    query_own, key_own, value_own = swap([query_raw_b, key_raw_b, value_grad_b], groups, False, 8)
    query_own, key_own, value_own, up_sum, down_sum = together(
        (query_own, key_own, value_own, up_sum, down_sum)
    )
    down_sum = exchange(down_sum.reshape(part, groups, cols).transpose(1, 0, 2))
    normed_grad = mm_nt(query_own, w_query) + mm_nt(key_own, w_key) + mm_nt(value_own, w_value)
    _, attn_back = jax.vjp(rms_norm, inputs, attn_gain)
    input_part, attn_gain_grad = attn_back(normed_grad)
    input_grad = resid_grad + input_part
    wide = [
        lax.dynamic_update_slice_in_dim(jnp.zeros((width,), F32), part, me * cols, 0)
        for part in (query_gain_part, key_gain_part)
    ]
    small = jnp.concatenate([router_w_grad.T, jnp.stack([mlp_gain_grad, attn_gain_grad] + wide)])
    devices = groups * sources
    small = small.reshape(-1, devices, width // devices).transpose(1, 0, 2).reshape(devices, -1)
    used = small.shape[1]
    small = jnp.pad(small, ((0, 0), (0, -used % 1024))).reshape(devices, -1, 128)
    small = small_sum(small, ("group", "expert"), True, 9).reshape(-1)[:used]
    small = small.reshape(-1, width // devices)
    return (
        result[None],
        input_grad[None],
        small[experts + 1],
        qkv_part[:, :, 0].reshape(-1, width),
        qkv_part[:, :, 1].reshape(-1, width),
        qkv_part[:, :, 2].reshape(-1, width),
        small[experts + 2],
        small[experts + 3],
        qkv_part[:, :, 3].reshape(-1, width),
        small[experts],
        small[:experts].T,
        slices_out(gate_sum),
        slices_out(up_sum),
        down_sum.reshape(local_experts, hidden_size, cols).astype(F32),
    )


def solution(mesh):
    token = P("expert", "group", None)
    every = P(("group", "expert"))
    return jax.shard_map(
        shards,
        mesh=mesh,
        in_specs=(token, P("expert", "group"), token, token)
        + (P(),) * 9
        + (token, token, P("expert", None, "group")),
        out_specs=(token, token)
        + (every,) * 9
        + (token, token, P("expert", None, "group")),
        check_vma=False,
    )
```

```python
import functools
import math

import jax
import jax.numpy as jnp
from jax import lax
from jax.experimental import pallas as pl
from jax.experimental.pallas import tpu as pltpu
from jax.sharding import PartitionSpec as P

HEADS = 16
EPSILON = 1e-05
MASKED = -1000000000.0
BF16 = jnp.bfloat16
F32 = jnp.float32
MESH = pl.DeviceIdType.MESH
DMA = pltpu.SemaphoreType.DMA
VMEM_SPEC = pl.BlockSpec(memory_space=pltpu.VMEM)


def remote(src, dst, send_sem, recv_sem, where):
    return pltpu.make_async_remote_copy(
        src, dst, send_sem, recv_sem, device_id=where, device_id_type=MESH
    )


def comm_params(collective_id):
    return pltpu.CompilerParams(collective_id=collective_id, has_side_effects=True)


def greet(peers):
    barrier = pltpu.get_barrier_semaphore()
    total = 0
    for here, where in peers:

        @pl.when(here)
        def _(where=where):
            pl.semaphore_signal(barrier, inc=1, device_id=where, device_id_type=MESH)

        total = total + jnp.where(here, 1, 0)
    pl.semaphore_wait(barrier, total)


def greet_all(count, device):
    barrier = pltpu.get_barrier_semaphore()

    def body(k, carry):
        pl.semaphore_signal(barrier, inc=1, device_id=device(k), device_id_type=MESH)
        return carry

    lax.fori_loop(1, count, body, 0)
    pl.semaphore_wait(barrier, count - 1)


def gather_kernel(nz, ny, pieces, count, *refs):
    noted = len(refs) > 2 * count + 3
    ins, outs, sems = refs[: count + noted], refs[count + noted : -3 - 2 * noted], refs[-3 - 2 * noted :]
    own_sem, send_sem, recv_sem = sems[:3]
    me = lax.axis_index("group")
    z, y = me // ny, me % ny

    def at(z_to, y_to):
        return {"group": z_to * ny + y_to}

    def note_copy(k):
        to = {"group": lax.rem(me + k, nz * ny)}
        return remote(ins[count], outs[count].at[me], sems[3].at[k], sems[4].at[k], to)

    if noted:
        greet_all(nz * ny, lambda k: {"group": lax.rem(me + k, nz * ny)})
        for k in range(1, nz * ny):
            note_copy(k).start()
        outs[count][me] = ins[count][...]
    else:
        greet(
            [
                (z > 0, at(z - 1, y)),
                (z < nz - 1, at(z + 1, y)),
                (y > 0, at(z, y - 1)),
                (y < ny - 1, at(z, y + 1)),
            ]
        )
    owns = [pltpu.make_async_copy(ins[n], outs[n].at[me], own_sem.at[n]) for n in range(count)]
    for own in owns:
        own.start()

    def part(ref, c):
        rows = ref.shape[0] // pieces
        return ref.at[pl.ds(c * rows, rows)]

    def copy(slot, source, n, c, where, first):
        return remote(
            part(ins[n], c) if first else part(outs[n].at[source], c),
            part(outs[n].at[source], c),
            send_sem.at[n, slot, source, c],
            recv_sem.at[n, source, c],
            where,
        )

    def outgoing(source, go):
        sz, sy = source // ny, source % ny
        column = go & (sy == y)
        return [
            (column & (sz <= z) & (z < nz - 1), 0, at(z + 1, y)),
            (column & (sz >= z) & (z > 0), 1, at(z - 1, y)),
            (go & (sy <= y) & (y < ny - 1), 2, at(z, y + 1)),
            (go & (sy >= y) & (y > 0), 3, at(z, y - 1)),
        ]

    def act(source, n, first, go, start):
        for c in range(pieces):
            if start and not first:

                @pl.when(go)
                def _():
                    copy(0, source, n, c, at(z, y), False).wait_recv()

            for cond, slot, where in outgoing(source, go):

                @pl.when(cond)
                def _(slot=slot, where=where):
                    one = copy(slot, source, n, c, where, first)
                    if start:
                        one.start()
                    else:
                        one.wait_send()

    order = []
    for dz in range(nz):
        for sz in [z] if dz == 0 else [z - dz, z + dz]:
            for dy in range(ny):
                for sy in [y] if dy == 0 else [y - dy, y + dy]:
                    inside = (sz >= 0) & (sz < nz) & (sy >= 0) & (sy < ny)
                    source = jnp.clip(sz, 0, nz - 1) * ny + jnp.clip(sy, 0, ny - 1)
                    order.append((dz + dy, dz, source, inside))
    order = sorted(order, key=lambda t: (t[0], -t[1]))
    for start in (True, False):
        for distance, _, source, inside in order:
            for n in range(count):
                act(source, n, distance == 0, inside, start)
        if start:
            for own in owns:
                own.wait()
    if noted:
        for k in range(1, nz * ny):
            note_copy(k).wait()


def gather_rows(blocks, groups, collective_id, pieces=2, note=None):
    nz = min(4, groups)
    count = len(blocks)
    notes = [] if note is None else [note]
    outs = pl.pallas_call(
        functools.partial(gather_kernel, nz, groups // nz, pieces, count),
        name="gather_rows",
        out_shape=[jax.ShapeDtypeStruct((groups,) + a.shape, a.dtype) for a in blocks + notes],
        in_specs=[VMEM_SPEC] * (count + len(notes)),
        out_specs=[pl.BlockSpec(memory_space=pl.ANY)] * count + [VMEM_SPEC] * len(notes),
        scratch_shapes=[DMA((count,)), DMA((count, 4, groups, pieces)), DMA((count, groups, pieces))]
        + [DMA((groups,))] * 2 * len(notes),
        compiler_params=comm_params(collective_id),
        cost_estimate=pl.CostEstimate(
            flops=0, bytes_accessed=200_000_000 * count, transcendentals=0
        ),
    )(*blocks, *notes)
    rows = [a.reshape(groups * b.shape[0], b.shape[1]) for a, b in zip(outs, blocks)]
    return rows + list(outs[count:])


def reduce_kernel(
    nz, ny, pieces, parts, note, out, note_out, ybuf, zbuf, landed, ysend, yrecv, zsend, zrecv, nsend, nrecv
):
    me = lax.axis_index("group")
    z, y = me // ny, me % ny
    rows = parts.shape[1] // pieces

    def at(z_to, y_to):
        return {"group": z_to * ny + y_to}

    def note_copy(k):
        to = lax.rem(me + k, nz * ny)
        return remote(note.at[to], landed.at[k], nsend.at[k], nrecv.at[k], {"group": to})

    greet_all(nz * ny, lambda k: {"group": lax.rem(me + k, nz * ny)})
    for k in range(1, nz * ny):
        note_copy(k).start()
    landed[0] = note[me]

    def part(ref, c):
        return ref.at[pl.ds(c * rows, rows)]

    def y_copy(dest, c):
        src, dst = part(parts.at[dest * ny + 1 - y], c), part(ybuf.at[dest], c)
        return remote(src, dst, ysend.at[dest, c], yrecv.at[dest, c], at(z, 1 - y))

    def z_copy(side, dest, c):
        src, dst = part(ybuf.at[dest], c), part(zbuf.at[side, dest], c)
        where = at(z - 1, y) if side else at(z + 1, y)
        return remote(src, dst, zsend.at[dest, c], zrecv.at[side, dest, c], where)

    order = []
    for d in range(nz - 1, 0, -1):
        order += [(z + d, z + d < nz, 0), (z - d, z - d >= 0, 1)]
    order = [(jnp.clip(dest, 0, nz - 1), inside, side) for dest, inside, side in order]
    for dest, inside, side in order:

        @pl.when(inside)
        def _():
            for c in range(pieces):
                y_copy(dest, c).start()

    for c in range(pieces):
        y_copy(z, c).start()
    for dest, inside, side in order:
        further = (z < nz - 1) if side else (z > 0)
        for c in range(pieces):
            span = pl.ds(c * rows, rows)

            @pl.when(inside)
            def _():
                y_copy(dest, c).wait_recv()
                pair = parts[dest * ny + y, span, :].astype(F32) + ybuf[dest, span, :].astype(F32)

                @pl.when(further)
                def _():
                    z_copy(side, dest, c).wait_recv()
                    ybuf[dest, span, :] = (pair + zbuf[side, dest, span, :].astype(F32)).astype(BF16)

                @pl.when(jnp.logical_not(further))
                def _():
                    ybuf[dest, span, :] = pair.astype(BF16)

                z_copy(side, dest, c).start()

    for c in range(pieces):
        span = pl.ds(c * rows, rows)
        y_copy(z, c).wait_recv()
        out[span, :] = parts[me, span, :].astype(F32) + ybuf[z, span, :].astype(F32)

        @pl.when(z > 0)
        def _():
            z_copy(0, z, c).wait_recv()
            out[span, :] += zbuf[0, z, span, :].astype(F32)

        @pl.when(z < nz - 1)
        def _():
            z_copy(1, z, c).wait_recv()
            out[span, :] += zbuf[1, z, span, :].astype(F32)

    for dest, inside, side in order:

        @pl.when(inside)
        def _():
            for c in range(pieces):
                y_copy(dest, c).wait_send()
                z_copy(side, dest, c).wait_send()

    for c in range(pieces):
        y_copy(z, c).wait_send()
    for k in range(1, nz * ny):
        note_copy(k).wait()
    note_out[...] = jnp.sum(landed[...], axis=0)


def reduce_rows(parts, note, groups, collective_id, pieces=2):
    nz = min(4, groups)
    ny = groups // nz
    if ny != 2:
        total = lax.psum_scatter(parts, "group", scatter_dimension=0, tiled=True).astype(F32)
        return total, lax.psum_scatter(note, "group", scatter_dimension=0, tiled=False)
    rows, width = parts.shape[0] // groups, parts.shape[1]
    return pl.pallas_call(
        functools.partial(reduce_kernel, nz, ny, pieces),
        name="reduce_rows",
        out_shape=[
            jax.ShapeDtypeStruct((rows, width), F32),
            jax.ShapeDtypeStruct(note.shape[1:], F32),
        ],
        in_specs=[VMEM_SPEC] * 2,
        out_specs=[VMEM_SPEC] * 2,
        scratch_shapes=[
            pltpu.VMEM((nz, rows, width), BF16),
            pltpu.VMEM((2, nz, rows, width), BF16),
            pltpu.VMEM(note.shape, F32),
            DMA((nz, pieces)),
            DMA((nz, pieces)),
            DMA((nz, pieces)),
            DMA((2, nz, pieces)),
            DMA((groups,)),
            DMA((groups,)),
        ],
        compiler_params=comm_params(collective_id),
        cost_estimate=pl.CostEstimate(flops=0, bytes_accessed=200_000_000, transcendentals=0),
    )(parts.reshape(groups, rows, width), note)


def swap_kernel(groups, to_rows, *refs):
    count = (len(refs) - 2) // 2
    ins, outs, (send_sem, recv_sem) = refs[:count], refs[count : 2 * count], refs[2 * count :]
    me = lax.axis_index("group")
    columns = ins[0].shape[-1] // (groups if to_rows else 1)
    wide = lambda ref, i: ref.at[:, pl.ds(pl.multiple_of(i * columns, columns), columns)]
    thin = lambda ref, i: ref.at[i]
    source, target = (wide, thin) if to_rows else (thin, wide)

    def peer(k):
        return lax.rem(me + k, groups)

    greet_all(groups, lambda k: {"group": peer(k)})

    def copy(n, k):
        to = peer(k)
        return remote(
            source(ins[n], to), target(outs[n], me), send_sem.at[n, k], recv_sem.at[n, k], {"group": to}
        )

    for k in range(1, groups):
        for n in range(count):
            copy(n, k).start()
    for n in range(count):
        if to_rows:
            outs[n][me] = ins[n][:, pl.ds(pl.multiple_of(me * columns, columns), columns)]
        else:
            outs[n][:, pl.ds(pl.multiple_of(me * columns, columns), columns)] = ins[n][me]
    for k in range(1, groups):
        for n in range(count):
            copy(n, k).wait()


def swap(arrays, groups, to_rows, collective_id):
    shape, count = arrays[0].shape, len(arrays)
    if to_rows:
        rows, columns = shape[0], shape[1] // groups
        out = (groups, rows, columns)
    else:
        rows, columns = shape[0] // groups, shape[1]
        arrays = [a.reshape(groups, rows, columns) for a in arrays]
        out = (rows, groups * columns)
    outs = pl.pallas_call(
        functools.partial(swap_kernel, groups, to_rows),
        name="swap",
        out_shape=[jax.ShapeDtypeStruct(out, a.dtype) for a in arrays],
        in_specs=[VMEM_SPEC] * count,
        out_specs=[VMEM_SPEC] * count,
        scratch_shapes=[DMA((count, groups)), DMA((count, groups))],
        compiler_params=comm_params(collective_id),
        cost_estimate=pl.CostEstimate(flops=0, bytes_accessed=30_000_000, transcendentals=0),
    )(*arrays)
    return [o.reshape(groups * rows, columns) if to_rows else o for o in outs]


def small_sum_kernel(axes, scatter, values, out, landed, send_sem, recv_sem):
    sizes = [lax.axis_size(a) for a in axes]
    count = math.prod(sizes)
    me = 0
    for a, n in zip(axes, sizes):
        me = me * n + lax.axis_index(a)

    def peer(k):
        return lax.rem(me + k, count)

    def device(k):
        to = peer(k)
        if len(axes) == 1:
            return {axes[0]: to}
        return {axes[0]: to // sizes[1], axes[1]: lax.rem(to, sizes[1])}

    greet_all(count, device)

    def copy(k):
        src = values.at[peer(k)] if scatter else values
        return remote(src, landed.at[k], send_sem.at[k], recv_sem.at[k], device(k))

    def start(k, carry):
        copy(k).start()
        return carry

    def wait(k, carry):
        copy(k).wait()
        return carry

    lax.fori_loop(1, count, start, 0)
    landed[0] = values[me] if scatter else values[...]
    lax.fori_loop(1, count, wait, 0)
    out[...] = jnp.sum(landed[...], axis=0)


def small_sum(values, axes, scatter, collective_id):
    count = math.prod(lax.axis_size(a) for a in axes)
    shape = values.shape[-2:]
    return pl.pallas_call(
        functools.partial(small_sum_kernel, axes, scatter),
        name="small_sum",
        out_shape=jax.ShapeDtypeStruct(shape, F32),
        in_specs=[VMEM_SPEC],
        out_specs=VMEM_SPEC,
        scratch_shapes=[pltpu.VMEM((count,) + shape, F32), DMA((count,)), DMA((count,))],
        compiler_params=comm_params(collective_id),
        cost_estimate=pl.CostEstimate(flops=0, bytes_accessed=10_000_000, transcendentals=0),
    )(values)


def rms_norm(values_in, gain_vec):
    return (
        values_in
        * lax.rsqrt(jnp.mean(values_in * values_in, axis=-1, keepdims=True) + EPSILON)
        * gain_vec
    )


def angles(row_count, head_dim):
    places = jnp.arange(row_count, dtype=jnp.int32).astype(F32)
    frequency = jnp.exp(-math.log(10000.0) * 2.0 * jnp.arange(head_dim // 2, dtype=F32) / head_dim)
    turn_angle = places[:, None] * frequency[None, :]
    return (jnp.cos(turn_angle)[:, None, :], jnp.sin(turn_angle)[:, None, :])


def rotate(values_in, cosine, sine):
    half_dim = values_in.shape[-1] // 2
    first_half = values_in[..., :half_dim]
    second = values_in[..., half_dim:]
    return jnp.concatenate(
        [first_half * cosine - second * sine, second * cosine + first_half * sine], axis=-1
    )


def mm(left, right):
    return jnp.dot(left, right, preferred_element_type=F32)


def mm_tn(left, right):
    return lax.dot_general(left, right, (((0,), (0,)), ((), ())), preferred_element_type=F32)


def mm_nt(left, right):
    return lax.dot_general(left, right, (((1,), (1,)), ((), ())), preferred_element_type=F32)


def ein(spec, *ops):
    return jnp.einsum(spec, *ops, preferred_element_type=F32)


def shards(
    layer_in,
    segment_ids,
    routing,
    out_grad,
    attn_gain,
    w_query,
    w_key,
    w_value,
    query_gain,
    key_gain,
    w_out,
    mlp_gain,
    w_router,
    w_gate,
    w_up,
    w_down,
):
    groups = lax.axis_size("group")
    sources = lax.axis_size("expert")
    me = lax.axis_index("group")
    rows = layer_in.shape[1]
    width = layer_in.shape[2]
    length = rows * groups
    head_dim = width // HEADS
    heads = HEADS // groups
    cols = width // groups
    local_experts = w_gate.shape[0]
    experts = local_experts * sources
    hidden_size = w_gate.shape[2]
    parts = groups // local_experts
    part = hidden_size // parts
    score_scale = 1.0 / math.sqrt(head_dim)

    def own_cols(matrix, axis):
        return lax.dynamic_slice_in_dim(matrix, me * cols, cols, axis)

    def slices(w):
        w = w.reshape(local_experts, w.shape[1], parts, part).transpose(0, 2, 1, 3)
        return w.reshape(groups, w.shape[2], part)

    def exchange(w):
        return lax.all_to_all(w, "group", 0, 0, tiled=True)

    def row_of_devices(w):
        return lax.all_gather(w, "expert", axis=0, tiled=False)

    together = lax.optimization_barrier
    gate_own = exchange(slices(w_gate))

    inputs = layer_in[0].astype(F32)
    normed_b = rms_norm(inputs, attn_gain).astype(BF16)
    expert_ids = jnp.arange(experts, dtype=jnp.int32)
    marks = jnp.any(routing[0][:, :, None] == expert_ids[None, None, :], axis=1).astype(F32)
    marks = jnp.concatenate([marks.T, segment_ids[0].astype(F32)[None]], axis=0)
    normed_all, grad_all, marks = gather_rows([normed_b, out_grad[0]], groups, 1, note=marks)
    marks = marks.transpose(1, 0, 2).reshape(experts + 1, length)
    chosen, seg_all = marks[:experts].T > 0.5, marks[experts]
    down_in = w_down.reshape(groups, part, cols)
    gate_own, down_in, normed_late = together((gate_own, down_in, normed_all))
    gate_w = row_of_devices(gate_own.reshape(width, part))
    down_own = exchange(down_in)
    wq, wk, wv = own_cols(w_query, 1), own_cols(w_key, 1), own_cols(w_value, 1)
    query_raw, key_raw = mm(normed_all, wq), mm(normed_all, wk)
    values_b = mm(normed_all, wv).astype(BF16).reshape(length, heads, head_dim)

    def row_sums(first, second, collective_id):
        sums = jnp.stack([jnp.sum(first, axis=1), jnp.sum(second, axis=1)])
        sums = small_sum(sums.reshape(-1, 128), ("group",), False, collective_id)
        return sums.reshape(2, length, 1) / width

    scales = lax.rsqrt(row_sums(query_raw * query_raw, key_raw * key_raw, 2) + EPSILON)
    query_scale, key_scale = scales[0], scales[1]
    query_gain_c, key_gain_c = own_cols(query_gain, 0), own_cols(key_gain, 0)
    cosine, sine = angles(length, head_dim)

    def turned(raw, scale, gain):
        return rotate((raw * scale * gain).reshape(length, heads, head_dim), cosine, sine)

    queries_b = turned(query_raw, query_scale, query_gain_c).astype(BF16)
    keys_b = turned(key_raw, key_scale, key_gain_c).astype(BF16)
    place = jnp.arange(length, dtype=jnp.int32)
    allowed = (seg_all[:, None] == seg_all[None, :]) & (place[None, :] <= place[:, None])
    scores = jnp.where(allowed[None], ein("qhd,khd->hqk", queries_b, keys_b) * score_scale, MASKED)
    top_score = jnp.max(scores, axis=-1, keepdims=True)
    log_total = top_score + jnp.log(jnp.sum(jnp.exp(scores - top_score), axis=-1, keepdims=True))
    probs = jnp.exp(scores - log_total)
    probs_b = probs.astype(BF16)
    mixed_c = ein("hqk,khd->qhd", probs_b, values_b).reshape(length, cols).astype(BF16)
    down_own, mixed_in = together((down_own, mixed_c))
    down_w = row_of_devices(down_own.transpose(1, 0, 2).reshape(part, width))
    (mixed_b,) = swap([mixed_in], groups, False, 3)
    up_in, mixed_b = together((slices(w_up), mixed_b))
    up_own = exchange(up_in)
    resid = inputs + mm(mixed_b, w_out)
    normed_mlp_b = rms_norm(resid, mlp_gain).astype(BF16)
    (mlp_all,) = gather_rows([normed_mlp_b], groups, 4)
    up_own, down_w, mlp_late = together((up_own, down_w, mlp_all))
    up_w = row_of_devices(up_own.reshape(width, part))

    router_all = jax.nn.softmax(mm(mlp_all, w_router), axis=-1)
    picked = jnp.where(chosen, router_all, 0.0).reshape(length, sources, local_experts)
    picked = lax.dynamic_index_in_dim(picked, me // parts, 2, keepdims=True)
    gate_pre = ein("td,edf->tef", mlp_all, gate_w)
    up_pre = ein("td,edf->tef", mlp_all, up_w)
    sigma = jax.nn.sigmoid(gate_pre)
    hidden = gate_pre * sigma * up_pre
    hidden_b = (hidden * picked).astype(BF16)
    out_part = ein("tef,efd->td", hidden_b, down_w).astype(BF16)
    mixture = lax.psum_scatter(out_part, "group", scatter_dimension=0, tiled=True)
    hidden_grad = ein("td,efd->tef", grad_all, down_w)
    picked_grad = jnp.sum(hidden * hidden_grad, axis=2)
    hidden_grad = hidden_grad * picked
    gate_grad_b = (hidden_grad * up_pre * sigma * (1.0 + gate_pre * (1.0 - sigma))).astype(BF16)
    up_grad_b = (hidden_grad * gate_pre * sigma).astype(BF16)
    own_expert = jnp.arange(local_experts, dtype=jnp.int32) == me // parts
    full_part = jnp.where(own_expert[None, None, :], picked_grad[:, :, None], 0.0)
    full_part = jnp.where(chosen, full_part.reshape(length, experts), 0.0)
    full_part = full_part.T.reshape(experts, groups, rows).transpose(1, 0, 2)
    gate_w_part = ein("td,tef->edf", mlp_late, gate_grad_b).astype(BF16)
    up_w_part = ein("td,tef->edf", mlp_late, up_grad_b).astype(BF16)
    down_w_part = ein("tef,td->efd", hidden_b, grad_all).astype(BF16)
    up_w_part, down_w_part, gate_grad_b, up_grad_b = together(
        (up_w_part, down_w_part, gate_grad_b, up_grad_b)
    )

    def over_row(w):
        return lax.psum_scatter(w, "expert", scatter_dimension=0, tiled=False)

    gate_sum, up_sum, down_sum = over_row(gate_w_part), over_row(up_w_part), over_row(down_w_part)
    slot_part = ein("tef,edf->td", gate_grad_b, gate_w) + ein("tef,edf->td", up_grad_b, up_w)
    slot_part, mixture = together((slot_part.astype(BF16), mixture))
    slot_sum, router_full_grad = reduce_rows(slot_part, full_part, groups, 5)
    router_full_grad = router_full_grad.T

    def slices_out(w):
        w = w.reshape(local_experts, parts, cols, part).transpose(0, 2, 1, 3)
        return w.reshape(local_experts, cols, hidden_size).astype(F32)

    result = (resid + mixture.astype(F32)).astype(BF16)
    grad_out = out_grad[0].astype(F32)
    router = jax.nn.softmax(mm(normed_mlp_b, w_router), axis=-1)
    logits_grad_b = (
        router * (router_full_grad - jnp.sum(router * router_full_grad, axis=-1, keepdims=True))
    ).astype(BF16)
    router_w_grad = mm_tn(normed_mlp_b, logits_grad_b)
    mlp_in_grad = slot_sum + mm_nt(logits_grad_b, w_router)
    _, mlp_back = jax.vjp(rms_norm, resid, mlp_gain)
    resid_part, mlp_gain_grad = mlp_back(mlp_in_grad)
    resid_grad = grad_out + resid_part
    attn_grad_b = resid_grad.astype(BF16)
    (attn_grad_all,) = gather_rows([attn_grad_b], groups, 6)
    gate_sum, up_sum, attn_grad_late = together((gate_sum, up_sum, attn_grad_all))
    gate_up_sum = jnp.concatenate([gate_sum, up_sum], axis=1).reshape(groups, cols, 2 * part)
    gate_up_sum = exchange(gate_up_sum)
    mixed_grad_c = mm_nt(attn_grad_all, own_cols(w_out, 0)).astype(BF16)
    mixed_grad_c = mixed_grad_c.reshape(length, heads, head_dim)

    prob_grad = ein("qhd,khd->hqk", mixed_grad_c, values_b)
    delta = jnp.sum(probs * prob_grad, axis=-1, keepdims=True)
    score_grad_b = (probs * (prob_grad - delta) * score_scale).astype(BF16)
    query_grad = ein("hqk,khd->qhd", score_grad_b, keys_b)
    key_grad = ein("hqk,qhd->khd", score_grad_b, queries_b)
    value_grad_b = ein("hqk,qhd->khd", probs_b, mixed_grad_c).astype(BF16).reshape(length, cols)

    def unturned(grad):
        return rotate(grad, cosine, -sine).reshape(length, cols)

    query_turn, key_turn = unturned(query_grad), unturned(key_grad)
    query_mix, key_mix = query_turn * query_gain_c, key_turn * key_gain_c
    dots = row_sums(query_mix * query_raw, key_mix * key_raw, 7)
    query_raw_b = (
        query_scale * query_mix - query_raw * query_scale**3 * dots[0]
    ).astype(BF16)
    key_raw_b = (key_scale * key_mix - key_raw * key_scale**3 * dots[1]).astype(BF16)
    query_gain_part = jnp.sum(query_turn * query_raw * query_scale, axis=0)
    key_gain_part = jnp.sum(key_turn * key_raw * key_scale, axis=0)
    raw_grads = [query_raw_b, key_raw_b, value_grad_b]
    (query_own, key_own, value_own), raw_grads, gate_up_sum, down_sum = together(
        (swap(raw_grads, groups, False, 8), raw_grads, gate_up_sum, down_sum)
    )
    down_sum = exchange(down_sum.reshape(part, groups, cols).transpose(1, 0, 2))
    out_w_part = mm_tn(mixed_c, attn_grad_late).astype(BF16)
    out_w_grad = lax.psum_scatter(out_w_part, "expert", scatter_dimension=0, tiled=True)
    qkv_part = mm_tn(normed_late, jnp.concatenate(raw_grads, axis=1)).astype(BF16)
    qkv_part = qkv_part.reshape(groups, sources, -1, 3 * cols).transpose(1, 0, 2, 3)
    qkv_part = over_row(qkv_part.reshape(sources, -1, 3 * cols)).reshape(groups, -1, 3 * cols)
    qkv_part = exchange(qkv_part)
    qkv_part = qkv_part.transpose(1, 0, 2).reshape(-1, groups, 3, cols).astype(F32)
    normed_grad = mm_nt(query_own, w_query) + mm_nt(key_own, w_key) + mm_nt(value_own, w_value)
    _, attn_back = jax.vjp(rms_norm, inputs, attn_gain)
    input_part, attn_gain_grad = attn_back(normed_grad)
    input_grad = resid_grad + input_part
    wide = [
        lax.dynamic_update_slice_in_dim(jnp.zeros((width,), F32), part, me * cols, 0)
        for part in (query_gain_part, key_gain_part)
    ]
    small = jnp.concatenate([router_w_grad.T, jnp.stack([mlp_gain_grad, attn_gain_grad] + wide)])
    devices = groups * sources
    small = small.reshape(-1, devices, width // devices).transpose(1, 0, 2).reshape(devices, -1)
    used = small.shape[1]
    small = jnp.pad(small, ((0, 0), (0, -used % 1024))).reshape(devices, -1, 128)
    small = small_sum(small, ("group", "expert"), True, 9).reshape(-1)[:used]
    small = small.reshape(-1, width // devices)
    return (
        result[None],
        input_grad[None],
        small[experts + 1],
        qkv_part[:, :, 0].reshape(-1, width),
        qkv_part[:, :, 1].reshape(-1, width),
        qkv_part[:, :, 2].reshape(-1, width),
        small[experts + 2],
        small[experts + 3],
        out_w_grad.astype(F32),
        small[experts],
        small[:experts].T,
        slices_out(gate_up_sum[:, :, :part]),
        slices_out(gate_up_sum[:, :, part:]),
        down_sum.reshape(local_experts, hidden_size, cols).astype(F32),
    )


def solution(mesh):
    token = P("expert", "group", None)
    every = P(("group", "expert"))
    return jax.shard_map(
        shards,
        mesh=mesh,
        in_specs=(token, P("expert", "group"), token, token)
        + (P(),) * 9
        + (token, token, P("expert", None, "group")),
        out_specs=(token, token)
        + (every,) * 9
        + (token, token, P("expert", None, "group")),
        check_vma=False,
    )
```

```python
import functools
import math

import jax
import jax.numpy as jnp
from jax import lax
from jax.experimental import pallas as pl
from jax.experimental.pallas import tpu as pltpu
from jax.sharding import PartitionSpec as P

HEADS = 16
EPSILON = 1e-05
MASKED = -1000000000.0
BF16 = jnp.bfloat16
F32 = jnp.float32
MESH = pl.DeviceIdType.MESH
DMA = pltpu.SemaphoreType.DMA
VMEM_SPEC = pl.BlockSpec(memory_space=pltpu.VMEM)


def remote(src, dst, send_sem, recv_sem, where):
    return pltpu.make_async_remote_copy(
        src, dst, send_sem, recv_sem, device_id=where, device_id_type=MESH
    )


def comm_params(collective_id):
    return pltpu.CompilerParams(collective_id=collective_id, has_side_effects=True)


def greet(peers):
    barrier = pltpu.get_barrier_semaphore()
    total = 0
    for here, where in peers:

        @pl.when(here)
        def _(where=where):
            pl.semaphore_signal(barrier, inc=1, device_id=where, device_id_type=MESH)

        total = total + jnp.where(here, 1, 0)
    pl.semaphore_wait(barrier, total)


def greet_all(count, device):
    barrier = pltpu.get_barrier_semaphore()

    def body(k, carry):
        pl.semaphore_signal(barrier, inc=1, device_id=device(k), device_id_type=MESH)
        return carry

    lax.fori_loop(1, count, body, 0)
    pl.semaphore_wait(barrier, count - 1)


def gather_kernel(nz, ny, pieces, count, *refs):
    noted = len(refs) > 2 * count + 3
    ins, outs, sems = refs[: count + noted], refs[count + noted : -3 - 2 * noted], refs[-3 - 2 * noted :]
    own_sem, send_sem, recv_sem = sems[:3]
    me = lax.axis_index("group")
    z, y = me // ny, me % ny

    def at(z_to, y_to):
        return {"group": z_to * ny + y_to}

    def note_copy(k):
        to = {"group": lax.rem(me + k, nz * ny)}
        return remote(ins[count], outs[count].at[me], sems[3].at[k], sems[4].at[k], to)

    if noted:
        greet_all(nz * ny, lambda k: {"group": lax.rem(me + k, nz * ny)})
        for k in range(1, nz * ny):
            note_copy(k).start()
        outs[count][me] = ins[count][...]
    else:
        greet(
            [
                (z > 0, at(z - 1, y)),
                (z < nz - 1, at(z + 1, y)),
                (y > 0, at(z, y - 1)),
                (y < ny - 1, at(z, y + 1)),
            ]
        )
    owns = [pltpu.make_async_copy(ins[n], outs[n].at[me], own_sem.at[n]) for n in range(count)]
    for own in owns:
        own.start()

    def part(ref, c):
        rows = ref.shape[0] // pieces
        return ref.at[pl.ds(c * rows, rows)]

    def copy(slot, source, n, c, where, first):
        return remote(
            part(ins[n], c) if first else part(outs[n].at[source], c),
            part(outs[n].at[source], c),
            send_sem.at[n, slot, source, c],
            recv_sem.at[n, source, c],
            where,
        )

    def outgoing(source, go):
        sz, sy = source // ny, source % ny
        column = go & (sy == y)
        return [
            (column & (sz <= z) & (z < nz - 1), 0, at(z + 1, y)),
            (column & (sz >= z) & (z > 0), 1, at(z - 1, y)),
            (go & (sy <= y) & (y < ny - 1), 2, at(z, y + 1)),
            (go & (sy >= y) & (y > 0), 3, at(z, y - 1)),
        ]

    def act(source, n, first, go, start):
        for c in range(pieces):
            if start and not first:

                @pl.when(go)
                def _():
                    copy(0, source, n, c, at(z, y), False).wait_recv()

            for cond, slot, where in outgoing(source, go):

                @pl.when(cond)
                def _(slot=slot, where=where):
                    one = copy(slot, source, n, c, where, first)
                    if start:
                        one.start()
                    else:
                        one.wait_send()

    order = []
    for dz in range(nz):
        for sz in [z] if dz == 0 else [z - dz, z + dz]:
            for dy in range(ny):
                for sy in [y] if dy == 0 else [y - dy, y + dy]:
                    inside = (sz >= 0) & (sz < nz) & (sy >= 0) & (sy < ny)
                    source = jnp.clip(sz, 0, nz - 1) * ny + jnp.clip(sy, 0, ny - 1)
                    order.append((dz + dy, dz, source, inside))
    order = sorted(order, key=lambda t: (t[0], -t[1]))
    for start in (True, False):
        for distance, _, source, inside in order:
            for n in range(count):
                act(source, n, distance == 0, inside, start)
        if start:
            for own in owns:
                own.wait()
    if noted:
        for k in range(1, nz * ny):
            note_copy(k).wait()


def gather_rows(blocks, groups, collective_id, pieces=2, note=None):
    nz = min(4, groups)
    count = len(blocks)
    notes = [] if note is None else [note]
    outs = pl.pallas_call(
        functools.partial(gather_kernel, nz, groups // nz, pieces, count),
        name="gather_rows",
        out_shape=[jax.ShapeDtypeStruct((groups,) + a.shape, a.dtype) for a in blocks + notes],
        in_specs=[VMEM_SPEC] * (count + len(notes)),
        out_specs=[pl.BlockSpec(memory_space=pl.ANY)] * count + [VMEM_SPEC] * len(notes),
        scratch_shapes=[DMA((count,)), DMA((count, 4, groups, pieces)), DMA((count, groups, pieces))]
        + [DMA((groups,))] * 2 * len(notes),
        compiler_params=comm_params(collective_id),
        cost_estimate=pl.CostEstimate(
            flops=0, bytes_accessed=200_000_000 * count, transcendentals=0
        ),
    )(*blocks, *notes)
    rows = [a.reshape(groups * b.shape[0], b.shape[1]) for a, b in zip(outs, blocks)]
    return rows + list(outs[count:])


def reduce_kernel(
    nz, ny, pieces, parts, note, out, note_out, ybuf, zbuf, landed, ysend, yrecv, zsend, zrecv, nsend, nrecv
):
    me = lax.axis_index("group")
    z, y = me // ny, me % ny
    rows = parts.shape[1] // pieces

    def at(z_to, y_to):
        return {"group": z_to * ny + y_to}

    def note_copy(k):
        to = lax.rem(me + k, nz * ny)
        return remote(note.at[to], landed.at[k], nsend.at[k], nrecv.at[k], {"group": to})

    greet_all(nz * ny, lambda k: {"group": lax.rem(me + k, nz * ny)})
    for k in range(1, nz * ny):
        note_copy(k).start()
    landed[0] = note[me]

    def part(ref, c):
        return ref.at[pl.ds(c * rows, rows)]

    def y_copy(dest, c):
        src, dst = part(parts.at[dest * ny + 1 - y], c), part(ybuf.at[dest], c)
        return remote(src, dst, ysend.at[dest, c], yrecv.at[dest, c], at(z, 1 - y))

    def z_copy(side, dest, c):
        src, dst = part(ybuf.at[dest], c), part(zbuf.at[side, dest], c)
        where = at(z - 1, y) if side else at(z + 1, y)
        return remote(src, dst, zsend.at[dest, c], zrecv.at[side, dest, c], where)

    order = []
    for d in range(nz - 1, 0, -1):
        order += [(z + d, z + d < nz, 0), (z - d, z - d >= 0, 1)]
    order = [(jnp.clip(dest, 0, nz - 1), inside, side) for dest, inside, side in order]
    for dest, inside, side in order:

        @pl.when(inside)
        def _():
            for c in range(pieces):
                y_copy(dest, c).start()

    for c in range(pieces):
        y_copy(z, c).start()
    for dest, inside, side in order:
        further = (z < nz - 1) if side else (z > 0)
        for c in range(pieces):
            span = pl.ds(c * rows, rows)

            @pl.when(inside)
            def _():
                y_copy(dest, c).wait_recv()
                pair = parts[dest * ny + y, span, :].astype(F32) + ybuf[dest, span, :].astype(F32)

                @pl.when(further)
                def _():
                    z_copy(side, dest, c).wait_recv()
                    ybuf[dest, span, :] = (pair + zbuf[side, dest, span, :].astype(F32)).astype(BF16)

                @pl.when(jnp.logical_not(further))
                def _():
                    ybuf[dest, span, :] = pair.astype(BF16)

                z_copy(side, dest, c).start()

    for c in range(pieces):
        span = pl.ds(c * rows, rows)
        y_copy(z, c).wait_recv()
        out[span, :] = parts[me, span, :].astype(F32) + ybuf[z, span, :].astype(F32)

        @pl.when(z > 0)
        def _():
            z_copy(0, z, c).wait_recv()
            out[span, :] += zbuf[0, z, span, :].astype(F32)

        @pl.when(z < nz - 1)
        def _():
            z_copy(1, z, c).wait_recv()
            out[span, :] += zbuf[1, z, span, :].astype(F32)

    for dest, inside, side in order:

        @pl.when(inside)
        def _():
            for c in range(pieces):
                y_copy(dest, c).wait_send()
                z_copy(side, dest, c).wait_send()

    for c in range(pieces):
        y_copy(z, c).wait_send()
    for k in range(1, nz * ny):
        note_copy(k).wait()
    note_out[...] = jnp.sum(landed[...], axis=0)


def reduce_rows(parts, note, groups, collective_id, pieces=2):
    nz = min(4, groups)
    ny = groups // nz
    if ny != 2:
        total = lax.psum_scatter(parts, "group", scatter_dimension=0, tiled=True).astype(F32)
        return total, lax.psum_scatter(note, "group", scatter_dimension=0, tiled=False)
    rows, width = parts.shape[0] // groups, parts.shape[1]
    return pl.pallas_call(
        functools.partial(reduce_kernel, nz, ny, pieces),
        name="reduce_rows",
        out_shape=[
            jax.ShapeDtypeStruct((rows, width), F32),
            jax.ShapeDtypeStruct(note.shape[1:], F32),
        ],
        in_specs=[VMEM_SPEC] * 2,
        out_specs=[VMEM_SPEC] * 2,
        scratch_shapes=[
            pltpu.VMEM((nz, rows, width), BF16),
            pltpu.VMEM((2, nz, rows, width), BF16),
            pltpu.VMEM(note.shape, F32),
            DMA((nz, pieces)),
            DMA((nz, pieces)),
            DMA((nz, pieces)),
            DMA((2, nz, pieces)),
            DMA((groups,)),
            DMA((groups,)),
        ],
        compiler_params=comm_params(collective_id),
        cost_estimate=pl.CostEstimate(flops=0, bytes_accessed=200_000_000, transcendentals=0),
    )(parts.reshape(groups, rows, width), note)


def swap_kernel(groups, to_rows, *refs):
    count = (len(refs) - 2) // 2
    ins, outs, (send_sem, recv_sem) = refs[:count], refs[count : 2 * count], refs[2 * count :]
    me = lax.axis_index("group")
    columns = ins[0].shape[-1] // (groups if to_rows else 1)
    wide = lambda ref, i: ref.at[:, pl.ds(pl.multiple_of(i * columns, columns), columns)]
    thin = lambda ref, i: ref.at[i]
    source, target = (wide, thin) if to_rows else (thin, wide)

    def peer(k):
        return lax.rem(me + k, groups)

    greet_all(groups, lambda k: {"group": peer(k)})

    def copy(n, k):
        to = peer(k)
        return remote(
            source(ins[n], to), target(outs[n], me), send_sem.at[n, k], recv_sem.at[n, k], {"group": to}
        )

    for k in range(1, groups):
        for n in range(count):
            copy(n, k).start()
    for n in range(count):
        if to_rows:
            outs[n][me] = ins[n][:, pl.ds(pl.multiple_of(me * columns, columns), columns)]
        else:
            outs[n][:, pl.ds(pl.multiple_of(me * columns, columns), columns)] = ins[n][me]
    for k in range(1, groups):
        for n in range(count):
            copy(n, k).wait()


def swap(arrays, groups, to_rows, collective_id):
    shape, count = arrays[0].shape, len(arrays)
    if to_rows:
        rows, columns = shape[0], shape[1] // groups
        out = (groups, rows, columns)
    else:
        rows, columns = shape[0] // groups, shape[1]
        arrays = [a.reshape(groups, rows, columns) for a in arrays]
        out = (rows, groups * columns)
    outs = pl.pallas_call(
        functools.partial(swap_kernel, groups, to_rows),
        name="swap",
        out_shape=[jax.ShapeDtypeStruct(out, a.dtype) for a in arrays],
        in_specs=[VMEM_SPEC] * count,
        out_specs=[VMEM_SPEC] * count,
        scratch_shapes=[DMA((count, groups)), DMA((count, groups))],
        compiler_params=comm_params(collective_id),
        cost_estimate=pl.CostEstimate(flops=0, bytes_accessed=30_000_000, transcendentals=0),
    )(*arrays)
    return [o.reshape(groups * rows, columns) if to_rows else o for o in outs]


def small_sum_kernel(axes, scatter, values, out, landed, send_sem, recv_sem):
    sizes = [lax.axis_size(a) for a in axes]
    count = math.prod(sizes)
    me = 0
    for a, n in zip(axes, sizes):
        me = me * n + lax.axis_index(a)

    def peer(k):
        return lax.rem(me + k, count)

    def device(k):
        to = peer(k)
        if len(axes) == 1:
            return {axes[0]: to}
        return {axes[0]: to // sizes[1], axes[1]: lax.rem(to, sizes[1])}

    greet_all(count, device)

    def copy(k):
        src = values.at[peer(k)] if scatter else values
        return remote(src, landed.at[k], send_sem.at[k], recv_sem.at[k], device(k))

    def start(k, carry):
        copy(k).start()
        return carry

    def wait(k, carry):
        copy(k).wait()
        return carry

    lax.fori_loop(1, count, start, 0)
    landed[0] = values[me] if scatter else values[...]
    lax.fori_loop(1, count, wait, 0)
    out[...] = jnp.sum(landed[...], axis=0)


def small_sum(values, axes, scatter, collective_id):
    count = math.prod(lax.axis_size(a) for a in axes)
    shape = values.shape[-2:]
    return pl.pallas_call(
        functools.partial(small_sum_kernel, axes, scatter),
        name="small_sum",
        out_shape=jax.ShapeDtypeStruct(shape, F32),
        in_specs=[VMEM_SPEC],
        out_specs=VMEM_SPEC,
        scratch_shapes=[pltpu.VMEM((count,) + shape, F32), DMA((count,)), DMA((count,))],
        compiler_params=comm_params(collective_id),
        cost_estimate=pl.CostEstimate(flops=0, bytes_accessed=10_000_000, transcendentals=0),
    )(values)


def rms_norm(values_in, gain_vec):
    return (
        values_in
        * lax.rsqrt(jnp.mean(values_in * values_in, axis=-1, keepdims=True) + EPSILON)
        * gain_vec
    )


def angles(row_count, head_dim):
    places = jnp.arange(row_count, dtype=jnp.int32).astype(F32)
    frequency = jnp.exp(-math.log(10000.0) * 2.0 * jnp.arange(head_dim // 2, dtype=F32) / head_dim)
    turn_angle = places[:, None] * frequency[None, :]
    return (jnp.cos(turn_angle)[:, None, :], jnp.sin(turn_angle)[:, None, :])


def rotate(values_in, cosine, sine):
    half_dim = values_in.shape[-1] // 2
    first_half = values_in[..., :half_dim]
    second = values_in[..., half_dim:]
    return jnp.concatenate(
        [first_half * cosine - second * sine, second * cosine + first_half * sine], axis=-1
    )


def mm(left, right):
    return jnp.dot(left, right, preferred_element_type=F32)


def mm_tn(left, right):
    return lax.dot_general(left, right, (((0,), (0,)), ((), ())), preferred_element_type=F32)


def mm_nt(left, right):
    return lax.dot_general(left, right, (((1,), (1,)), ((), ())), preferred_element_type=F32)


def ein(spec, *ops):
    return jnp.einsum(spec, *ops, preferred_element_type=F32)


def shards(
    layer_in,
    segment_ids,
    routing,
    out_grad,
    attn_gain,
    w_query,
    w_key,
    w_value,
    query_gain,
    key_gain,
    w_out,
    mlp_gain,
    w_router,
    w_gate,
    w_up,
    w_down,
):
    groups = lax.axis_size("group")
    sources = lax.axis_size("expert")
    me = lax.axis_index("group")
    rows = layer_in.shape[1]
    width = layer_in.shape[2]
    length = rows * groups
    head_dim = width // HEADS
    heads = HEADS // groups
    cols = width // groups
    local_experts = w_gate.shape[0]
    experts = local_experts * sources
    hidden_size = w_gate.shape[2]
    parts = groups // local_experts
    part = hidden_size // parts
    score_scale = 1.0 / math.sqrt(head_dim)

    def own_cols(matrix, axis):
        return lax.dynamic_slice_in_dim(matrix, me * cols, cols, axis)

    def slices(w):
        w = w.reshape(local_experts, w.shape[1], parts, part).transpose(0, 2, 1, 3)
        return w.reshape(groups, w.shape[2], part)

    def exchange(w):
        return lax.all_to_all(w, "group", 0, 0, tiled=True)

    def row_of_devices(w):
        return lax.all_gather(w, "expert", axis=0, tiled=False)

    together = lax.optimization_barrier
    gate_own = exchange(slices(w_gate))

    inputs = layer_in[0].astype(F32)
    normed_b = rms_norm(inputs, attn_gain).astype(BF16)
    expert_ids = jnp.arange(experts, dtype=jnp.int32)
    marks = jnp.any(routing[0][:, :, None] == expert_ids[None, None, :], axis=1).astype(F32)
    marks = jnp.concatenate([marks.T, segment_ids[0].astype(F32)[None]], axis=0)
    normed_all, marks = gather_rows([normed_b], groups, 1, note=marks)
    marks = marks.transpose(1, 0, 2).reshape(experts + 1, length)
    chosen, seg_all = marks[:experts].T > 0.5, marks[experts]
    down_in = w_down.reshape(groups, part, cols)
    gate_own, down_in, normed_late = together((gate_own, down_in, normed_all))
    gate_w = row_of_devices(gate_own.reshape(width, part))
    down_own = exchange(down_in)
    wq, wk, wv = own_cols(w_query, 1), own_cols(w_key, 1), own_cols(w_value, 1)
    query_raw, key_raw = mm(normed_all, wq), mm(normed_all, wk)
    values_b = mm(normed_all, wv).astype(BF16).reshape(length, heads, head_dim)

    def row_sums(first, second, collective_id):
        sums = jnp.stack([jnp.sum(first, axis=1), jnp.sum(second, axis=1)])
        sums = small_sum(sums.reshape(-1, 128), ("group",), False, collective_id)
        return sums.reshape(2, length, 1) / width

    scales = lax.rsqrt(row_sums(query_raw * query_raw, key_raw * key_raw, 2) + EPSILON)
    query_scale, key_scale = scales[0], scales[1]
    query_gain_c, key_gain_c = own_cols(query_gain, 0), own_cols(key_gain, 0)
    cosine, sine = angles(length, head_dim)

    def turned(raw, scale, gain):
        return rotate((raw * scale * gain).reshape(length, heads, head_dim), cosine, sine)

    queries_b = turned(query_raw, query_scale, query_gain_c).astype(BF16)
    keys_b = turned(key_raw, key_scale, key_gain_c).astype(BF16)
    place = jnp.arange(length, dtype=jnp.int32)
    allowed = (seg_all[:, None] == seg_all[None, :]) & (place[None, :] <= place[:, None])
    scores = jnp.where(allowed[None], ein("qhd,khd->hqk", queries_b, keys_b) * score_scale, MASKED)
    top_score = jnp.max(scores, axis=-1, keepdims=True)
    log_total = top_score + jnp.log(jnp.sum(jnp.exp(scores - top_score), axis=-1, keepdims=True))
    probs = jnp.exp(scores - log_total)
    probs_b = probs.astype(BF16)
    mixed_c = ein("hqk,khd->qhd", probs_b, values_b).reshape(length, cols).astype(BF16)
    down_own, mixed_in = together((down_own, mixed_c))
    down_w = row_of_devices(down_own.transpose(1, 0, 2).reshape(part, width))
    (mixed_b,) = swap([mixed_in], groups, False, 3)
    up_in, mixed_b = together((slices(w_up), mixed_b))
    up_own = exchange(up_in)
    resid = inputs + mm(mixed_b, w_out)
    normed_mlp_b = rms_norm(resid, mlp_gain).astype(BF16)
    (mlp_all,) = gather_rows([normed_mlp_b], groups, 4)
    up_own, down_w, mlp_late, grad_in = together((up_own, down_w, mlp_all, out_grad[0]))
    up_w = row_of_devices(up_own.reshape(width, part))
    (grad_all,) = gather_rows([grad_in], groups, 10)
    up_w, grad_all = together((up_w, grad_all))

    router_all = jax.nn.softmax(mm(mlp_all, w_router), axis=-1)
    picked = jnp.where(chosen, router_all, 0.0).reshape(length, sources, local_experts)
    picked = lax.dynamic_index_in_dim(picked, me // parts, 2, keepdims=True)
    gate_pre = ein("td,edf->tef", mlp_all, gate_w)
    up_pre = ein("td,edf->tef", mlp_all, up_w)
    sigma = jax.nn.sigmoid(gate_pre)
    hidden = gate_pre * sigma * up_pre
    hidden_b = (hidden * picked).astype(BF16)
    out_part = ein("tef,efd->td", hidden_b, down_w).astype(BF16)
    mixture = lax.psum_scatter(out_part, "group", scatter_dimension=0, tiled=True)
    hidden_grad = ein("td,efd->tef", grad_all, down_w)
    picked_grad = jnp.sum(hidden * hidden_grad, axis=2)
    hidden_grad = hidden_grad * picked
    gate_grad_b = (hidden_grad * up_pre * sigma * (1.0 + gate_pre * (1.0 - sigma))).astype(BF16)
    up_grad_b = (hidden_grad * gate_pre * sigma).astype(BF16)
    own_expert = jnp.arange(local_experts, dtype=jnp.int32) == me // parts
    full_part = jnp.where(own_expert[None, None, :], picked_grad[:, :, None], 0.0)
    full_part = jnp.where(chosen, full_part.reshape(length, experts), 0.0)
    full_part = full_part.T.reshape(experts, groups, rows).transpose(1, 0, 2)
    gate_w_part = ein("td,tef->edf", mlp_late, gate_grad_b).astype(BF16)
    up_w_part = ein("td,tef->edf", mlp_late, up_grad_b).astype(BF16)
    down_w_part = ein("tef,td->efd", hidden_b, grad_all).astype(BF16)
    up_w_part, down_w_part, gate_grad_b, up_grad_b = together(
        (up_w_part, down_w_part, gate_grad_b, up_grad_b)
    )

    def over_row(w):
        return lax.psum_scatter(w, "expert", scatter_dimension=0, tiled=False)

    gate_sum, up_sum, down_sum = over_row(gate_w_part), over_row(up_w_part), over_row(down_w_part)
    slot_part = ein("tef,edf->td", gate_grad_b, gate_w) + ein("tef,edf->td", up_grad_b, up_w)
    slot_part, mixture = together((slot_part.astype(BF16), mixture))
    slot_sum, router_full_grad = reduce_rows(slot_part, full_part, groups, 5)
    router_full_grad = router_full_grad.T

    def slices_out(w):
        w = w.reshape(local_experts, parts, cols, part).transpose(0, 2, 1, 3)
        return w.reshape(local_experts, cols, hidden_size).astype(F32)

    result = (resid + mixture.astype(F32)).astype(BF16)
    grad_out = out_grad[0].astype(F32)
    router = jax.nn.softmax(mm(normed_mlp_b, w_router), axis=-1)
    logits_grad_b = (
        router * (router_full_grad - jnp.sum(router * router_full_grad, axis=-1, keepdims=True))
    ).astype(BF16)
    router_w_grad = mm_tn(normed_mlp_b, logits_grad_b)
    mlp_in_grad = slot_sum + mm_nt(logits_grad_b, w_router)
    _, mlp_back = jax.vjp(rms_norm, resid, mlp_gain)
    resid_part, mlp_gain_grad = mlp_back(mlp_in_grad)
    resid_grad = grad_out + resid_part
    attn_grad_b = resid_grad.astype(BF16)
    (attn_grad_all,) = gather_rows([attn_grad_b], groups, 6)
    gate_sum, attn_grad_late = together((gate_sum, attn_grad_all))
    gate_sum = exchange(gate_sum.reshape(groups, cols, part))
    mixed_grad_c = mm_nt(attn_grad_all, own_cols(w_out, 0)).astype(BF16)
    mixed_grad_c = mixed_grad_c.reshape(length, heads, head_dim)

    prob_grad = ein("qhd,khd->hqk", mixed_grad_c, values_b)
    delta = jnp.sum(probs * prob_grad, axis=-1, keepdims=True)
    score_grad_b = (probs * (prob_grad - delta) * score_scale).astype(BF16)
    score_grad_b, probs_b = together((score_grad_b, probs_b))
    query_grad = ein("hqk,khd->qhd", score_grad_b, keys_b)
    key_grad = ein("hqk,qhd->khd", score_grad_b, queries_b)
    gate_sum, up_sum, query_grad, key_grad = together((gate_sum, up_sum, query_grad, key_grad))
    up_sum = exchange(up_sum.reshape(groups, cols, part))
    value_grad_b = ein("hqk,qhd->khd", probs_b, mixed_grad_c).astype(BF16).reshape(length, cols)

    def unturned(grad):
        return rotate(grad, cosine, -sine).reshape(length, cols)

    query_turn, key_turn = unturned(query_grad), unturned(key_grad)
    query_mix, key_mix = query_turn * query_gain_c, key_turn * key_gain_c
    dots = row_sums(query_mix * query_raw, key_mix * key_raw, 7)
    query_raw_b = (
        query_scale * query_mix - query_raw * query_scale**3 * dots[0]
    ).astype(BF16)
    key_raw_b = (key_scale * key_mix - key_raw * key_scale**3 * dots[1]).astype(BF16)
    query_gain_part = jnp.sum(query_turn * query_raw * query_scale, axis=0)
    key_gain_part = jnp.sum(key_turn * key_raw * key_scale, axis=0)
    raw_grads = [query_raw_b, key_raw_b, value_grad_b]
    (query_own, key_own, value_own), raw_grads, up_sum, down_sum = together(
        (swap(raw_grads, groups, False, 8), raw_grads, up_sum, down_sum)
    )
    down_sum = exchange(down_sum.reshape(part, groups, cols).transpose(1, 0, 2))
    out_w_part = mm_tn(mixed_c, attn_grad_late).astype(BF16)
    out_w_grad = lax.psum_scatter(out_w_part, "expert", scatter_dimension=0, tiled=True)
    qkv_part = mm_tn(normed_late, jnp.concatenate(raw_grads, axis=1)).astype(BF16)
    qkv_part = qkv_part.reshape(groups, sources, -1, 3 * cols).transpose(1, 0, 2, 3)
    qkv_part = over_row(qkv_part.reshape(sources, -1, 3 * cols)).reshape(groups, -1, 3 * cols)
    normed_grad = mm_nt(query_own, w_query) + mm_nt(key_own, w_key) + mm_nt(value_own, w_value)
    _, attn_back = jax.vjp(rms_norm, inputs, attn_gain)
    input_part, attn_gain_grad = attn_back(normed_grad)
    input_grad = resid_grad + input_part
    wide = [
        lax.dynamic_update_slice_in_dim(jnp.zeros((width,), F32), part, me * cols, 0)
        for part in (query_gain_part, key_gain_part)
    ]
    small = jnp.concatenate([router_w_grad.T, jnp.stack([mlp_gain_grad, attn_gain_grad] + wide)])
    devices = groups * sources
    small = small.reshape(-1, devices, width // devices).transpose(1, 0, 2).reshape(devices, -1)
    used = small.shape[1]
    small = jnp.pad(small, ((0, 0), (0, -used % 1024))).reshape(devices, -1, 128)
    small, qkv_part, down_sum = together((small, qkv_part, down_sum))
    qkv_part = exchange(qkv_part)
    qkv_part = qkv_part.transpose(1, 0, 2).reshape(-1, groups, 3, cols).astype(F32)
    small = small_sum(small, ("group", "expert"), True, 9).reshape(-1)[:used]
    small = small.reshape(-1, width // devices)
    return (
        result[None],
        input_grad[None],
        small[experts + 1],
        qkv_part[:, :, 0].reshape(-1, width),
        qkv_part[:, :, 1].reshape(-1, width),
        qkv_part[:, :, 2].reshape(-1, width),
        small[experts + 2],
        small[experts + 3],
        out_w_grad.astype(F32),
        small[experts],
        small[:experts].T,
        slices_out(gate_sum),
        slices_out(up_sum),
        down_sum.reshape(local_experts, hidden_size, cols).astype(F32),
    )


def solution(mesh):
    token = P("expert", "group", None)
    every = P(("group", "expert"))
    return jax.shard_map(
        shards,
        mesh=mesh,
        in_specs=(token, P("expert", "group"), token, token)
        + (P(),) * 9
        + (token, token, P("expert", None, "group")),
        out_specs=(token, token)
        + (every,) * 9
        + (token, token, P("expert", None, "group")),
        check_vma=False,
    )
```

```python
import functools
import math

import jax
import jax.numpy as jnp
from jax import lax
from jax.experimental import pallas as pl
from jax.experimental.pallas import tpu as pltpu
from jax.sharding import PartitionSpec as P

HEADS = 16
EPSILON = 1e-05
MASKED = -1000000000.0
BF16 = jnp.bfloat16
F32 = jnp.float32
MESH = pl.DeviceIdType.MESH
DMA = pltpu.SemaphoreType.DMA
VMEM_SPEC = pl.BlockSpec(memory_space=pltpu.VMEM)


def remote(src, dst, send_sem, recv_sem, where):
    return pltpu.make_async_remote_copy(
        src, dst, send_sem, recv_sem, device_id=where, device_id_type=MESH
    )


def comm_params(collective_id):
    return pltpu.CompilerParams(collective_id=collective_id, has_side_effects=True)


def greet(peers):
    barrier = pltpu.get_barrier_semaphore()
    total = 0
    for here, where in peers:

        @pl.when(here)
        def _(where=where):
            pl.semaphore_signal(barrier, inc=1, device_id=where, device_id_type=MESH)

        total = total + jnp.where(here, 1, 0)
    pl.semaphore_wait(barrier, total)


def greet_all(count, device):
    barrier = pltpu.get_barrier_semaphore()

    def body(k, carry):
        pl.semaphore_signal(barrier, inc=1, device_id=device(k), device_id_type=MESH)
        return carry

    lax.fori_loop(1, count, body, 0)
    pl.semaphore_wait(barrier, count - 1)


def gather_kernel(nz, ny, pieces, count, *refs):
    noted = len(refs) > 2 * count + 3
    ins, outs, sems = refs[: count + noted], refs[count + noted : -3 - 2 * noted], refs[-3 - 2 * noted :]
    own_sem, send_sem, recv_sem = sems[:3]
    me = lax.axis_index("group")
    z, y = me // ny, me % ny

    def at(z_to, y_to):
        return {"group": z_to * ny + y_to}

    def note_copy(k):
        to = {"group": lax.rem(me + k, nz * ny)}
        return remote(ins[count], outs[count].at[me], sems[3].at[k], sems[4].at[k], to)

    if noted:
        greet_all(nz * ny, lambda k: {"group": lax.rem(me + k, nz * ny)})
        for k in range(1, nz * ny):
            note_copy(k).start()
        outs[count][me] = ins[count][...]
    else:
        greet(
            [
                (z > 0, at(z - 1, y)),
                (z < nz - 1, at(z + 1, y)),
                (y > 0, at(z, y - 1)),
                (y < ny - 1, at(z, y + 1)),
            ]
        )
    owns = [pltpu.make_async_copy(ins[n], outs[n].at[me], own_sem.at[n]) for n in range(count)]
    for own in owns:
        own.start()

    def part(ref, c):
        rows = ref.shape[0] // pieces
        return ref.at[pl.ds(c * rows, rows)]

    def copy(slot, source, n, c, where, first):
        return remote(
            part(ins[n], c) if first else part(outs[n].at[source], c),
            part(outs[n].at[source], c),
            send_sem.at[n, slot, source, c],
            recv_sem.at[n, source, c],
            where,
        )

    def outgoing(source, go):
        sz, sy = source // ny, source % ny
        column = go & (sy == y)
        return [
            (column & (sz <= z) & (z < nz - 1), 0, at(z + 1, y)),
            (column & (sz >= z) & (z > 0), 1, at(z - 1, y)),
            (go & (sy <= y) & (y < ny - 1), 2, at(z, y + 1)),
            (go & (sy >= y) & (y > 0), 3, at(z, y - 1)),
        ]

    def act(source, n, first, go, start):
        for c in range(pieces):
            if start and not first:

                @pl.when(go)
                def _():
                    copy(0, source, n, c, at(z, y), False).wait_recv()

            for cond, slot, where in outgoing(source, go):

                @pl.when(cond)
                def _(slot=slot, where=where):
                    one = copy(slot, source, n, c, where, first)
                    if start:
                        one.start()
                    else:
                        one.wait_send()

    order = []
    for dz in range(nz):
        for sz in [z] if dz == 0 else [z - dz, z + dz]:
            for dy in range(ny):
                for sy in [y] if dy == 0 else [y - dy, y + dy]:
                    inside = (sz >= 0) & (sz < nz) & (sy >= 0) & (sy < ny)
                    source = jnp.clip(sz, 0, nz - 1) * ny + jnp.clip(sy, 0, ny - 1)
                    order.append((dz + dy, dz, source, inside))
    order = sorted(order, key=lambda t: (t[0], -t[1]))
    for start in (True, False):
        for distance, _, source, inside in order:
            for n in range(count):
                act(source, n, distance == 0, inside, start)
        if start:
            for own in owns:
                own.wait()
    if noted:
        for k in range(1, nz * ny):
            note_copy(k).wait()


def gather_rows(blocks, groups, collective_id, pieces=2, note=None):
    nz = min(4, groups)
    count = len(blocks)
    notes = [] if note is None else [note]
    outs = pl.pallas_call(
        functools.partial(gather_kernel, nz, groups // nz, pieces, count),
        name="gather_rows",
        out_shape=[jax.ShapeDtypeStruct((groups,) + a.shape, a.dtype) for a in blocks + notes],
        in_specs=[VMEM_SPEC] * (count + len(notes)),
        out_specs=[pl.BlockSpec(memory_space=pl.ANY)] * count + [VMEM_SPEC] * len(notes),
        scratch_shapes=[DMA((count,)), DMA((count, 4, groups, pieces)), DMA((count, groups, pieces))]
        + [DMA((groups,))] * 2 * len(notes),
        compiler_params=comm_params(collective_id),
        cost_estimate=pl.CostEstimate(
            flops=0, bytes_accessed=200_000_000 * count, transcendentals=0
        ),
    )(*blocks, *notes)
    rows = [a.reshape(groups * b.shape[0], b.shape[1]) for a, b in zip(outs, blocks)]
    return rows + list(outs[count:])


def reduce_kernel(
    nz, ny, pieces, parts, note, out, note_out, ybuf, zbuf, landed, ysend, yrecv, zsend, zrecv, nsend, nrecv
):
    me = lax.axis_index("group")
    z, y = me // ny, me % ny
    rows = parts.shape[1] // pieces

    def at(z_to, y_to):
        return {"group": z_to * ny + y_to}

    def note_copy(k):
        to = lax.rem(me + k, nz * ny)
        return remote(note.at[to], landed.at[k], nsend.at[k], nrecv.at[k], {"group": to})

    greet_all(nz * ny, lambda k: {"group": lax.rem(me + k, nz * ny)})
    for k in range(1, nz * ny):
        note_copy(k).start()
    landed[0] = note[me]

    def part(ref, c):
        return ref.at[pl.ds(c * rows, rows)]

    def y_copy(dest, c):
        src, dst = part(parts.at[dest * ny + 1 - y], c), part(ybuf.at[dest], c)
        return remote(src, dst, ysend.at[dest, c], yrecv.at[dest, c], at(z, 1 - y))

    def z_copy(side, dest, c):
        src, dst = part(ybuf.at[dest], c), part(zbuf.at[side, dest], c)
        where = at(z - 1, y) if side else at(z + 1, y)
        return remote(src, dst, zsend.at[dest, c], zrecv.at[side, dest, c], where)

    order = []
    for d in range(nz - 1, 0, -1):
        order += [(z + d, z + d < nz, 0), (z - d, z - d >= 0, 1)]
    order = [(jnp.clip(dest, 0, nz - 1), inside, side) for dest, inside, side in order]
    for dest, inside, side in order:

        @pl.when(inside)
        def _():
            for c in range(pieces):
                y_copy(dest, c).start()

    for c in range(pieces):
        y_copy(z, c).start()
    for dest, inside, side in order:
        further = (z < nz - 1) if side else (z > 0)
        for c in range(pieces):
            span = pl.ds(c * rows, rows)

            @pl.when(inside)
            def _():
                y_copy(dest, c).wait_recv()
                pair = parts[dest * ny + y, span, :].astype(F32) + ybuf[dest, span, :].astype(F32)

                @pl.when(further)
                def _():
                    z_copy(side, dest, c).wait_recv()
                    ybuf[dest, span, :] = (pair + zbuf[side, dest, span, :].astype(F32)).astype(BF16)

                @pl.when(jnp.logical_not(further))
                def _():
                    ybuf[dest, span, :] = pair.astype(BF16)

                z_copy(side, dest, c).start()

    for c in range(pieces):
        span = pl.ds(c * rows, rows)
        y_copy(z, c).wait_recv()
        out[span, :] = parts[me, span, :].astype(F32) + ybuf[z, span, :].astype(F32)

        @pl.when(z > 0)
        def _():
            z_copy(0, z, c).wait_recv()
            out[span, :] += zbuf[0, z, span, :].astype(F32)

        @pl.when(z < nz - 1)
        def _():
            z_copy(1, z, c).wait_recv()
            out[span, :] += zbuf[1, z, span, :].astype(F32)

    for dest, inside, side in order:

        @pl.when(inside)
        def _():
            for c in range(pieces):
                y_copy(dest, c).wait_send()
                z_copy(side, dest, c).wait_send()

    for c in range(pieces):
        y_copy(z, c).wait_send()
    for k in range(1, nz * ny):
        note_copy(k).wait()
    note_out[...] = jnp.sum(landed[...], axis=0)


def reduce_rows(parts, note, groups, collective_id, pieces=2):
    nz = min(4, groups)
    ny = groups // nz
    if ny != 2:
        total = lax.psum_scatter(parts, "group", scatter_dimension=0, tiled=True).astype(F32)
        return total, lax.psum_scatter(note, "group", scatter_dimension=0, tiled=False)
    rows, width = parts.shape[0] // groups, parts.shape[1]
    return pl.pallas_call(
        functools.partial(reduce_kernel, nz, ny, pieces),
        name="reduce_rows",
        out_shape=[
            jax.ShapeDtypeStruct((rows, width), F32),
            jax.ShapeDtypeStruct(note.shape[1:], F32),
        ],
        in_specs=[VMEM_SPEC] * 2,
        out_specs=[VMEM_SPEC] * 2,
        scratch_shapes=[
            pltpu.VMEM((nz, rows, width), BF16),
            pltpu.VMEM((2, nz, rows, width), BF16),
            pltpu.VMEM(note.shape, F32),
            DMA((nz, pieces)),
            DMA((nz, pieces)),
            DMA((nz, pieces)),
            DMA((2, nz, pieces)),
            DMA((groups,)),
            DMA((groups,)),
        ],
        compiler_params=comm_params(collective_id),
        cost_estimate=pl.CostEstimate(flops=0, bytes_accessed=200_000_000, transcendentals=0),
    )(parts.reshape(groups, rows, width), note)


def swap_kernel(groups, to_rows, *refs):
    count = (len(refs) - 2) // 2
    ins, outs, (send_sem, recv_sem) = refs[:count], refs[count : 2 * count], refs[2 * count :]
    me = lax.axis_index("group")
    columns = ins[0].shape[-1] // (groups if to_rows else 1)
    wide = lambda ref, i: ref.at[:, pl.ds(pl.multiple_of(i * columns, columns), columns)]
    thin = lambda ref, i: ref.at[i]
    source, target = (wide, thin) if to_rows else (thin, wide)

    def peer(k):
        return lax.rem(me + k, groups)

    greet_all(groups, lambda k: {"group": peer(k)})

    def copy(n, k):
        to = peer(k)
        return remote(
            source(ins[n], to), target(outs[n], me), send_sem.at[n, k], recv_sem.at[n, k], {"group": to}
        )

    for k in range(1, groups):
        for n in range(count):
            copy(n, k).start()
    for n in range(count):
        if to_rows:
            outs[n][me] = ins[n][:, pl.ds(pl.multiple_of(me * columns, columns), columns)]
        else:
            outs[n][:, pl.ds(pl.multiple_of(me * columns, columns), columns)] = ins[n][me]
    for k in range(1, groups):
        for n in range(count):
            copy(n, k).wait()


def swap(arrays, groups, to_rows, collective_id):
    shape, count = arrays[0].shape, len(arrays)
    if to_rows:
        rows, columns = shape[0], shape[1] // groups
        out = (groups, rows, columns)
    else:
        rows, columns = shape[0] // groups, shape[1]
        arrays = [a.reshape(groups, rows, columns) for a in arrays]
        out = (rows, groups * columns)
    outs = pl.pallas_call(
        functools.partial(swap_kernel, groups, to_rows),
        name="swap",
        out_shape=[jax.ShapeDtypeStruct(out, a.dtype) for a in arrays],
        in_specs=[VMEM_SPEC] * count,
        out_specs=[VMEM_SPEC] * count,
        scratch_shapes=[DMA((count, groups)), DMA((count, groups))],
        compiler_params=comm_params(collective_id),
        cost_estimate=pl.CostEstimate(flops=0, bytes_accessed=30_000_000, transcendentals=0),
    )(*arrays)
    return [o.reshape(groups * rows, columns) if to_rows else o for o in outs]


def small_sum_kernel(axes, scatter, values, out, landed, send_sem, recv_sem):
    sizes = [lax.axis_size(a) for a in axes]
    count = math.prod(sizes)
    me = 0
    for a, n in zip(axes, sizes):
        me = me * n + lax.axis_index(a)

    def peer(k):
        return lax.rem(me + k, count)

    def device(k):
        to = peer(k)
        if len(axes) == 1:
            return {axes[0]: to}
        return {axes[0]: to // sizes[1], axes[1]: lax.rem(to, sizes[1])}

    greet_all(count, device)

    def copy(k):
        src = values.at[peer(k)] if scatter else values
        return remote(src, landed.at[k], send_sem.at[k], recv_sem.at[k], device(k))

    def start(k, carry):
        copy(k).start()
        return carry

    def wait(k, carry):
        copy(k).wait()
        return carry

    lax.fori_loop(1, count, start, 0)
    landed[0] = values[me] if scatter else values[...]
    lax.fori_loop(1, count, wait, 0)
    out[...] = jnp.sum(landed[...], axis=0)


def small_sum(values, axes, scatter, collective_id):
    count = math.prod(lax.axis_size(a) for a in axes)
    shape = values.shape[-2:]
    return pl.pallas_call(
        functools.partial(small_sum_kernel, axes, scatter),
        name="small_sum",
        out_shape=jax.ShapeDtypeStruct(shape, F32),
        in_specs=[VMEM_SPEC],
        out_specs=VMEM_SPEC,
        scratch_shapes=[pltpu.VMEM((count,) + shape, F32), DMA((count,)), DMA((count,))],
        compiler_params=comm_params(collective_id),
        cost_estimate=pl.CostEstimate(flops=0, bytes_accessed=10_000_000, transcendentals=0),
    )(values)


def rms_norm(values_in, gain_vec):
    return (
        values_in
        * lax.rsqrt(jnp.mean(values_in * values_in, axis=-1, keepdims=True) + EPSILON)
        * gain_vec
    )


def angles(row_count, head_dim):
    places = jnp.arange(row_count, dtype=jnp.int32).astype(F32)
    frequency = jnp.exp(-math.log(10000.0) * 2.0 * jnp.arange(head_dim // 2, dtype=F32) / head_dim)
    turn_angle = places[:, None] * frequency[None, :]
    return (jnp.cos(turn_angle)[:, None, :], jnp.sin(turn_angle)[:, None, :])


def rotate(values_in, cosine, sine):
    half_dim = values_in.shape[-1] // 2
    first_half = values_in[..., :half_dim]
    second = values_in[..., half_dim:]
    return jnp.concatenate(
        [first_half * cosine - second * sine, second * cosine + first_half * sine], axis=-1
    )


def mm(left, right):
    return jnp.dot(left, right, preferred_element_type=F32)


def mm_tn(left, right):
    return lax.dot_general(left, right, (((0,), (0,)), ((), ())), preferred_element_type=F32)


def mm_nt(left, right):
    return lax.dot_general(left, right, (((1,), (1,)), ((), ())), preferred_element_type=F32)


def ein(spec, *ops):
    return jnp.einsum(spec, *ops, preferred_element_type=F32)


def shards(
    layer_in,
    segment_ids,
    routing,
    out_grad,
    attn_gain,
    w_query,
    w_key,
    w_value,
    query_gain,
    key_gain,
    w_out,
    mlp_gain,
    w_router,
    w_gate,
    w_up,
    w_down,
):
    groups = lax.axis_size("group")
    sources = lax.axis_size("expert")
    me = lax.axis_index("group")
    rows = layer_in.shape[1]
    width = layer_in.shape[2]
    length = rows * groups
    head_dim = width // HEADS
    heads = HEADS // groups
    cols = width // groups
    local_experts = w_gate.shape[0]
    experts = local_experts * sources
    hidden_size = w_gate.shape[2]
    parts = groups // local_experts
    part = hidden_size // parts
    score_scale = 1.0 / math.sqrt(head_dim)

    def own_cols(matrix, axis):
        return lax.dynamic_slice_in_dim(matrix, me * cols, cols, axis)

    def slices(w):
        w = w.reshape(local_experts, w.shape[1], parts, part).transpose(0, 2, 1, 3)
        return w.reshape(groups, w.shape[2], part)

    def exchange(w):
        return lax.all_to_all(w, "group", 0, 0, tiled=True)

    def row_of_devices(w):
        return lax.all_gather(w, "expert", axis=0, tiled=False)

    together = lax.optimization_barrier
    gate_own = exchange(slices(w_gate))

    inputs = layer_in[0].astype(F32)
    normed_b = rms_norm(inputs, attn_gain).astype(BF16)
    expert_ids = jnp.arange(experts, dtype=jnp.int32)
    marks = jnp.any(routing[0][:, :, None] == expert_ids[None, None, :], axis=1).astype(F32)
    own_scales = [
        lax.rsqrt(jnp.mean(jnp.square(mm(normed_b, w)), axis=1) + EPSILON)[None] for w in (w_query, w_key)
    ]
    marks = jnp.concatenate([marks.T, segment_ids[0].astype(F32)[None]] + own_scales, axis=0)
    normed_all, marks = gather_rows([normed_b], groups, 1, note=marks)
    marks = marks.transpose(1, 0, 2).reshape(experts + 3, length)
    chosen, seg_all = marks[:experts].T > 0.5, marks[experts]
    down_in = w_down.reshape(groups, part, cols)
    gate_own, down_in, normed_late = together((gate_own, down_in, normed_all))
    gate_w = row_of_devices(gate_own.reshape(width, part))
    down_own = exchange(down_in)
    wq, wk, wv = own_cols(w_query, 1), own_cols(w_key, 1), own_cols(w_value, 1)
    query_raw, key_raw = mm(normed_all, wq), mm(normed_all, wk)
    values_b = mm(normed_all, wv).astype(BF16).reshape(length, heads, head_dim)

    def row_sums(first, second, collective_id):
        sums = jnp.stack([jnp.sum(first, axis=1), jnp.sum(second, axis=1)])
        sums = small_sum(sums.reshape(-1, 128), ("group",), False, collective_id)
        return sums.reshape(2, length, 1) / width

    query_scale, key_scale = marks[experts + 1][:, None], marks[experts + 2][:, None]
    query_gain_c, key_gain_c = own_cols(query_gain, 0), own_cols(key_gain, 0)
    cosine, sine = angles(length, head_dim)

    def turned(raw, scale, gain):
        return rotate((raw * scale * gain).reshape(length, heads, head_dim), cosine, sine)

    queries_b = turned(query_raw, query_scale, query_gain_c).astype(BF16)
    keys_b = turned(key_raw, key_scale, key_gain_c).astype(BF16)
    place = jnp.arange(length, dtype=jnp.int32)
    allowed = (seg_all[:, None] == seg_all[None, :]) & (place[None, :] <= place[:, None])
    scores = jnp.where(allowed[None], ein("qhd,khd->hqk", queries_b, keys_b) * score_scale, MASKED)
    top_score = jnp.max(scores, axis=-1, keepdims=True)
    log_total = top_score + jnp.log(jnp.sum(jnp.exp(scores - top_score), axis=-1, keepdims=True))
    probs = jnp.exp(scores - log_total)
    probs_b = probs.astype(BF16)
    mixed_c = ein("hqk,khd->qhd", probs_b, values_b).reshape(length, cols).astype(BF16)
    down_own, gate_w, mixed_in = together((down_own, gate_w, mixed_c))
    (mixed_b,) = swap([mixed_in], groups, False, 3)
    up_in, down_own, mixed_b = together((slices(w_up), down_own, mixed_b))
    down_w = row_of_devices(down_own.transpose(1, 0, 2).reshape(part, width))
    up_own = exchange(up_in)
    resid = inputs + mm(mixed_b, w_out)
    normed_mlp_b = rms_norm(resid, mlp_gain).astype(BF16)
    (mlp_all,) = gather_rows([normed_mlp_b], groups, 4)
    up_own, down_w, mlp_late, grad_in = together((up_own, down_w, mlp_all, out_grad[0]))
    up_w = row_of_devices(up_own.reshape(width, part))
    (grad_all,) = gather_rows([grad_in], groups, 10)
    up_w, grad_all = together((up_w, grad_all))

    router_all = jax.nn.softmax(mm(mlp_all, w_router), axis=-1)
    picked = jnp.where(chosen, router_all, 0.0).reshape(length, sources, local_experts)
    picked = lax.dynamic_index_in_dim(picked, me // parts, 2, keepdims=True)
    gate_pre = ein("td,edf->tef", mlp_all, gate_w)
    up_pre = ein("td,edf->tef", mlp_all, up_w)
    sigma = jax.nn.sigmoid(gate_pre)
    hidden = gate_pre * sigma * up_pre
    hidden_b = (hidden * picked).astype(BF16)
    out_part = ein("tef,efd->td", hidden_b, down_w).astype(BF16)
    out_part, grad_all = together((out_part, grad_all))
    mixture = lax.psum_scatter(out_part, "group", scatter_dimension=0, tiled=True)
    hidden_grad = ein("td,efd->tef", grad_all, down_w)
    picked_grad = jnp.sum(hidden * hidden_grad, axis=2)
    hidden_grad = hidden_grad * picked
    gate_grad_b = (hidden_grad * up_pre * sigma * (1.0 + gate_pre * (1.0 - sigma))).astype(BF16)
    up_grad_b = (hidden_grad * gate_pre * sigma).astype(BF16)
    own_expert = jnp.arange(local_experts, dtype=jnp.int32) == me // parts
    full_part = jnp.where(own_expert[None, None, :], picked_grad[:, :, None], 0.0)
    full_part = jnp.where(chosen, full_part.reshape(length, experts), 0.0)
    full_part = full_part.T.reshape(experts, groups, rows).transpose(1, 0, 2)
    gate_w_part = ein("td,tef->edf", mlp_late, gate_grad_b).astype(BF16)
    up_w_part = ein("td,tef->edf", mlp_late, up_grad_b).astype(BF16)
    up_w_part, gate_grad_b, up_grad_b = together((up_w_part, gate_grad_b, up_grad_b))

    def over_row(w):
        return lax.psum_scatter(w, "expert", scatter_dimension=0, tiled=False)

    gate_sum, up_sum = over_row(gate_w_part), over_row(up_w_part)
    slot_part = ein("tef,edf->td", gate_grad_b, gate_w) + ein("tef,edf->td", up_grad_b, up_w)
    slot_part, mixture = together((slot_part.astype(BF16), mixture))
    slot_sum, router_full_grad = reduce_rows(slot_part, full_part, groups, 5)
    router_full_grad = router_full_grad.T

    def slices_out(w):
        w = w.reshape(local_experts, parts, cols, part).transpose(0, 2, 1, 3)
        return w.reshape(local_experts, cols, hidden_size).astype(F32)

    result = (resid + mixture.astype(F32)).astype(BF16)
    grad_out = out_grad[0].astype(F32)
    router = jax.nn.softmax(mm(normed_mlp_b, w_router), axis=-1)
    logits_grad_b = (
        router * (router_full_grad - jnp.sum(router * router_full_grad, axis=-1, keepdims=True))
    ).astype(BF16)
    router_w_grad = mm_tn(normed_mlp_b, logits_grad_b)
    mlp_in_grad = slot_sum + mm_nt(logits_grad_b, w_router)
    _, mlp_back = jax.vjp(rms_norm, resid, mlp_gain)
    resid_part, mlp_gain_grad = mlp_back(mlp_in_grad)
    resid_grad = grad_out + resid_part
    attn_grad_b = resid_grad.astype(BF16)
    (attn_grad_all,) = gather_rows([attn_grad_b], groups, 6)
    gate_sum, attn_grad_late = together((gate_sum, attn_grad_all))
    gate_sum = exchange(gate_sum.reshape(groups, cols, part))
    mixed_grad_c = mm_nt(attn_grad_late, own_cols(w_out, 0)).astype(BF16)
    mixed_grad_c = mixed_grad_c.reshape(length, heads, head_dim)

    prob_grad = ein("qhd,khd->hqk", mixed_grad_c, values_b)
    delta = jnp.sum(probs * prob_grad, axis=-1, keepdims=True)
    score_grad_b = (probs * (prob_grad - delta) * score_scale).astype(BF16)
    score_grad_b, probs_b = together((score_grad_b, probs_b))
    query_grad = ein("hqk,khd->qhd", score_grad_b, keys_b)
    key_grad = ein("hqk,qhd->khd", score_grad_b, queries_b)
    query_grad, key_grad, hidden_b = together((query_grad, key_grad, hidden_b))
    down_w_part = ein("tef,td->efd", hidden_b, grad_all).astype(BF16)
    gate_sum, up_sum, query_grad, key_grad, probs_b, down_w_part = together(
        (gate_sum, up_sum, query_grad, key_grad, probs_b, down_w_part)
    )
    down_sum = over_row(down_w_part)
    up_sum = exchange(up_sum.reshape(groups, cols, part))
    value_grad_b = ein("hqk,qhd->khd", probs_b, mixed_grad_c).astype(BF16).reshape(length, cols)

    def unturned(grad):
        return rotate(grad, cosine, -sine).reshape(length, cols)

    query_turn, key_turn = unturned(query_grad), unturned(key_grad)
    query_mix, key_mix = query_turn * query_gain_c, key_turn * key_gain_c
    dots = row_sums(query_mix * query_raw, key_mix * key_raw, 7)
    query_raw_b = (
        query_scale * query_mix - query_raw * query_scale**3 * dots[0]
    ).astype(BF16)
    key_raw_b = (key_scale * key_mix - key_raw * key_scale**3 * dots[1]).astype(BF16)
    query_gain_part = jnp.sum(query_turn * query_raw * query_scale, axis=0)
    key_gain_part = jnp.sum(key_turn * key_raw * key_scale, axis=0)
    raw_grads = [query_raw_b, key_raw_b, value_grad_b]
    down_sum = down_sum.reshape(part, groups, cols).transpose(1, 0, 2)
    (query_own, key_own, value_own), raw_grads, up_sum, down_sum = together(
        (swap(raw_grads, groups, False, 8), raw_grads, up_sum, down_sum)
    )
    down_sum = exchange(down_sum)
    out_w_part = mm_tn(mixed_c, attn_grad_late).astype(BF16)
    out_w_grad = lax.psum_scatter(out_w_part, "expert", scatter_dimension=0, tiled=True)
    qkv_part = mm_tn(normed_late, jnp.concatenate(raw_grads, axis=1)).astype(BF16)
    qkv_part = qkv_part.reshape(groups, sources, -1, 3 * cols).transpose(1, 0, 2, 3)
    qkv_part = over_row(qkv_part.reshape(sources, -1, 3 * cols)).reshape(groups, -1, 3 * cols)
    normed_grad = mm_nt(query_own, w_query) + mm_nt(key_own, w_key) + mm_nt(value_own, w_value)
    _, attn_back = jax.vjp(rms_norm, inputs, attn_gain)
    input_part, attn_gain_grad = attn_back(normed_grad)
    input_grad = resid_grad + input_part
    wide = [
        lax.dynamic_update_slice_in_dim(jnp.zeros((width,), F32), part, me * cols, 0)
        for part in (query_gain_part, key_gain_part)
    ]
    small = jnp.concatenate([router_w_grad.T, jnp.stack([mlp_gain_grad, attn_gain_grad] + wide)])
    devices = groups * sources
    small = small.reshape(-1, devices, width // devices).transpose(1, 0, 2).reshape(devices, -1)
    used = small.shape[1]
    small = jnp.pad(small, ((0, 0), (0, -used % 1024))).reshape(devices, -1, 128)
    small, qkv_part, down_sum = together((small, qkv_part, down_sum))
    qkv_part = exchange(qkv_part)
    qkv_part = qkv_part.transpose(1, 0, 2).reshape(-1, groups, 3, cols).astype(F32)
    small = small_sum(small, ("group", "expert"), True, 9).reshape(-1)[:used]
    small = small.reshape(-1, width // devices)
    return (
        result[None],
        input_grad[None],
        small[experts + 1],
        qkv_part[:, :, 0].reshape(-1, width),
        qkv_part[:, :, 1].reshape(-1, width),
        qkv_part[:, :, 2].reshape(-1, width),
        small[experts + 2],
        small[experts + 3],
        out_w_grad.astype(F32),
        small[experts],
        small[:experts].T,
        slices_out(gate_sum),
        slices_out(up_sum),
        down_sum.reshape(local_experts, hidden_size, cols).astype(F32),
    )


def solution(mesh):
    token = P("expert", "group", None)
    every = P(("group", "expert"))
    return jax.shard_map(
        shards,
        mesh=mesh,
        in_specs=(token, P("expert", "group"), token, token)
        + (P(),) * 9
        + (token, token, P("expert", None, "group")),
        out_specs=(token, token)
        + (every,) * 9
        + (token, token, P("expert", None, "group")),
        check_vma=False,
    )
```

```python
import functools
import math

import jax
import jax.numpy as jnp
from jax import lax
from jax.experimental import pallas as pl
from jax.experimental.pallas import tpu as pltpu
from jax.sharding import PartitionSpec as P

HEADS = 16
EPSILON = 1e-05
MASKED = -1000000000.0
BF16 = jnp.bfloat16
F32 = jnp.float32
MESH = pl.DeviceIdType.MESH
DMA = pltpu.SemaphoreType.DMA
VMEM_SPEC = pl.BlockSpec(memory_space=pltpu.VMEM)


def remote(src, dst, send_sem, recv_sem, where):
    return pltpu.make_async_remote_copy(
        src, dst, send_sem, recv_sem, device_id=where, device_id_type=MESH
    )


def comm_params(collective_id):
    return pltpu.CompilerParams(collective_id=collective_id, has_side_effects=True)


def greet(peers):
    barrier = pltpu.get_barrier_semaphore()
    total = 0
    for here, where in peers:

        @pl.when(here)
        def _(where=where):
            pl.semaphore_signal(barrier, inc=1, device_id=where, device_id_type=MESH)

        total = total + jnp.where(here, 1, 0)
    pl.semaphore_wait(barrier, total)


def greet_all(count, device):
    barrier = pltpu.get_barrier_semaphore()

    def body(k, carry):
        pl.semaphore_signal(barrier, inc=1, device_id=device(k), device_id_type=MESH)
        return carry

    lax.fori_loop(1, count, body, 0)
    pl.semaphore_wait(barrier, count - 1)


def gather_kernel(nz, ny, pieces, count, *refs):
    noted = len(refs) > 2 * count + 3
    ins, outs, sems = refs[: count + noted], refs[count + noted : -3 - 2 * noted], refs[-3 - 2 * noted :]
    own_sem, send_sem, recv_sem = sems[:3]
    me = lax.axis_index("group")
    z, y = me // ny, me % ny

    def at(z_to, y_to):
        return {"group": z_to * ny + y_to}

    def note_copy(k):
        to = {"group": lax.rem(me + k, nz * ny)}
        return remote(ins[count], outs[count].at[me], sems[3].at[k], sems[4].at[k], to)

    if noted:
        greet_all(nz * ny, lambda k: {"group": lax.rem(me + k, nz * ny)})
        for k in range(1, nz * ny):
            note_copy(k).start()
        outs[count][me] = ins[count][...]
    else:
        greet(
            [
                (z > 0, at(z - 1, y)),
                (z < nz - 1, at(z + 1, y)),
                (y > 0, at(z, y - 1)),
                (y < ny - 1, at(z, y + 1)),
            ]
        )
    owns = [pltpu.make_async_copy(ins[n], outs[n].at[me], own_sem.at[n]) for n in range(count)]
    for own in owns:
        own.start()

    def part(ref, c):
        rows = ref.shape[0] // pieces
        return ref.at[pl.ds(c * rows, rows)]

    def copy(slot, source, n, c, where, first):
        return remote(
            part(ins[n], c) if first else part(outs[n].at[source], c),
            part(outs[n].at[source], c),
            send_sem.at[n, slot, source, c],
            recv_sem.at[n, source, c],
            where,
        )

    def outgoing(source, go):
        sz, sy = source // ny, source % ny
        column = go & (sy == y)
        return [
            (column & (sz <= z) & (z < nz - 1), 0, at(z + 1, y)),
            (column & (sz >= z) & (z > 0), 1, at(z - 1, y)),
            (go & (sy <= y) & (y < ny - 1), 2, at(z, y + 1)),
            (go & (sy >= y) & (y > 0), 3, at(z, y - 1)),
        ]

    def act(source, n, first, go, start):
        for c in range(pieces):
            if start and not first:

                @pl.when(go)
                def _():
                    copy(0, source, n, c, at(z, y), False).wait_recv()

            for cond, slot, where in outgoing(source, go):

                @pl.when(cond)
                def _(slot=slot, where=where):
                    one = copy(slot, source, n, c, where, first)
                    if start:
                        one.start()
                    else:
                        one.wait_send()

    order = []
    for dz in range(nz):
        for sz in [z] if dz == 0 else [z - dz, z + dz]:
            for dy in range(ny):
                for sy in [y] if dy == 0 else [y - dy, y + dy]:
                    inside = (sz >= 0) & (sz < nz) & (sy >= 0) & (sy < ny)
                    source = jnp.clip(sz, 0, nz - 1) * ny + jnp.clip(sy, 0, ny - 1)
                    order.append((dz + dy, dz, source, inside))
    order = sorted(order, key=lambda t: (t[0], -t[1]))
    for start in (True, False):
        for distance, _, source, inside in order:
            for n in range(count):
                act(source, n, distance == 0, inside, start)
        if start:
            for own in owns:
                own.wait()
    if noted:
        for k in range(1, nz * ny):
            note_copy(k).wait()


def gather_rows(blocks, groups, collective_id, pieces=2, note=None):
    nz = min(4, groups)
    count = len(blocks)
    notes = [] if note is None else [note]
    outs = pl.pallas_call(
        functools.partial(gather_kernel, nz, groups // nz, pieces, count),
        name="gather_rows",
        out_shape=[jax.ShapeDtypeStruct((groups,) + a.shape, a.dtype) for a in blocks + notes],
        in_specs=[VMEM_SPEC] * (count + len(notes)),
        out_specs=[pl.BlockSpec(memory_space=pl.ANY)] * count + [VMEM_SPEC] * len(notes),
        scratch_shapes=[DMA((count,)), DMA((count, 4, groups, pieces)), DMA((count, groups, pieces))]
        + [DMA((groups,))] * 2 * len(notes),
        compiler_params=comm_params(collective_id),
        cost_estimate=pl.CostEstimate(
            flops=0, bytes_accessed=200_000_000 * count, transcendentals=0
        ),
    )(*blocks, *notes)
    rows = [a.reshape(groups * b.shape[0], b.shape[1]) for a, b in zip(outs, blocks)]
    return rows + list(outs[count:])


def reduce_kernel(
    nz, ny, pieces, parts, note, out, note_out, ybuf, zbuf, landed, ysend, yrecv, zsend, zrecv, nsend, nrecv
):
    me = lax.axis_index("group")
    z, y = me // ny, me % ny
    rows = parts.shape[1] // pieces

    def at(z_to, y_to):
        return {"group": z_to * ny + y_to}

    def note_copy(k):
        to = lax.rem(me + k, nz * ny)
        return remote(note.at[to], landed.at[k], nsend.at[k], nrecv.at[k], {"group": to})

    greet_all(nz * ny, lambda k: {"group": lax.rem(me + k, nz * ny)})
    for k in range(1, nz * ny):
        note_copy(k).start()
    landed[0] = note[me]

    def part(ref, c):
        return ref.at[pl.ds(c * rows, rows)]

    def y_copy(dest, c):
        src, dst = part(parts.at[dest * ny + 1 - y], c), part(ybuf.at[dest], c)
        return remote(src, dst, ysend.at[dest, c], yrecv.at[dest, c], at(z, 1 - y))

    def z_copy(side, dest, c):
        src, dst = part(ybuf.at[dest], c), part(zbuf.at[side, dest], c)
        where = at(z - 1, y) if side else at(z + 1, y)
        return remote(src, dst, zsend.at[dest, c], zrecv.at[side, dest, c], where)

    order = []
    for d in range(nz - 1, 0, -1):
        order += [(z + d, z + d < nz, 0), (z - d, z - d >= 0, 1)]
    order = [(jnp.clip(dest, 0, nz - 1), inside, side) for dest, inside, side in order]
    for dest, inside, side in order:

        @pl.when(inside)
        def _():
            for c in range(pieces):
                y_copy(dest, c).start()

    for c in range(pieces):
        y_copy(z, c).start()
    for dest, inside, side in order:
        further = (z < nz - 1) if side else (z > 0)
        for c in range(pieces):
            span = pl.ds(c * rows, rows)

            @pl.when(inside)
            def _():
                y_copy(dest, c).wait_recv()
                pair = parts[dest * ny + y, span, :].astype(F32) + ybuf[dest, span, :].astype(F32)

                @pl.when(further)
                def _():
                    z_copy(side, dest, c).wait_recv()
                    ybuf[dest, span, :] = (pair + zbuf[side, dest, span, :].astype(F32)).astype(BF16)

                @pl.when(jnp.logical_not(further))
                def _():
                    ybuf[dest, span, :] = pair.astype(BF16)

                z_copy(side, dest, c).start()

    for c in range(pieces):
        span = pl.ds(c * rows, rows)
        y_copy(z, c).wait_recv()
        out[span, :] = parts[me, span, :].astype(F32) + ybuf[z, span, :].astype(F32)

        @pl.when(z > 0)
        def _():
            z_copy(0, z, c).wait_recv()
            out[span, :] += zbuf[0, z, span, :].astype(F32)

        @pl.when(z < nz - 1)
        def _():
            z_copy(1, z, c).wait_recv()
            out[span, :] += zbuf[1, z, span, :].astype(F32)

    for dest, inside, side in order:

        @pl.when(inside)
        def _():
            for c in range(pieces):
                y_copy(dest, c).wait_send()
                z_copy(side, dest, c).wait_send()

    for c in range(pieces):
        y_copy(z, c).wait_send()
    for k in range(1, nz * ny):
        note_copy(k).wait()
    note_out[...] = jnp.sum(landed[...], axis=0)


def reduce_rows(parts, note, groups, collective_id, pieces=2):
    nz = min(4, groups)
    ny = groups // nz
    if ny != 2:
        total = lax.psum_scatter(parts, "group", scatter_dimension=0, tiled=True).astype(F32)
        return total, lax.psum_scatter(note, "group", scatter_dimension=0, tiled=False)
    rows, width = parts.shape[0] // groups, parts.shape[1]
    return pl.pallas_call(
        functools.partial(reduce_kernel, nz, ny, pieces),
        name="reduce_rows",
        out_shape=[
            jax.ShapeDtypeStruct((rows, width), F32),
            jax.ShapeDtypeStruct(note.shape[1:], F32),
        ],
        in_specs=[VMEM_SPEC] * 2,
        out_specs=[VMEM_SPEC] * 2,
        scratch_shapes=[
            pltpu.VMEM((nz, rows, width), BF16),
            pltpu.VMEM((2, nz, rows, width), BF16),
            pltpu.VMEM(note.shape, F32),
            DMA((nz, pieces)),
            DMA((nz, pieces)),
            DMA((nz, pieces)),
            DMA((2, nz, pieces)),
            DMA((groups,)),
            DMA((groups,)),
        ],
        compiler_params=comm_params(collective_id),
        cost_estimate=pl.CostEstimate(flops=0, bytes_accessed=200_000_000, transcendentals=0),
    )(parts.reshape(groups, rows, width), note)


def swap_kernel(groups, to_rows, *refs):
    count = (len(refs) - 2) // 2
    ins, outs, (send_sem, recv_sem) = refs[:count], refs[count : 2 * count], refs[2 * count :]
    me = lax.axis_index("group")
    columns = ins[0].shape[-1] // (groups if to_rows else 1)
    wide = lambda ref, i: ref.at[:, pl.ds(pl.multiple_of(i * columns, columns), columns)]
    thin = lambda ref, i: ref.at[i]
    source, target = (wide, thin) if to_rows else (thin, wide)

    def peer(k):
        return lax.rem(me + k, groups)

    greet_all(groups, lambda k: {"group": peer(k)})

    def copy(n, k):
        to = peer(k)
        return remote(
            source(ins[n], to), target(outs[n], me), send_sem.at[n, k], recv_sem.at[n, k], {"group": to}
        )

    for k in range(1, groups):
        for n in range(count):
            copy(n, k).start()
    for n in range(count):
        if to_rows:
            outs[n][me] = ins[n][:, pl.ds(pl.multiple_of(me * columns, columns), columns)]
        else:
            outs[n][:, pl.ds(pl.multiple_of(me * columns, columns), columns)] = ins[n][me]
    for k in range(1, groups):
        for n in range(count):
            copy(n, k).wait()


def swap(arrays, groups, to_rows, collective_id):
    shape, count = arrays[0].shape, len(arrays)
    if to_rows:
        rows, columns = shape[0], shape[1] // groups
        out = (groups, rows, columns)
    else:
        rows, columns = shape[0] // groups, shape[1]
        arrays = [a.reshape(groups, rows, columns) for a in arrays]
        out = (rows, groups * columns)
    outs = pl.pallas_call(
        functools.partial(swap_kernel, groups, to_rows),
        name="swap",
        out_shape=[jax.ShapeDtypeStruct(out, a.dtype) for a in arrays],
        in_specs=[VMEM_SPEC] * count,
        out_specs=[VMEM_SPEC] * count,
        scratch_shapes=[DMA((count, groups)), DMA((count, groups))],
        compiler_params=comm_params(collective_id),
        cost_estimate=pl.CostEstimate(flops=0, bytes_accessed=30_000_000, transcendentals=0),
    )(*arrays)
    return [o.reshape(groups * rows, columns) if to_rows else o for o in outs]


def small_sum_kernel(axes, scatter, values, out, landed, send_sem, recv_sem):
    sizes = [lax.axis_size(a) for a in axes]
    count = math.prod(sizes)
    me = 0
    for a, n in zip(axes, sizes):
        me = me * n + lax.axis_index(a)

    def peer(k):
        return lax.rem(me + k, count)

    def device(k):
        to = peer(k)
        if len(axes) == 1:
            return {axes[0]: to}
        return {axes[0]: to // sizes[1], axes[1]: lax.rem(to, sizes[1])}

    greet_all(count, device)

    def copy(k):
        src = values.at[peer(k)] if scatter else values
        return remote(src, landed.at[k], send_sem.at[k], recv_sem.at[k], device(k))

    def start(k, carry):
        copy(k).start()
        return carry

    def wait(k, carry):
        copy(k).wait()
        return carry

    lax.fori_loop(1, count, start, 0)
    landed[0] = values[me] if scatter else values[...]
    lax.fori_loop(1, count, wait, 0)
    out[...] = jnp.sum(landed[...], axis=0)


def small_sum(values, axes, scatter, collective_id):
    count = math.prod(lax.axis_size(a) for a in axes)
    shape = values.shape[-2:]
    return pl.pallas_call(
        functools.partial(small_sum_kernel, axes, scatter),
        name="small_sum",
        out_shape=jax.ShapeDtypeStruct(shape, F32),
        in_specs=[VMEM_SPEC],
        out_specs=VMEM_SPEC,
        scratch_shapes=[pltpu.VMEM((count,) + shape, F32), DMA((count,)), DMA((count,))],
        compiler_params=comm_params(collective_id),
        cost_estimate=pl.CostEstimate(flops=0, bytes_accessed=10_000_000, transcendentals=0),
    )(values)


def rms_norm(values_in, gain_vec):
    return (
        values_in
        * lax.rsqrt(jnp.mean(values_in * values_in, axis=-1, keepdims=True) + EPSILON)
        * gain_vec
    )


def angles(row_count, head_dim):
    places = jnp.arange(row_count, dtype=jnp.int32).astype(F32)
    frequency = jnp.exp(-math.log(10000.0) * 2.0 * jnp.arange(head_dim // 2, dtype=F32) / head_dim)
    turn_angle = places[:, None] * frequency[None, :]
    return (jnp.cos(turn_angle)[:, None, :], jnp.sin(turn_angle)[:, None, :])


def rotate(values_in, cosine, sine):
    half_dim = values_in.shape[-1] // 2
    first_half = values_in[..., :half_dim]
    second = values_in[..., half_dim:]
    return jnp.concatenate(
        [first_half * cosine - second * sine, second * cosine + first_half * sine], axis=-1
    )


def mm(left, right):
    return jnp.dot(left, right, preferred_element_type=F32)


def mm_tn(left, right):
    return lax.dot_general(left, right, (((0,), (0,)), ((), ())), preferred_element_type=F32)


def mm_nt(left, right):
    return lax.dot_general(left, right, (((1,), (1,)), ((), ())), preferred_element_type=F32)


def ein(spec, *ops):
    return jnp.einsum(spec, *ops, preferred_element_type=F32)


def shards(
    layer_in,
    segment_ids,
    routing,
    out_grad,
    attn_gain,
    w_query,
    w_key,
    w_value,
    query_gain,
    key_gain,
    w_out,
    mlp_gain,
    w_router,
    w_gate,
    w_up,
    w_down,
):
    groups = lax.axis_size("group")
    sources = lax.axis_size("expert")
    me = lax.axis_index("group")
    rows = layer_in.shape[1]
    width = layer_in.shape[2]
    length = rows * groups
    head_dim = width // HEADS
    heads = HEADS // groups
    cols = width // groups
    local_experts = w_gate.shape[0]
    experts = local_experts * sources
    hidden_size = w_gate.shape[2]
    parts = groups // local_experts
    part = hidden_size // parts
    score_scale = 1.0 / math.sqrt(head_dim)

    def own_cols(matrix, axis):
        return lax.dynamic_slice_in_dim(matrix, me * cols, cols, axis)

    def slices(w):
        w = w.reshape(local_experts, w.shape[1], parts, part).transpose(0, 2, 1, 3)
        return w.reshape(groups, w.shape[2], part)

    def exchange(w):
        return lax.all_to_all(w, "group", 0, 0, tiled=True)

    def row_of_devices(w):
        return lax.all_gather(w, "expert", axis=0, tiled=False)

    together = lax.optimization_barrier
    gate_own = exchange(slices(w_gate))

    inputs = layer_in[0].astype(F32)
    normed_b = rms_norm(inputs, attn_gain).astype(BF16)
    expert_ids = jnp.arange(experts, dtype=jnp.int32)
    marks = jnp.any(routing[0][:, :, None] == expert_ids[None, None, :], axis=1).astype(F32)
    own_scales = [
        lax.rsqrt(jnp.mean(jnp.square(mm(normed_b, w)), axis=1) + EPSILON)[None] for w in (w_query, w_key)
    ]
    marks = jnp.concatenate([marks.T, segment_ids[0].astype(F32)[None]] + own_scales, axis=0)
    normed_all, marks = gather_rows([normed_b], groups, 1, note=marks)
    marks = marks.transpose(1, 0, 2).reshape(experts + 3, length)
    chosen, seg_all = marks[:experts].T > 0.5, marks[experts]
    down_in = w_down.reshape(groups, part, cols)
    gate_own, down_in, normed_late = together((gate_own, down_in, normed_all))
    gate_w = row_of_devices(gate_own.reshape(width, part))
    down_own = exchange(down_in)
    wq, wk, wv = own_cols(w_query, 1), own_cols(w_key, 1), own_cols(w_value, 1)
    query_raw, key_raw = mm(normed_all, wq), mm(normed_all, wk)
    values_b = mm(normed_all, wv).astype(BF16).reshape(length, heads, head_dim)

    def row_sums(first, second, collective_id):
        sums = jnp.stack([jnp.sum(first, axis=1), jnp.sum(second, axis=1)])
        sums = small_sum(sums.reshape(-1, 128), ("group",), False, collective_id)
        return sums.reshape(2, length, 1) / width

    query_scale, key_scale = marks[experts + 1][:, None], marks[experts + 2][:, None]
    query_gain_c, key_gain_c = own_cols(query_gain, 0), own_cols(key_gain, 0)
    cosine, sine = angles(length, head_dim)

    def turned(raw, scale, gain):
        return rotate((raw * scale * gain).reshape(length, heads, head_dim), cosine, sine)

    queries_b = turned(query_raw, query_scale, query_gain_c).astype(BF16)
    keys_b = turned(key_raw, key_scale, key_gain_c).astype(BF16)
    down_own, queries_b, keys_b = together((down_own, queries_b, keys_b))
    place = jnp.arange(length, dtype=jnp.int32)
    allowed = (seg_all[:, None] == seg_all[None, :]) & (place[None, :] <= place[:, None])
    scores = jnp.where(allowed[None], ein("qhd,khd->hqk", queries_b, keys_b) * score_scale, MASKED)
    top_score = jnp.max(scores, axis=-1, keepdims=True)
    log_total = top_score + jnp.log(jnp.sum(jnp.exp(scores - top_score), axis=-1, keepdims=True))
    probs = jnp.exp(scores - log_total)
    probs_b = probs.astype(BF16)
    mixed_c = ein("hqk,khd->qhd", probs_b, values_b).reshape(length, cols).astype(BF16)
    gate_w, mixed_in = together((gate_w, mixed_c))
    (mixed_b,) = swap([mixed_in], groups, False, 3)
    up_in, down_own, mixed_b = together((slices(w_up), down_own, mixed_b))
    down_w = row_of_devices(down_own.transpose(1, 0, 2).reshape(part, width))
    up_own = exchange(up_in)
    resid = inputs + mm(mixed_b, w_out)
    normed_mlp_b = rms_norm(resid, mlp_gain).astype(BF16)
    (mlp_all,) = gather_rows([normed_mlp_b], groups, 4)
    up_own, down_w, mlp_late, grad_in = together((up_own, down_w, mlp_all, out_grad[0]))
    up_w = row_of_devices(up_own.reshape(width, part))
    (grad_all,) = gather_rows([grad_in], groups, 10)
    up_w, grad_all = together((up_w, grad_all))

    router_all = jax.nn.softmax(mm(mlp_all, w_router), axis=-1)
    picked = jnp.where(chosen, router_all, 0.0).reshape(length, sources, local_experts)
    picked = lax.dynamic_index_in_dim(picked, me // parts, 2, keepdims=True)
    gate_pre = ein("td,edf->tef", mlp_all, gate_w)
    up_pre = ein("td,edf->tef", mlp_all, up_w)
    sigma = jax.nn.sigmoid(gate_pre)
    hidden = gate_pre * sigma * up_pre
    hidden_b = (hidden * picked).astype(BF16)
    out_part = ein("tef,efd->td", hidden_b, down_w).astype(BF16)
    out_part, grad_all = together((out_part, grad_all))
    mixture = lax.psum_scatter(out_part, "group", scatter_dimension=0, tiled=True)
    hidden_grad = ein("td,efd->tef", grad_all, down_w)
    picked_grad = jnp.sum(hidden * hidden_grad, axis=2)
    hidden_grad = hidden_grad * picked
    gate_grad_b = (hidden_grad * up_pre * sigma * (1.0 + gate_pre * (1.0 - sigma))).astype(BF16)
    up_grad_b = (hidden_grad * gate_pre * sigma).astype(BF16)
    own_expert = jnp.arange(local_experts, dtype=jnp.int32) == me // parts
    full_part = jnp.where(own_expert[None, None, :], picked_grad[:, :, None], 0.0)
    full_part = jnp.where(chosen, full_part.reshape(length, experts), 0.0)
    full_part = full_part.T.reshape(experts, groups, rows).transpose(1, 0, 2)
    gate_w_part = ein("td,tef->edf", mlp_late, gate_grad_b).astype(BF16)
    up_w_part = ein("td,tef->edf", mlp_late, up_grad_b).astype(BF16)
    up_w_part, gate_grad_b, up_grad_b = together((up_w_part, gate_grad_b, up_grad_b))

    def over_row(w):
        return lax.psum_scatter(w, "expert", scatter_dimension=0, tiled=False)

    gate_sum, up_sum = over_row(gate_w_part), over_row(up_w_part)
    slot_part = ein("tef,edf->td", gate_grad_b, gate_w) + ein("tef,edf->td", up_grad_b, up_w)
    slot_part, mixture = together((slot_part.astype(BF16), mixture))
    slot_sum, router_full_grad = reduce_rows(slot_part, full_part, groups, 5)
    router_full_grad = router_full_grad.T

    def slices_out(w):
        w = w.reshape(local_experts, parts, cols, part).transpose(0, 2, 1, 3)
        return w.reshape(local_experts, cols, hidden_size).astype(F32)

    result = (resid + mixture.astype(F32)).astype(BF16)
    grad_out = out_grad[0].astype(F32)
    router = jax.nn.softmax(mm(normed_mlp_b, w_router), axis=-1)
    logits_grad_b = (
        router * (router_full_grad - jnp.sum(router * router_full_grad, axis=-1, keepdims=True))
    ).astype(BF16)
    router_w_grad = mm_tn(normed_mlp_b, logits_grad_b)
    mlp_in_grad = slot_sum + mm_nt(logits_grad_b, w_router)
    _, mlp_back = jax.vjp(rms_norm, resid, mlp_gain)
    resid_part, mlp_gain_grad = mlp_back(mlp_in_grad)
    resid_grad = grad_out + resid_part
    attn_grad_b = resid_grad.astype(BF16)
    (attn_grad_all,) = gather_rows([attn_grad_b], groups, 6)
    gate_sum, attn_grad_late = together((gate_sum, attn_grad_all))
    gate_sum = exchange(gate_sum.reshape(groups, cols, part))
    mixed_grad_c = mm_nt(attn_grad_late, own_cols(w_out, 0)).astype(BF16)
    mixed_grad_c = mixed_grad_c.reshape(length, heads, head_dim)

    prob_grad = ein("qhd,khd->hqk", mixed_grad_c, values_b)
    delta = jnp.sum(probs * prob_grad, axis=-1, keepdims=True)
    score_grad_b = (probs * (prob_grad - delta) * score_scale).astype(BF16)
    score_grad_b, probs_b = together((score_grad_b, probs_b))
    query_grad = ein("hqk,khd->qhd", score_grad_b, keys_b)
    key_grad = ein("hqk,qhd->khd", score_grad_b, queries_b)
    query_grad, key_grad, hidden_b = together((query_grad, key_grad, hidden_b))
    down_w_part = ein("tef,td->efd", hidden_b, grad_all).astype(BF16)
    gate_sum, up_sum, query_grad, key_grad, probs_b, down_w_part = together(
        (gate_sum, up_sum, query_grad, key_grad, probs_b, down_w_part)
    )
    down_sum = over_row(down_w_part)
    up_sum = exchange(up_sum.reshape(groups, cols, part))
    value_grad_b = ein("hqk,qhd->khd", probs_b, mixed_grad_c).astype(BF16).reshape(length, cols)

    def unturned(grad):
        return rotate(grad, cosine, -sine).reshape(length, cols)

    query_turn, key_turn = unturned(query_grad), unturned(key_grad)
    query_mix, key_mix = query_turn * query_gain_c, key_turn * key_gain_c
    query_dots, key_dots, value_grad_b = together(
        (query_mix * query_raw, key_mix * key_raw, value_grad_b)
    )
    dots = row_sums(query_dots, key_dots, 7)
    query_raw_b = (
        query_scale * query_mix - query_raw * query_scale**3 * dots[0]
    ).astype(BF16)
    key_raw_b = (key_scale * key_mix - key_raw * key_scale**3 * dots[1]).astype(BF16)
    query_gain_part = jnp.sum(query_turn * query_raw * query_scale, axis=0)
    key_gain_part = jnp.sum(key_turn * key_raw * key_scale, axis=0)
    raw_grads = [query_raw_b, key_raw_b, value_grad_b]
    down_sum = down_sum.reshape(part, groups, cols).transpose(1, 0, 2)
    (query_own, key_own, value_own), raw_grads, up_sum, down_sum = together(
        (swap(raw_grads, groups, False, 8), raw_grads, up_sum, down_sum)
    )
    down_sum = exchange(down_sum)
    out_w_part = mm_tn(mixed_c, attn_grad_late).astype(BF16)
    out_w_grad = lax.psum_scatter(out_w_part, "expert", scatter_dimension=0, tiled=True)
    qkv_part = mm_tn(normed_late, jnp.concatenate(raw_grads, axis=1)).astype(BF16)
    qkv_part = qkv_part.reshape(groups, sources, -1, 3 * cols).transpose(1, 0, 2, 3)
    qkv_part = over_row(qkv_part.reshape(sources, -1, 3 * cols)).reshape(groups, -1, 3 * cols)
    normed_grad = mm_nt(query_own, w_query) + mm_nt(key_own, w_key) + mm_nt(value_own, w_value)
    _, attn_back = jax.vjp(rms_norm, inputs, attn_gain)
    input_part, attn_gain_grad = attn_back(normed_grad)
    input_grad = resid_grad + input_part
    wide = [
        lax.dynamic_update_slice_in_dim(jnp.zeros((width,), F32), part, me * cols, 0)
        for part in (query_gain_part, key_gain_part)
    ]
    small = jnp.concatenate([router_w_grad.T, jnp.stack([mlp_gain_grad, attn_gain_grad] + wide)])
    devices = groups * sources
    small = small.reshape(-1, devices, width // devices).transpose(1, 0, 2).reshape(devices, -1)
    used = small.shape[1]
    small = jnp.pad(small, ((0, 0), (0, -used % 1024))).reshape(devices, -1, 128)
    small = small_sum(small, ("group", "expert"), True, 9)
    small, qkv_part, down_sum = together((small, qkv_part, down_sum))
    qkv_part = exchange(qkv_part)
    qkv_part = qkv_part.transpose(1, 0, 2).reshape(-1, groups, 3, cols).astype(F32)
    small = small.reshape(-1)[:used]
    small = small.reshape(-1, width // devices)
    return (
        result[None],
        input_grad[None],
        small[experts + 1],
        qkv_part[:, :, 0].reshape(-1, width),
        qkv_part[:, :, 1].reshape(-1, width),
        qkv_part[:, :, 2].reshape(-1, width),
        small[experts + 2],
        small[experts + 3],
        out_w_grad.astype(F32),
        small[experts],
        small[:experts].T,
        slices_out(gate_sum),
        slices_out(up_sum),
        down_sum.reshape(local_experts, hidden_size, cols).astype(F32),
    )


def solution(mesh):
    token = P("expert", "group", None)
    every = P(("group", "expert"))
    return jax.shard_map(
        shards,
        mesh=mesh,
        in_specs=(token, P("expert", "group"), token, token)
        + (P(),) * 9
        + (token, token, P("expert", None, "group")),
        out_specs=(token, token)
        + (every,) * 9
        + (token, token, P("expert", None, "group")),
        check_vma=False,
    )
```

```python
import functools
import math

import jax
import jax.numpy as jnp
from jax import lax
from jax.experimental import pallas as pl
from jax.experimental.pallas import tpu as pltpu
from jax.sharding import PartitionSpec as P

HEADS = 16
EPSILON = 1e-05
MASKED = -1000000000.0
BF16 = jnp.bfloat16
F32 = jnp.float32
MESH = pl.DeviceIdType.MESH
DMA = pltpu.SemaphoreType.DMA
VMEM_SPEC = pl.BlockSpec(memory_space=pltpu.VMEM)


def remote(src, dst, send_sem, recv_sem, where):
    return pltpu.make_async_remote_copy(
        src, dst, send_sem, recv_sem, device_id=where, device_id_type=MESH
    )


def comm_params(collective_id):
    return pltpu.CompilerParams(collective_id=collective_id, has_side_effects=True)


def greet(peers):
    barrier = pltpu.get_barrier_semaphore()
    total = 0
    for here, where in peers:

        @pl.when(here)
        def _(where=where):
            pl.semaphore_signal(barrier, inc=1, device_id=where, device_id_type=MESH)

        total = total + jnp.where(here, 1, 0)
    pl.semaphore_wait(barrier, total)


def greet_all(count, device):
    barrier = pltpu.get_barrier_semaphore()

    def body(k, carry):
        pl.semaphore_signal(barrier, inc=1, device_id=device(k), device_id_type=MESH)
        return carry

    lax.fori_loop(1, count, body, 0)
    pl.semaphore_wait(barrier, count - 1)


def gather_kernel(nz, ny, pieces, count, *refs):
    noted = len(refs) > 2 * count + 3
    ins, outs, sems = refs[: count + noted], refs[count + noted : -3 - 2 * noted], refs[-3 - 2 * noted :]
    own_sem, send_sem, recv_sem = sems[:3]
    me = lax.axis_index("group")
    z, y = me // ny, me % ny

    def at(z_to, y_to):
        return {"group": z_to * ny + y_to}

    def note_copy(k):
        to = {"group": lax.rem(me + k, nz * ny)}
        return remote(ins[count], outs[count].at[me], sems[3].at[k], sems[4].at[k], to)

    if noted:
        greet_all(nz * ny, lambda k: {"group": lax.rem(me + k, nz * ny)})
        for k in range(1, nz * ny):
            note_copy(k).start()
        outs[count][me] = ins[count][...]
    else:
        greet(
            [
                (z > 0, at(z - 1, y)),
                (z < nz - 1, at(z + 1, y)),
                (y > 0, at(z, y - 1)),
                (y < ny - 1, at(z, y + 1)),
            ]
        )
    owns = [pltpu.make_async_copy(ins[n], outs[n].at[me], own_sem.at[n]) for n in range(count)]
    for own in owns:
        own.start()

    def part(ref, c):
        rows = ref.shape[0] // pieces
        return ref.at[pl.ds(c * rows, rows)]

    def copy(slot, source, n, c, where, first):
        return remote(
            part(ins[n], c) if first else part(outs[n].at[source], c),
            part(outs[n].at[source], c),
            send_sem.at[n, slot, source, c],
            recv_sem.at[n, source, c],
            where,
        )

    def outgoing(source, go):
        sz, sy = source // ny, source % ny
        column = go & (sy == y)
        return [
            (column & (sz <= z) & (z < nz - 1), 0, at(z + 1, y)),
            (column & (sz >= z) & (z > 0), 1, at(z - 1, y)),
            (go & (sy <= y) & (y < ny - 1), 2, at(z, y + 1)),
            (go & (sy >= y) & (y > 0), 3, at(z, y - 1)),
        ]

    def act(source, n, first, go, start):
        for c in range(pieces):
            if start and not first:

                @pl.when(go)
                def _():
                    copy(0, source, n, c, at(z, y), False).wait_recv()

            for cond, slot, where in outgoing(source, go):

                @pl.when(cond)
                def _(slot=slot, where=where):
                    one = copy(slot, source, n, c, where, first)
                    if start:
                        one.start()
                    else:
                        one.wait_send()

    order = []
    for dz in range(nz):
        for sz in [z] if dz == 0 else [z - dz, z + dz]:
            for dy in range(ny):
                for sy in [y] if dy == 0 else [y - dy, y + dy]:
                    inside = (sz >= 0) & (sz < nz) & (sy >= 0) & (sy < ny)
                    source = jnp.clip(sz, 0, nz - 1) * ny + jnp.clip(sy, 0, ny - 1)
                    order.append((dz + dy, dz, source, inside))
    order = sorted(order, key=lambda t: (t[0], -t[1]))
    for start in (True, False):
        for distance, _, source, inside in order:
            for n in range(count):
                act(source, n, distance == 0, inside, start)
        if start:
            for own in owns:
                own.wait()
    if noted:
        for k in range(1, nz * ny):
            note_copy(k).wait()


def gather_rows(blocks, groups, collective_id, pieces=2, note=None):
    nz = min(4, groups)
    count = len(blocks)
    notes = [] if note is None else [note]
    outs = pl.pallas_call(
        functools.partial(gather_kernel, nz, groups // nz, pieces, count),
        name="gather_rows",
        out_shape=[jax.ShapeDtypeStruct((groups,) + a.shape, a.dtype) for a in blocks + notes],
        in_specs=[VMEM_SPEC] * (count + len(notes)),
        out_specs=[pl.BlockSpec(memory_space=pl.ANY)] * count + [VMEM_SPEC] * len(notes),
        scratch_shapes=[DMA((count,)), DMA((count, 4, groups, pieces)), DMA((count, groups, pieces))]
        + [DMA((groups,))] * 2 * len(notes),
        compiler_params=comm_params(collective_id),
        cost_estimate=pl.CostEstimate(
            flops=0, bytes_accessed=200_000_000 * count, transcendentals=0
        ),
    )(*blocks, *notes)
    rows = [a.reshape(groups * b.shape[0], b.shape[1]) for a, b in zip(outs, blocks)]
    return rows + list(outs[count:])


def reduce_kernel(
    nz, ny, pieces, parts, note, out, note_out, ybuf, zbuf, landed, ysend, yrecv, zsend, zrecv, nsend, nrecv
):
    me = lax.axis_index("group")
    z, y = me // ny, me % ny
    rows = parts.shape[1] // pieces

    def at(z_to, y_to):
        return {"group": z_to * ny + y_to}

    def note_copy(k):
        to = lax.rem(me + k, nz * ny)
        return remote(note.at[to], landed.at[k], nsend.at[k], nrecv.at[k], {"group": to})

    greet_all(nz * ny, lambda k: {"group": lax.rem(me + k, nz * ny)})
    for k in range(1, nz * ny):
        note_copy(k).start()
    landed[0] = note[me]

    def part(ref, c):
        return ref.at[pl.ds(c * rows, rows)]

    def y_copy(dest, c):
        src, dst = part(parts.at[dest * ny + 1 - y], c), part(ybuf.at[dest], c)
        return remote(src, dst, ysend.at[dest, c], yrecv.at[dest, c], at(z, 1 - y))

    def z_copy(side, dest, c):
        src, dst = part(ybuf.at[dest], c), part(zbuf.at[side, dest], c)
        where = at(z - 1, y) if side else at(z + 1, y)
        return remote(src, dst, zsend.at[dest, c], zrecv.at[side, dest, c], where)

    order = []
    for d in range(nz - 1, 0, -1):
        order += [(z + d, z + d < nz, 0), (z - d, z - d >= 0, 1)]
    order = [(jnp.clip(dest, 0, nz - 1), inside, side) for dest, inside, side in order]
    for dest, inside, side in order:

        @pl.when(inside)
        def _():
            for c in range(pieces):
                y_copy(dest, c).start()

    for c in range(pieces):
        y_copy(z, c).start()
    for dest, inside, side in order:
        further = (z < nz - 1) if side else (z > 0)
        for c in range(pieces):
            span = pl.ds(c * rows, rows)

            @pl.when(inside)
            def _():
                y_copy(dest, c).wait_recv()
                pair = parts[dest * ny + y, span, :].astype(F32) + ybuf[dest, span, :].astype(F32)

                @pl.when(further)
                def _():
                    z_copy(side, dest, c).wait_recv()
                    ybuf[dest, span, :] = (pair + zbuf[side, dest, span, :].astype(F32)).astype(BF16)

                @pl.when(jnp.logical_not(further))
                def _():
                    ybuf[dest, span, :] = pair.astype(BF16)

                z_copy(side, dest, c).start()

    for c in range(pieces):
        span = pl.ds(c * rows, rows)
        y_copy(z, c).wait_recv()
        out[span, :] = parts[me, span, :].astype(F32) + ybuf[z, span, :].astype(F32)

        @pl.when(z > 0)
        def _():
            z_copy(0, z, c).wait_recv()
            out[span, :] += zbuf[0, z, span, :].astype(F32)

        @pl.when(z < nz - 1)
        def _():
            z_copy(1, z, c).wait_recv()
            out[span, :] += zbuf[1, z, span, :].astype(F32)

    for dest, inside, side in order:

        @pl.when(inside)
        def _():
            for c in range(pieces):
                y_copy(dest, c).wait_send()
                z_copy(side, dest, c).wait_send()

    for c in range(pieces):
        y_copy(z, c).wait_send()
    for k in range(1, nz * ny):
        note_copy(k).wait()
    note_out[...] = jnp.sum(landed[...], axis=0)


def reduce_rows(parts, note, groups, collective_id, pieces=2):
    nz = min(4, groups)
    ny = groups // nz
    if ny != 2:
        total = lax.psum_scatter(parts, "group", scatter_dimension=0, tiled=True).astype(F32)
        return total, lax.psum_scatter(note, "group", scatter_dimension=0, tiled=False)
    rows, width = parts.shape[0] // groups, parts.shape[1]
    return pl.pallas_call(
        functools.partial(reduce_kernel, nz, ny, pieces),
        name="reduce_rows",
        out_shape=[
            jax.ShapeDtypeStruct((rows, width), F32),
            jax.ShapeDtypeStruct(note.shape[1:], F32),
        ],
        in_specs=[VMEM_SPEC] * 2,
        out_specs=[VMEM_SPEC] * 2,
        scratch_shapes=[
            pltpu.VMEM((nz, rows, width), BF16),
            pltpu.VMEM((2, nz, rows, width), BF16),
            pltpu.VMEM(note.shape, F32),
            DMA((nz, pieces)),
            DMA((nz, pieces)),
            DMA((nz, pieces)),
            DMA((2, nz, pieces)),
            DMA((groups,)),
            DMA((groups,)),
        ],
        compiler_params=comm_params(collective_id),
        cost_estimate=pl.CostEstimate(flops=0, bytes_accessed=200_000_000, transcendentals=0),
    )(parts.reshape(groups, rows, width), note)


def swap_kernel(groups, to_rows, *refs):
    count = (len(refs) - 2) // 2
    ins, outs, (send_sem, recv_sem) = refs[:count], refs[count : 2 * count], refs[2 * count :]
    me = lax.axis_index("group")
    columns = ins[0].shape[-1] // (groups if to_rows else 1)
    wide = lambda ref, i: ref.at[:, pl.ds(pl.multiple_of(i * columns, columns), columns)]
    thin = lambda ref, i: ref.at[i]
    source, target = (wide, thin) if to_rows else (thin, wide)

    def peer(k):
        return lax.rem(me + k, groups)

    greet_all(groups, lambda k: {"group": peer(k)})

    def copy(n, k):
        to = peer(k)
        return remote(
            source(ins[n], to), target(outs[n], me), send_sem.at[n, k], recv_sem.at[n, k], {"group": to}
        )

    for k in range(1, groups):
        for n in range(count):
            copy(n, k).start()
    for n in range(count):
        if to_rows:
            outs[n][me] = ins[n][:, pl.ds(pl.multiple_of(me * columns, columns), columns)]
        else:
            outs[n][:, pl.ds(pl.multiple_of(me * columns, columns), columns)] = ins[n][me]
    for k in range(1, groups):
        for n in range(count):
            copy(n, k).wait()


def swap(arrays, groups, to_rows, collective_id):
    shape, count = arrays[0].shape, len(arrays)
    if to_rows:
        rows, columns = shape[0], shape[1] // groups
        out = (groups, rows, columns)
    else:
        rows, columns = shape[0] // groups, shape[1]
        arrays = [a.reshape(groups, rows, columns) for a in arrays]
        out = (rows, groups * columns)
    outs = pl.pallas_call(
        functools.partial(swap_kernel, groups, to_rows),
        name="swap",
        out_shape=[jax.ShapeDtypeStruct(out, a.dtype) for a in arrays],
        in_specs=[VMEM_SPEC] * count,
        out_specs=[VMEM_SPEC] * count,
        scratch_shapes=[DMA((count, groups)), DMA((count, groups))],
        compiler_params=comm_params(collective_id),
        cost_estimate=pl.CostEstimate(flops=0, bytes_accessed=30_000_000, transcendentals=0),
    )(*arrays)
    return [o.reshape(groups * rows, columns) if to_rows else o for o in outs]


def small_sum_kernel(axes, scatter, values, out, landed, send_sem, recv_sem):
    sizes = [lax.axis_size(a) for a in axes]
    count = math.prod(sizes)
    me = 0
    for a, n in zip(axes, sizes):
        me = me * n + lax.axis_index(a)

    def peer(k):
        return lax.rem(me + k, count)

    def device(k):
        to = peer(k)
        if len(axes) == 1:
            return {axes[0]: to}
        return {axes[0]: to // sizes[1], axes[1]: lax.rem(to, sizes[1])}

    greet_all(count, device)

    def copy(k):
        src = values.at[peer(k)] if scatter else values
        return remote(src, landed.at[k], send_sem.at[k], recv_sem.at[k], device(k))

    def start(k, carry):
        copy(k).start()
        return carry

    def wait(k, carry):
        copy(k).wait()
        return carry

    lax.fori_loop(1, count, start, 0)
    landed[0] = values[me] if scatter else values[...]
    lax.fori_loop(1, count, wait, 0)
    out[...] = jnp.sum(landed[...], axis=0)


def small_sum(values, axes, scatter, collective_id):
    count = math.prod(lax.axis_size(a) for a in axes)
    shape = values.shape[-2:]
    return pl.pallas_call(
        functools.partial(small_sum_kernel, axes, scatter),
        name="small_sum",
        out_shape=jax.ShapeDtypeStruct(shape, F32),
        in_specs=[VMEM_SPEC],
        out_specs=VMEM_SPEC,
        scratch_shapes=[pltpu.VMEM((count,) + shape, F32), DMA((count,)), DMA((count,))],
        compiler_params=comm_params(collective_id),
        cost_estimate=pl.CostEstimate(flops=0, bytes_accessed=10_000_000, transcendentals=0),
    )(values)


def rms_norm(values_in, gain_vec):
    return (
        values_in
        * lax.rsqrt(jnp.mean(values_in * values_in, axis=-1, keepdims=True) + EPSILON)
        * gain_vec
    )


def angles(row_count, head_dim):
    places = jnp.arange(row_count, dtype=jnp.int32).astype(F32)
    frequency = jnp.exp(-math.log(10000.0) * 2.0 * jnp.arange(head_dim // 2, dtype=F32) / head_dim)
    turn_angle = places[:, None] * frequency[None, :]
    return (jnp.cos(turn_angle)[:, None, :], jnp.sin(turn_angle)[:, None, :])


def rotate(values_in, cosine, sine):
    half_dim = values_in.shape[-1] // 2
    first_half = values_in[..., :half_dim]
    second = values_in[..., half_dim:]
    return jnp.concatenate(
        [first_half * cosine - second * sine, second * cosine + first_half * sine], axis=-1
    )


def mm(left, right):
    return jnp.dot(left, right, preferred_element_type=F32)


def mm_tn(left, right):
    return lax.dot_general(left, right, (((0,), (0,)), ((), ())), preferred_element_type=F32)


def mm_nt(left, right):
    return lax.dot_general(left, right, (((1,), (1,)), ((), ())), preferred_element_type=F32)


def ein(spec, *ops):
    return jnp.einsum(spec, *ops, preferred_element_type=F32)


def shards(
    layer_in,
    segment_ids,
    routing,
    out_grad,
    attn_gain,
    w_query,
    w_key,
    w_value,
    query_gain,
    key_gain,
    w_out,
    mlp_gain,
    w_router,
    w_gate,
    w_up,
    w_down,
):
    groups = lax.axis_size("group")
    sources = lax.axis_size("expert")
    me = lax.axis_index("group")
    rows = layer_in.shape[1]
    width = layer_in.shape[2]
    length = rows * groups
    head_dim = width // HEADS
    heads = HEADS // groups
    cols = width // groups
    local_experts = w_gate.shape[0]
    experts = local_experts * sources
    hidden_size = w_gate.shape[2]
    parts = groups // local_experts
    part = hidden_size // parts
    score_scale = 1.0 / math.sqrt(head_dim)

    def own_cols(matrix, axis):
        return lax.dynamic_slice_in_dim(matrix, me * cols, cols, axis)

    def slices(w):
        w = w.reshape(local_experts, w.shape[1], parts, part).transpose(0, 2, 1, 3)
        return w.reshape(groups, w.shape[2], part)

    def exchange(w):
        return lax.all_to_all(w, "group", 0, 0, tiled=True)

    def row_of_devices(w):
        return lax.all_gather(w, "expert", axis=0, tiled=False)

    together = lax.optimization_barrier
    gate_own = exchange(slices(w_gate))

    inputs = layer_in[0].astype(F32)
    normed_b = rms_norm(inputs, attn_gain).astype(BF16)
    expert_ids = jnp.arange(experts, dtype=jnp.int32)
    marks = jnp.any(routing[0][:, :, None] == expert_ids[None, None, :], axis=1).astype(F32)
    own_scales = [
        lax.rsqrt(jnp.mean(jnp.square(mm(normed_b, w)), axis=1) + EPSILON)[None] for w in (w_query, w_key)
    ]
    marks = jnp.concatenate([marks.T, segment_ids[0].astype(F32)[None]] + own_scales, axis=0)
    normed_all, marks = gather_rows([normed_b], groups, 1, note=marks)
    marks = marks.transpose(1, 0, 2).reshape(experts + 3, length)
    chosen, seg_all = marks[:experts].T > 0.5, marks[experts]
    down_in = w_down.reshape(groups, part, cols)
    gate_own, down_in, normed_late = together((gate_own, down_in, normed_all))
    gate_w = row_of_devices(gate_own.reshape(width, part))
    down_own = exchange(down_in)
    wq, wk, wv = own_cols(w_query, 1), own_cols(w_key, 1), own_cols(w_value, 1)
    query_raw, key_raw = mm(normed_all, wq), mm(normed_all, wk)
    values_b = mm(normed_all, wv).astype(BF16).reshape(length, heads, head_dim)

    def row_sums(first, second, collective_id):
        sums = jnp.stack([jnp.sum(first, axis=1), jnp.sum(second, axis=1)])
        sums = small_sum(sums.reshape(-1, 128), ("group",), False, collective_id)
        return sums.reshape(2, length, 1) / width

    query_scale, key_scale = marks[experts + 1][:, None], marks[experts + 2][:, None]
    query_gain_c, key_gain_c = own_cols(query_gain, 0), own_cols(key_gain, 0)
    cosine, sine = angles(length, head_dim)

    def turned(raw, scale, gain):
        return rotate((raw * scale * gain).reshape(length, heads, head_dim), cosine, sine)

    queries_b = turned(query_raw, query_scale, query_gain_c).astype(BF16)
    keys_b = turned(key_raw, key_scale, key_gain_c).astype(BF16)
    down_own, queries_b, keys_b = together((down_own, queries_b, keys_b))
    place = jnp.arange(length, dtype=jnp.int32)
    allowed = (seg_all[:, None] == seg_all[None, :]) & (place[None, :] <= place[:, None])
    scores = jnp.where(allowed[None], ein("qhd,khd->hqk", queries_b, keys_b) * score_scale, MASKED)
    top_score = jnp.max(scores, axis=-1, keepdims=True)
    log_total = top_score + jnp.log(jnp.sum(jnp.exp(scores - top_score), axis=-1, keepdims=True))
    probs = jnp.exp(scores - log_total)
    probs_b = probs.astype(BF16)
    mixed_c = ein("hqk,khd->qhd", probs_b, values_b).reshape(length, cols).astype(BF16)
    gate_w, mixed_in = together((gate_w, mixed_c))
    (mixed_b,) = swap([mixed_in], groups, False, 3)
    up_in, down_own, mixed_b = together((slices(w_up), down_own, mixed_b))
    down_w = row_of_devices(down_own.transpose(1, 0, 2).reshape(part, width))
    up_own = exchange(up_in)
    resid = inputs + mm(mixed_b, w_out)
    normed_mlp_b = rms_norm(resid, mlp_gain).astype(BF16)
    (mlp_all,) = gather_rows([normed_mlp_b], groups, 4)
    up_own, down_w, mlp_late, grad_in = together((up_own, down_w, mlp_all, out_grad[0]))
    up_w = row_of_devices(up_own.reshape(width, part))
    (grad_all,) = gather_rows([grad_in], groups, 10)
    up_w, grad_all = together((up_w, grad_all))

    router_all = jax.nn.softmax(mm(mlp_all, w_router), axis=-1)
    picked = jnp.where(chosen, router_all, 0.0).reshape(length, sources, local_experts)
    picked = lax.dynamic_index_in_dim(picked, me // parts, 2, keepdims=True)
    gate_pre = ein("td,edf->tef", mlp_all, gate_w)
    up_pre = ein("td,edf->tef", mlp_all, up_w)
    sigma = jax.nn.sigmoid(gate_pre)
    hidden = gate_pre * sigma * up_pre
    hidden_b = (hidden * picked).astype(BF16)
    out_part = ein("tef,efd->td", hidden_b, down_w).astype(BF16)
    out_part, grad_all = together((out_part, grad_all))
    mixture = lax.psum_scatter(out_part, "group", scatter_dimension=0, tiled=True)
    hidden_grad = ein("td,efd->tef", grad_all, down_w)
    picked_grad = jnp.sum(hidden * hidden_grad, axis=2)
    hidden_grad = hidden_grad * picked
    gate_grad_b = (hidden_grad * up_pre * sigma * (1.0 + gate_pre * (1.0 - sigma))).astype(BF16)
    up_grad_b = (hidden_grad * gate_pre * sigma).astype(BF16)
    own_expert = jnp.arange(local_experts, dtype=jnp.int32) == me // parts
    full_part = jnp.where(own_expert[None, None, :], picked_grad[:, :, None], 0.0)
    full_part = jnp.where(chosen, full_part.reshape(length, experts), 0.0)
    full_part = full_part.T.reshape(experts, groups, rows).transpose(1, 0, 2)
    gate_w_part = ein("td,tef->edf", mlp_late, gate_grad_b).astype(BF16)
    up_w_part = ein("td,tef->edf", mlp_late, up_grad_b).astype(BF16)
    up_w_part, gate_grad_b, up_grad_b = together((up_w_part, gate_grad_b, up_grad_b))

    def over_row(w):
        return lax.psum_scatter(w, "expert", scatter_dimension=0, tiled=False)

    gate_sum, up_sum = over_row(gate_w_part), over_row(up_w_part)
    slot_part = ein("tef,edf->td", gate_grad_b, gate_w) + ein("tef,edf->td", up_grad_b, up_w)
    slot_part, mixture = together((slot_part.astype(BF16), mixture))
    slot_sum, router_full_grad = reduce_rows(slot_part, full_part, groups, 5)
    router_full_grad = router_full_grad.T

    def slices_out(w):
        w = w.reshape(local_experts, parts, cols, part).transpose(0, 2, 1, 3)
        return w.reshape(local_experts, cols, hidden_size).astype(F32)

    result = (resid + mixture.astype(F32)).astype(BF16)
    grad_out = out_grad[0].astype(F32)
    router = jax.nn.softmax(mm(normed_mlp_b, w_router), axis=-1)
    logits_grad_b = (
        router * (router_full_grad - jnp.sum(router * router_full_grad, axis=-1, keepdims=True))
    ).astype(BF16)
    router_w_grad = mm_tn(normed_mlp_b, logits_grad_b)
    mlp_in_grad = slot_sum + mm_nt(logits_grad_b, w_router)
    _, mlp_back = jax.vjp(rms_norm, resid, mlp_gain)
    resid_part, mlp_gain_grad = mlp_back(mlp_in_grad)
    resid_grad = grad_out + resid_part
    attn_grad_b = resid_grad.astype(BF16)
    (attn_grad_all,) = gather_rows([attn_grad_b], groups, 6)
    gate_sum, attn_grad_late = together((gate_sum, attn_grad_all))
    gate_sum = exchange(gate_sum.reshape(groups, cols, part))
    mixed_grad_c = mm_nt(attn_grad_late, own_cols(w_out, 0)).astype(BF16)
    mixed_grad_c = mixed_grad_c.reshape(length, heads, head_dim)

    prob_grad = ein("qhd,khd->hqk", mixed_grad_c, values_b)
    delta = jnp.sum(probs * prob_grad, axis=-1, keepdims=True)
    score_grad_b = (probs * (prob_grad - delta) * score_scale).astype(BF16)
    score_grad_b, probs_b = together((score_grad_b, probs_b))
    query_grad = ein("hqk,khd->qhd", score_grad_b, keys_b)
    key_grad = ein("hqk,qhd->khd", score_grad_b, queries_b)
    query_grad, key_grad, hidden_b = together((query_grad, key_grad, hidden_b))
    down_w_part = ein("tef,td->efd", hidden_b, grad_all).astype(BF16)
    gate_sum, up_sum, query_grad, key_grad, probs_b, down_w_part = together(
        (gate_sum, up_sum, query_grad, key_grad, probs_b, down_w_part)
    )
    down_sum = over_row(down_w_part)
    up_sum = exchange(up_sum.reshape(groups, cols, part))
    value_grad_b = ein("hqk,qhd->khd", probs_b, mixed_grad_c).astype(BF16).reshape(length, cols)

    def unturned(grad):
        return rotate(grad, cosine, -sine).reshape(length, cols)

    query_turn, key_turn = unturned(query_grad), unturned(key_grad)
    query_mix, key_mix = query_turn * query_gain_c, key_turn * key_gain_c
    query_gain_part = jnp.sum(query_turn * query_raw * query_scale, axis=0)
    key_gain_part = jnp.sum(key_turn * key_raw * key_scale, axis=0)
    query_dots, key_dots, value_grad_b, query_gain_part, key_gain_part = together(
        (query_mix * query_raw, key_mix * key_raw, value_grad_b, query_gain_part, key_gain_part)
    )
    dots = row_sums(query_dots, key_dots, 7)
    query_raw_b = (
        query_scale * query_mix - query_raw * query_scale**3 * dots[0]
    ).astype(BF16)
    key_raw_b = (key_scale * key_mix - key_raw * key_scale**3 * dots[1]).astype(BF16)
    raw_grads = [query_raw_b, key_raw_b, value_grad_b]
    down_sum = down_sum.reshape(part, groups, cols).transpose(1, 0, 2)
    (query_own, key_own, value_own), raw_grads, up_sum, down_sum = together(
        (swap(raw_grads, groups, False, 8), raw_grads, up_sum, down_sum)
    )
    down_sum = exchange(down_sum)
    out_w_part = mm_tn(mixed_c, attn_grad_late).astype(BF16)
    out_w_grad = lax.psum_scatter(out_w_part, "expert", scatter_dimension=0, tiled=True)
    qkv_part = mm_tn(normed_late, jnp.concatenate(raw_grads, axis=1)).astype(BF16)
    qkv_part = qkv_part.reshape(groups, sources, -1, 3 * cols).transpose(1, 0, 2, 3)
    qkv_part = over_row(qkv_part.reshape(sources, -1, 3 * cols)).reshape(groups, -1, 3 * cols)
    normed_grad = mm_nt(query_own, w_query) + mm_nt(key_own, w_key) + mm_nt(value_own, w_value)
    _, attn_back = jax.vjp(rms_norm, inputs, attn_gain)
    input_part, attn_gain_grad = attn_back(normed_grad)
    input_grad = resid_grad + input_part
    wide = [
        lax.dynamic_update_slice_in_dim(jnp.zeros((width,), F32), part, me * cols, 0)
        for part in (query_gain_part, key_gain_part)
    ]
    small = jnp.concatenate([router_w_grad.T, jnp.stack([mlp_gain_grad, attn_gain_grad] + wide)])
    devices = groups * sources
    small = small.reshape(-1, devices, width // devices).transpose(1, 0, 2).reshape(devices, -1)
    used = small.shape[1]
    small = jnp.pad(small, ((0, 0), (0, -used % 1024))).reshape(devices, -1, 128)
    small, up_out, down_sum = together((small, slices_out(up_sum), down_sum))
    small = small_sum(small, ("group", "expert"), True, 9)
    small, qkv_part = together((small, qkv_part))
    qkv_part = exchange(qkv_part)
    small = small.reshape(-1)[:used].reshape(-1, width // devices)
    qkv_part, small = together((qkv_part, small))
    qkv_part = qkv_part.transpose(1, 0, 2).reshape(-1, groups, 3, cols).astype(F32)
    return (
        result[None],
        input_grad[None],
        small[experts + 1],
        qkv_part[:, :, 0].reshape(-1, width),
        qkv_part[:, :, 1].reshape(-1, width),
        qkv_part[:, :, 2].reshape(-1, width),
        small[experts + 2],
        small[experts + 3],
        out_w_grad.astype(F32),
        small[experts],
        small[:experts].T,
        slices_out(gate_sum),
        up_out,
        down_sum.reshape(local_experts, hidden_size, cols).astype(F32),
    )


def solution(mesh):
    token = P("expert", "group", None)
    every = P(("group", "expert"))
    return jax.shard_map(
        shards,
        mesh=mesh,
        in_specs=(token, P("expert", "group"), token, token)
        + (P(),) * 9
        + (token, token, P("expert", None, "group")),
        out_specs=(token, token)
        + (every,) * 9
        + (token, token, P("expert", None, "group")),
        check_vma=False,
    )
```

```python
import functools
import math

import jax
import jax.numpy as jnp
from jax import lax
from jax.experimental import pallas as pl
from jax.experimental.pallas import tpu as pltpu
from jax.sharding import PartitionSpec as P

HEADS = 16
EPSILON = 1e-05
MASKED = -1000000000.0
BF16 = jnp.bfloat16
F32 = jnp.float32
MESH = pl.DeviceIdType.MESH
DMA = pltpu.SemaphoreType.DMA
VMEM_SPEC = pl.BlockSpec(memory_space=pltpu.VMEM)


def remote(src, dst, send_sem, recv_sem, where):
    return pltpu.make_async_remote_copy(
        src, dst, send_sem, recv_sem, device_id=where, device_id_type=MESH
    )


def comm_params(collective_id):
    return pltpu.CompilerParams(collective_id=collective_id, has_side_effects=True)


def greet(peers):
    barrier = pltpu.get_barrier_semaphore()
    total = 0
    for here, where in peers:

        @pl.when(here)
        def _(where=where):
            pl.semaphore_signal(barrier, inc=1, device_id=where, device_id_type=MESH)

        total = total + jnp.where(here, 1, 0)
    pl.semaphore_wait(barrier, total)


def greet_all(count, device):
    barrier = pltpu.get_barrier_semaphore()

    def body(k, carry):
        pl.semaphore_signal(barrier, inc=1, device_id=device(k), device_id_type=MESH)
        return carry

    lax.fori_loop(1, count, body, 0)
    pl.semaphore_wait(barrier, count - 1)


def gather_kernel(nz, ny, pieces, count, *refs):
    noted = len(refs) > 2 * count + 3
    ins, outs, sems = refs[: count + noted], refs[count + noted : -3 - 2 * noted], refs[-3 - 2 * noted :]
    own_sem, send_sem, recv_sem = sems[:3]
    me = lax.axis_index("group")
    z, y = me // ny, me % ny

    def at(z_to, y_to):
        return {"group": z_to * ny + y_to}

    def note_copy(k):
        to = {"group": lax.rem(me + k, nz * ny)}
        return remote(ins[count], outs[count].at[me], sems[3].at[k], sems[4].at[k], to)

    if noted:
        greet_all(nz * ny, lambda k: {"group": lax.rem(me + k, nz * ny)})
        for k in range(1, nz * ny):
            note_copy(k).start()
        outs[count][me] = ins[count][...]
    else:
        greet(
            [
                (z > 0, at(z - 1, y)),
                (z < nz - 1, at(z + 1, y)),
                (y > 0, at(z, y - 1)),
                (y < ny - 1, at(z, y + 1)),
            ]
        )
    owns = [pltpu.make_async_copy(ins[n], outs[n].at[me], own_sem.at[n]) for n in range(count)]
    for own in owns:
        own.start()

    def part(ref, c):
        rows = ref.shape[0] // pieces
        return ref.at[pl.ds(c * rows, rows)]

    def copy(slot, source, n, c, where, first):
        return remote(
            part(ins[n], c) if first else part(outs[n].at[source], c),
            part(outs[n].at[source], c),
            send_sem.at[n, slot, source, c],
            recv_sem.at[n, source, c],
            where,
        )

    def outgoing(source, go):
        sz, sy = source // ny, source % ny
        column = go & (sy == y)
        return [
            (column & (sz <= z) & (z < nz - 1), 0, at(z + 1, y)),
            (column & (sz >= z) & (z > 0), 1, at(z - 1, y)),
            (go & (sy <= y) & (y < ny - 1), 2, at(z, y + 1)),
            (go & (sy >= y) & (y > 0), 3, at(z, y - 1)),
        ]

    def act(source, n, first, go, start):
        for c in range(pieces):
            if start and not first:

                @pl.when(go)
                def _():
                    copy(0, source, n, c, at(z, y), False).wait_recv()

            for cond, slot, where in outgoing(source, go):

                @pl.when(cond)
                def _(slot=slot, where=where):
                    one = copy(slot, source, n, c, where, first)
                    if start:
                        one.start()
                    else:
                        one.wait_send()

    order = []
    for dz in range(nz):
        for sz in [z] if dz == 0 else [z - dz, z + dz]:
            for dy in range(ny):
                for sy in [y] if dy == 0 else [y - dy, y + dy]:
                    inside = (sz >= 0) & (sz < nz) & (sy >= 0) & (sy < ny)
                    source = jnp.clip(sz, 0, nz - 1) * ny + jnp.clip(sy, 0, ny - 1)
                    order.append((dz + dy, dz, source, inside))
    order = sorted(order, key=lambda t: (t[0], -t[1]))
    for start in (True, False):
        for distance, _, source, inside in order:
            for n in range(count):
                act(source, n, distance == 0, inside, start)
        if start:
            for own in owns:
                own.wait()
    if noted:
        for k in range(1, nz * ny):
            note_copy(k).wait()


def gather_rows(blocks, groups, collective_id, pieces=2, note=None):
    nz = min(4, groups)
    count = len(blocks)
    notes = [] if note is None else [note]
    outs = pl.pallas_call(
        functools.partial(gather_kernel, nz, groups // nz, pieces, count),
        name="gather_rows",
        out_shape=[jax.ShapeDtypeStruct((groups,) + a.shape, a.dtype) for a in blocks + notes],
        in_specs=[VMEM_SPEC] * (count + len(notes)),
        out_specs=[pl.BlockSpec(memory_space=pl.ANY)] * count + [VMEM_SPEC] * len(notes),
        scratch_shapes=[DMA((count,)), DMA((count, 4, groups, pieces)), DMA((count, groups, pieces))]
        + [DMA((groups,))] * 2 * len(notes),
        compiler_params=comm_params(collective_id),
        cost_estimate=pl.CostEstimate(
            flops=0, bytes_accessed=200_000_000 * count, transcendentals=0
        ),
    )(*blocks, *notes)
    rows = [a.reshape(groups * b.shape[0], b.shape[1]) for a, b in zip(outs, blocks)]
    return rows + list(outs[count:])


def reduce_kernel(
    nz, ny, pieces, parts, note, out, note_out, ybuf, zbuf, landed, ysend, yrecv, zsend, zrecv, nsend, nrecv
):
    me = lax.axis_index("group")
    z, y = me // ny, me % ny
    rows = parts.shape[1] // pieces

    def at(z_to, y_to):
        return {"group": z_to * ny + y_to}

    def note_copy(k):
        to = lax.rem(me + k, nz * ny)
        return remote(note.at[to], landed.at[k], nsend.at[k], nrecv.at[k], {"group": to})

    greet_all(nz * ny, lambda k: {"group": lax.rem(me + k, nz * ny)})
    for k in range(1, nz * ny):
        note_copy(k).start()
    landed[0] = note[me]

    def part(ref, c):
        return ref.at[pl.ds(c * rows, rows)]

    def y_copy(dest, c):
        src, dst = part(parts.at[dest * ny + 1 - y], c), part(ybuf.at[dest], c)
        return remote(src, dst, ysend.at[dest, c], yrecv.at[dest, c], at(z, 1 - y))

    def z_copy(side, dest, c):
        src, dst = part(ybuf.at[dest], c), part(zbuf.at[side, dest], c)
        where = at(z - 1, y) if side else at(z + 1, y)
        return remote(src, dst, zsend.at[dest, c], zrecv.at[side, dest, c], where)

    order = []
    for d in range(nz - 1, 0, -1):
        order += [(z + d, z + d < nz, 0), (z - d, z - d >= 0, 1)]
    order = [(jnp.clip(dest, 0, nz - 1), inside, side) for dest, inside, side in order]
    for dest, inside, side in order:

        @pl.when(inside)
        def _():
            for c in range(pieces):
                y_copy(dest, c).start()

    for c in range(pieces):
        y_copy(z, c).start()
    for dest, inside, side in order:
        further = (z < nz - 1) if side else (z > 0)
        for c in range(pieces):
            span = pl.ds(c * rows, rows)

            @pl.when(inside)
            def _():
                y_copy(dest, c).wait_recv()
                pair = parts[dest * ny + y, span, :].astype(F32) + ybuf[dest, span, :].astype(F32)

                @pl.when(further)
                def _():
                    z_copy(side, dest, c).wait_recv()
                    ybuf[dest, span, :] = (pair + zbuf[side, dest, span, :].astype(F32)).astype(BF16)

                @pl.when(jnp.logical_not(further))
                def _():
                    ybuf[dest, span, :] = pair.astype(BF16)

                z_copy(side, dest, c).start()

    for c in range(pieces):
        span = pl.ds(c * rows, rows)
        y_copy(z, c).wait_recv()
        out[span, :] = parts[me, span, :].astype(F32) + ybuf[z, span, :].astype(F32)

        @pl.when(z > 0)
        def _():
            z_copy(0, z, c).wait_recv()
            out[span, :] += zbuf[0, z, span, :].astype(F32)

        @pl.when(z < nz - 1)
        def _():
            z_copy(1, z, c).wait_recv()
            out[span, :] += zbuf[1, z, span, :].astype(F32)

    for dest, inside, side in order:

        @pl.when(inside)
        def _():
            for c in range(pieces):
                y_copy(dest, c).wait_send()
                z_copy(side, dest, c).wait_send()

    for c in range(pieces):
        y_copy(z, c).wait_send()
    for k in range(1, nz * ny):
        note_copy(k).wait()
    note_out[...] = jnp.sum(landed[...], axis=0)


def reduce_rows(parts, note, groups, collective_id, pieces=2):
    nz = min(4, groups)
    ny = groups // nz
    if ny != 2:
        total = lax.psum_scatter(parts, "group", scatter_dimension=0, tiled=True).astype(F32)
        return total, lax.psum_scatter(note, "group", scatter_dimension=0, tiled=False)
    rows, width = parts.shape[0] // groups, parts.shape[1]
    return pl.pallas_call(
        functools.partial(reduce_kernel, nz, ny, pieces),
        name="reduce_rows",
        out_shape=[
            jax.ShapeDtypeStruct((rows, width), F32),
            jax.ShapeDtypeStruct(note.shape[1:], F32),
        ],
        in_specs=[VMEM_SPEC] * 2,
        out_specs=[VMEM_SPEC] * 2,
        scratch_shapes=[
            pltpu.VMEM((nz, rows, width), BF16),
            pltpu.VMEM((2, nz, rows, width), BF16),
            pltpu.VMEM(note.shape, F32),
            DMA((nz, pieces)),
            DMA((nz, pieces)),
            DMA((nz, pieces)),
            DMA((2, nz, pieces)),
            DMA((groups,)),
            DMA((groups,)),
        ],
        compiler_params=comm_params(collective_id),
        cost_estimate=pl.CostEstimate(flops=0, bytes_accessed=200_000_000, transcendentals=0),
    )(parts.reshape(groups, rows, width), note)


def swap_kernel(groups, to_rows, *refs):
    count = (len(refs) - 2) // 2
    ins, outs, (send_sem, recv_sem) = refs[:count], refs[count : 2 * count], refs[2 * count :]
    me = lax.axis_index("group")
    columns = ins[0].shape[-1] // (groups if to_rows else 1)
    wide = lambda ref, i: ref.at[:, pl.ds(pl.multiple_of(i * columns, columns), columns)]
    thin = lambda ref, i: ref.at[i]
    source, target = (wide, thin) if to_rows else (thin, wide)

    def peer(k):
        return lax.rem(me + k, groups)

    greet_all(groups, lambda k: {"group": peer(k)})

    def copy(n, k):
        to = peer(k)
        return remote(
            source(ins[n], to), target(outs[n], me), send_sem.at[n, k], recv_sem.at[n, k], {"group": to}
        )

    for k in range(1, groups):
        for n in range(count):
            copy(n, k).start()
    for n in range(count):
        if to_rows:
            outs[n][me] = ins[n][:, pl.ds(pl.multiple_of(me * columns, columns), columns)]
        else:
            outs[n][:, pl.ds(pl.multiple_of(me * columns, columns), columns)] = ins[n][me]
    for k in range(1, groups):
        for n in range(count):
            copy(n, k).wait()


def swap(arrays, groups, to_rows, collective_id):
    shape, count = arrays[0].shape, len(arrays)
    if to_rows:
        rows, columns = shape[0], shape[1] // groups
        out = (groups, rows, columns)
    else:
        rows, columns = shape[0] // groups, shape[1]
        arrays = [a.reshape(groups, rows, columns) for a in arrays]
        out = (rows, groups * columns)
    outs = pl.pallas_call(
        functools.partial(swap_kernel, groups, to_rows),
        name="swap",
        out_shape=[jax.ShapeDtypeStruct(out, a.dtype) for a in arrays],
        in_specs=[VMEM_SPEC] * count,
        out_specs=[VMEM_SPEC] * count,
        scratch_shapes=[DMA((count, groups)), DMA((count, groups))],
        compiler_params=comm_params(collective_id),
        cost_estimate=pl.CostEstimate(flops=0, bytes_accessed=30_000_000, transcendentals=0),
    )(*arrays)
    return [o.reshape(groups * rows, columns) if to_rows else o for o in outs]


def small_sum_kernel(axes, scatter, values, out, landed, send_sem, recv_sem):
    sizes = [lax.axis_size(a) for a in axes]
    count = math.prod(sizes)
    me = 0
    for a, n in zip(axes, sizes):
        me = me * n + lax.axis_index(a)

    def peer(k):
        return lax.rem(me + k, count)

    def device(k):
        to = peer(k)
        if len(axes) == 1:
            return {axes[0]: to}
        return {axes[0]: to // sizes[1], axes[1]: lax.rem(to, sizes[1])}

    greet_all(count, device)

    def copy(k):
        src = values.at[peer(k)] if scatter else values
        return remote(src, landed.at[k], send_sem.at[k], recv_sem.at[k], device(k))

    def start(k, carry):
        copy(k).start()
        return carry

    def wait(k, carry):
        copy(k).wait()
        return carry

    lax.fori_loop(1, count, start, 0)
    landed[0] = values[me] if scatter else values[...]
    lax.fori_loop(1, count, wait, 0)
    out[...] = jnp.sum(landed[...], axis=0)


def small_sum(values, axes, scatter, collective_id):
    count = math.prod(lax.axis_size(a) for a in axes)
    shape = values.shape[-2:]
    return pl.pallas_call(
        functools.partial(small_sum_kernel, axes, scatter),
        name="small_sum",
        out_shape=jax.ShapeDtypeStruct(shape, F32),
        in_specs=[VMEM_SPEC],
        out_specs=VMEM_SPEC,
        scratch_shapes=[pltpu.VMEM((count,) + shape, F32), DMA((count,)), DMA((count,))],
        compiler_params=comm_params(collective_id),
        cost_estimate=pl.CostEstimate(flops=0, bytes_accessed=10_000_000, transcendentals=0),
    )(values)


def rms_norm(values_in, gain_vec):
    return (
        values_in
        * lax.rsqrt(jnp.mean(values_in * values_in, axis=-1, keepdims=True) + EPSILON)
        * gain_vec
    )


def angles(row_count, head_dim):
    places = jnp.arange(row_count, dtype=jnp.int32).astype(F32)
    frequency = jnp.exp(-math.log(10000.0) * 2.0 * jnp.arange(head_dim // 2, dtype=F32) / head_dim)
    turn_angle = places[:, None] * frequency[None, :]
    return (jnp.cos(turn_angle)[:, None, :], jnp.sin(turn_angle)[:, None, :])


def rotate(values_in, cosine, sine):
    half_dim = values_in.shape[-1] // 2
    first_half = values_in[..., :half_dim]
    second = values_in[..., half_dim:]
    return jnp.concatenate(
        [first_half * cosine - second * sine, second * cosine + first_half * sine], axis=-1
    )


def mm(left, right):
    return jnp.dot(left, right, preferred_element_type=F32)


def mm_tn(left, right):
    return lax.dot_general(left, right, (((0,), (0,)), ((), ())), preferred_element_type=F32)


def mm_nt(left, right):
    return lax.dot_general(left, right, (((1,), (1,)), ((), ())), preferred_element_type=F32)


def ein(spec, *ops):
    return jnp.einsum(spec, *ops, preferred_element_type=F32)


def shards(
    layer_in,
    segment_ids,
    routing,
    out_grad,
    attn_gain,
    w_query,
    w_key,
    w_value,
    query_gain,
    key_gain,
    w_out,
    mlp_gain,
    w_router,
    w_gate,
    w_up,
    w_down,
):
    groups = lax.axis_size("group")
    sources = lax.axis_size("expert")
    me = lax.axis_index("group")
    rows = layer_in.shape[1]
    width = layer_in.shape[2]
    length = rows * groups
    head_dim = width // HEADS
    heads = HEADS // groups
    cols = width // groups
    local_experts = w_gate.shape[0]
    experts = local_experts * sources
    hidden_size = w_gate.shape[2]
    parts = groups // local_experts
    part = hidden_size // parts
    score_scale = 1.0 / math.sqrt(head_dim)

    def own_cols(matrix, axis):
        return lax.dynamic_slice_in_dim(matrix, me * cols, cols, axis)

    def slices(w):
        w = w.reshape(local_experts, w.shape[1], parts, part).transpose(0, 2, 1, 3)
        return w.reshape(groups, w.shape[2], part)

    def exchange(w):
        return lax.all_to_all(w, "group", 0, 0, tiled=True)

    def row_of_devices(w):
        return lax.all_gather(w, "expert", axis=0, tiled=False)

    together = lax.optimization_barrier
    gate_own = exchange(slices(w_gate))

    inputs = layer_in[0].astype(F32)
    normed_b = rms_norm(inputs, attn_gain).astype(BF16)
    expert_ids = jnp.arange(experts, dtype=jnp.int32)
    marks = jnp.any(routing[0][:, :, None] == expert_ids[None, None, :], axis=1).astype(F32)
    own_scales = [
        lax.rsqrt(jnp.mean(jnp.square(mm(normed_b, w)), axis=1) + EPSILON)[None] for w in (w_query, w_key)
    ]
    marks = jnp.concatenate([marks.T, segment_ids[0].astype(F32)[None]] + own_scales, axis=0)
    normed_all, marks = gather_rows([normed_b], groups, 1, note=marks)
    marks = marks.transpose(1, 0, 2).reshape(experts + 3, length)
    chosen, seg_all = marks[:experts].T > 0.5, marks[experts]
    down_in = w_down.reshape(groups, part, cols)
    gate_own, down_in, normed_late = together((gate_own, down_in, normed_all))
    gate_w = row_of_devices(gate_own.reshape(width, part))
    down_own = exchange(down_in)
    wq, wk, wv = own_cols(w_query, 1), own_cols(w_key, 1), own_cols(w_value, 1)
    query_raw, key_raw = mm(normed_all, wq), mm(normed_all, wk)
    values_b = mm(normed_all, wv).astype(BF16).reshape(length, heads, head_dim)

    def row_sums(first, second, collective_id):
        sums = jnp.stack([jnp.sum(first, axis=1), jnp.sum(second, axis=1)])
        sums = small_sum(sums.reshape(-1, 128), ("group",), False, collective_id)
        return sums.reshape(2, length, 1) / width

    query_scale, key_scale = marks[experts + 1][:, None], marks[experts + 2][:, None]
    query_gain_c, key_gain_c = own_cols(query_gain, 0), own_cols(key_gain, 0)
    cosine, sine = angles(length, head_dim)

    def turned(raw, scale, gain):
        return rotate((raw * scale * gain).reshape(length, heads, head_dim), cosine, sine)

    queries_b = turned(query_raw, query_scale, query_gain_c).astype(BF16)
    keys_b = turned(key_raw, key_scale, key_gain_c).astype(BF16)
    down_own, queries_b, keys_b = together((down_own, queries_b, keys_b))
    place = jnp.arange(length, dtype=jnp.int32)
    allowed = (seg_all[:, None] == seg_all[None, :]) & (place[None, :] <= place[:, None])
    scores = jnp.where(allowed[None], ein("qhd,khd->hqk", queries_b, keys_b) * score_scale, MASKED)
    top_score = jnp.max(scores, axis=-1, keepdims=True)
    log_total = top_score + jnp.log(jnp.sum(jnp.exp(scores - top_score), axis=-1, keepdims=True))
    probs = jnp.exp(scores - log_total)
    probs_b = probs.astype(BF16)
    mixed_c = ein("hqk,khd->qhd", probs_b, values_b).reshape(length, cols).astype(BF16)
    gate_w, mixed_in = together((gate_w, mixed_c))
    (mixed_b,) = swap([mixed_in], groups, False, 3)
    up_in, down_own, mixed_b = together((slices(w_up), down_own, mixed_b))
    down_w = row_of_devices(down_own.transpose(1, 0, 2).reshape(part, width))
    up_own = exchange(up_in)
    resid = inputs + mm(mixed_b, w_out)
    normed_mlp_b = rms_norm(resid, mlp_gain).astype(BF16)
    (mlp_all,) = gather_rows([normed_mlp_b], groups, 4)
    up_own, down_w, mlp_late, grad_in = together((up_own, down_w, mlp_all, out_grad[0]))
    up_w = row_of_devices(up_own.reshape(width, part))
    (grad_all,) = gather_rows([grad_in], groups, 10)
    up_w, grad_all = together((up_w, grad_all))

    router_all = jax.nn.softmax(mm(mlp_all, w_router), axis=-1)
    picked = jnp.where(chosen, router_all, 0.0).reshape(length, sources, local_experts)
    picked = lax.dynamic_index_in_dim(picked, me // parts, 2, keepdims=True)
    gate_pre = ein("td,edf->tef", mlp_all, gate_w)
    up_pre = ein("td,edf->tef", mlp_all, up_w)
    sigma = jax.nn.sigmoid(gate_pre)
    hidden = gate_pre * sigma * up_pre
    hidden_b = (hidden * picked).astype(BF16)
    out_part = ein("tef,efd->td", hidden_b, down_w).astype(BF16)
    out_part, grad_all = together((out_part, grad_all))
    mixture = lax.psum_scatter(out_part, "group", scatter_dimension=0, tiled=True)
    hidden_grad = ein("td,efd->tef", grad_all, down_w)
    picked_grad = jnp.sum(hidden * hidden_grad, axis=2)
    hidden_grad = hidden_grad * picked
    gate_grad_b = (hidden_grad * up_pre * sigma * (1.0 + gate_pre * (1.0 - sigma))).astype(BF16)
    up_grad_b = (hidden_grad * gate_pre * sigma).astype(BF16)
    own_expert = jnp.arange(local_experts, dtype=jnp.int32) == me // parts
    full_part = jnp.where(own_expert[None, None, :], picked_grad[:, :, None], 0.0)
    full_part = jnp.where(chosen, full_part.reshape(length, experts), 0.0)
    full_part = full_part.T.reshape(experts, groups, rows).transpose(1, 0, 2)
    gate_w_part = ein("td,tef->edf", mlp_late, gate_grad_b).astype(BF16)
    up_w_part = ein("td,tef->edf", mlp_late, up_grad_b).astype(BF16)
    up_w_part, gate_grad_b, up_grad_b = together((up_w_part, gate_grad_b, up_grad_b))

    def over_row(w):
        return lax.psum_scatter(w, "expert", scatter_dimension=0, tiled=False)

    gate_sum, up_sum = over_row(gate_w_part), over_row(up_w_part)
    slot_part = ein("tef,edf->td", gate_grad_b, gate_w) + ein("tef,edf->td", up_grad_b, up_w)
    slot_part, mixture = together((slot_part.astype(BF16), mixture))
    slot_sum, router_full_grad = reduce_rows(slot_part, full_part, groups, 5)
    router_full_grad = router_full_grad.T

    def slices_out(w):
        w = w.reshape(local_experts, parts, cols, part).transpose(0, 2, 1, 3)
        return w.reshape(local_experts, cols, hidden_size).astype(F32)

    result = (resid + mixture.astype(F32)).astype(BF16)
    grad_out = out_grad[0].astype(F32)
    router = jax.nn.softmax(mm(normed_mlp_b, w_router), axis=-1)
    logits_grad_b = (
        router * (router_full_grad - jnp.sum(router * router_full_grad, axis=-1, keepdims=True))
    ).astype(BF16)
    router_w_grad = mm_tn(normed_mlp_b, logits_grad_b)
    mlp_in_grad = slot_sum + mm_nt(logits_grad_b, w_router)
    _, mlp_back = jax.vjp(rms_norm, resid, mlp_gain)
    resid_part, mlp_gain_grad = mlp_back(mlp_in_grad)
    resid_grad = grad_out + resid_part
    attn_grad_b = resid_grad.astype(BF16)
    (attn_grad_all,) = gather_rows([attn_grad_b], groups, 6)
    gate_sum, attn_grad_late = together((gate_sum, attn_grad_all))
    gate_sum = exchange(gate_sum.reshape(groups, cols, part))
    mixed_grad_c = mm_nt(attn_grad_late, own_cols(w_out, 0)).astype(BF16)
    mixed_grad_c = mixed_grad_c.reshape(length, heads, head_dim)

    prob_grad = ein("qhd,khd->hqk", mixed_grad_c, values_b)
    delta = jnp.sum(probs * prob_grad, axis=-1, keepdims=True)
    score_grad_b = (probs * (prob_grad - delta) * score_scale).astype(BF16)
    score_grad_b, probs_b = together((score_grad_b, probs_b))
    query_grad = ein("hqk,khd->qhd", score_grad_b, keys_b)
    key_grad = ein("hqk,qhd->khd", score_grad_b, queries_b)
    query_grad, key_grad, hidden_b = together((query_grad, key_grad, hidden_b))
    down_w_part = ein("tef,td->efd", hidden_b, grad_all).astype(BF16)
    gate_sum, up_sum, query_grad, key_grad, probs_b, down_w_part = together(
        (gate_sum, up_sum, query_grad, key_grad, probs_b, down_w_part)
    )
    down_sum = over_row(down_w_part)
    up_sum = exchange(up_sum.reshape(groups, cols, part))
    value_grad_b = ein("hqk,qhd->khd", probs_b, mixed_grad_c).astype(BF16).reshape(length, cols)

    def unturned(grad):
        return rotate(grad, cosine, -sine).reshape(length, cols)

    query_turn, key_turn = unturned(query_grad), unturned(key_grad)
    query_mix, key_mix = query_turn * query_gain_c, key_turn * key_gain_c
    query_gain_part = jnp.sum(query_turn * query_raw * query_scale, axis=0)
    key_gain_part = jnp.sum(key_turn * key_raw * key_scale, axis=0)
    query_dots, key_dots, value_grad_b, query_gain_part, key_gain_part = together(
        (query_mix * query_raw, key_mix * key_raw, value_grad_b, query_gain_part, key_gain_part)
    )
    dots = row_sums(query_dots, key_dots, 7)
    query_raw_b = (
        query_scale * query_mix - query_raw * query_scale**3 * dots[0]
    ).astype(BF16)
    key_raw_b = (key_scale * key_mix - key_raw * key_scale**3 * dots[1]).astype(BF16)
    raw_grads = [query_raw_b, key_raw_b, value_grad_b]
    down_sum = down_sum.reshape(part, groups, cols).transpose(1, 0, 2)
    (query_own, key_own, value_own), raw_grads, up_sum, down_sum = together(
        (swap(raw_grads, groups, False, 8), raw_grads, up_sum, down_sum)
    )
    down_sum = exchange(down_sum)
    out_w_part = mm_tn(mixed_c, attn_grad_late).astype(BF16)
    out_w_grad = lax.psum_scatter(out_w_part, "expert", scatter_dimension=0, tiled=True)
    qkv_part = mm_tn(normed_late, jnp.concatenate(raw_grads, axis=1)).astype(BF16)
    qkv_part = qkv_part.reshape(groups, sources, -1, 3 * cols).transpose(1, 0, 2, 3)
    qkv_part = over_row(qkv_part.reshape(sources, -1, 3 * cols)).reshape(groups, -1, 3 * cols)
    normed_grad = mm_nt(query_own, w_query) + mm_nt(key_own, w_key) + mm_nt(value_own, w_value)
    _, attn_back = jax.vjp(rms_norm, inputs, attn_gain)
    input_part, attn_gain_grad = attn_back(normed_grad)
    input_grad = resid_grad + input_part
    wide = [
        lax.dynamic_update_slice_in_dim(jnp.zeros((width,), F32), part, me * cols, 0)
        for part in (query_gain_part, key_gain_part)
    ]
    small = jnp.concatenate([router_w_grad.T, jnp.stack([mlp_gain_grad, attn_gain_grad] + wide)])
    devices = groups * sources
    small = small.reshape(-1, devices, width // devices).transpose(1, 0, 2).reshape(devices, -1)
    used = small.shape[1]
    small = jnp.pad(small, ((0, 0), (0, -used % 1024))).reshape(devices, -1, 128)
    small, up_out, down_sum = together((small, slices_out(up_sum), down_sum))
    small = small_sum(small, ("group", "expert"), True, 9)
    small, qkv_part = together((small, qkv_part))
    qkv_part = exchange(qkv_part)
    small = small.reshape(-1)[:used].reshape(-1, width // devices)
    qkv_part, small = together((qkv_part, small))
    query_w_grad, key_w_grad, value_w_grad = [
        qkv_part[:, :, i * cols : (i + 1) * cols].transpose(1, 0, 2).reshape(-1, width).astype(F32)
        for i in range(3)
    ]
    return (
        result[None],
        input_grad[None],
        small[experts + 1],
        query_w_grad,
        key_w_grad,
        value_w_grad,
        small[experts + 2],
        small[experts + 3],
        out_w_grad.astype(F32),
        small[experts],
        small[:experts].T,
        slices_out(gate_sum),
        up_out,
        down_sum.reshape(local_experts, hidden_size, cols).astype(F32),
    )


def solution(mesh):
    token = P("expert", "group", None)
    every = P(("group", "expert"))
    return jax.shard_map(
        shards,
        mesh=mesh,
        in_specs=(token, P("expert", "group"), token, token)
        + (P(),) * 9
        + (token, token, P("expert", None, "group")),
        out_specs=(token, token)
        + (every,) * 9
        + (token, token, P("expert", None, "group")),
        check_vma=False,
    )
```
